256 devices in a mesh: col: 32 (over x_hi, z, core), row: 8 (over y, x_lo).
Axes of the slice: x: 4 (x_hi: 2, x_lo: 2; x = x_hi * 2 + x_lo), y: 4, z: 8, core: 2. Of those that a mesh axis runs over, the one named last changes fastest.
Arguments:
- start_field: float32 [2, 512, 8192], P(None, 'row', 'col'), may hold values from -36 to 36
- seam_target: float32 [2, 2, 16, 65536], P(None, None, 'row', 'col'), may hold values from -6 to 6
- seam_rows: int32 [4, 16, 65536], P(None, 'row', 'col'), may hold values from 0 to 30
- seam_band: int32 [4, 16, 65536], P(None, 'row', 'col'), may hold values from 0 to 2
- seam_frac: int32 [4, 2, 16, 65536], P(None, None, 'row', 'col'), may hold values from 0 to 255
- adjacency: int32 [2, 16, 256], P(None, 'row', 'col'), may hold values 0 or 1
Outputs:
- refined_field: float32 [2, 512, 8192], P(None, 'row', 'col')
- last_residual: float32 [2, 512, 8192], P(None, 'row', 'col')
The draws below stay inside these ranges and needn't reach their ends.
Inputs may be any that keep to these rules, and one draw needn't show every extreme that they name: `seam_rows`: index of the cell along the seam, in control points of the tile. `seam_band`: depth of the cell from the tile's edge. `seam_frac`: offsets in 256ths of a cell.
All inputs are finite; a program needn't handle non-finite values. No bound on the sum of `adjacency` on one device may be relied on, other than what follows from the above.
Results may differ from the reference program's by a relative error of at most 0.0003.
Values sent between devices are 32-bit elements; how exact they have to be, the bound alone decides.
A program may use at most 64 MiB of HBM per device.

```python
import jax
import jax.numpy as jnp

GRID = 32
BAND = 4
SAMPLES = 256
ITERS = 3
OUTER = 1
MONT_ROWS = 16
MONT_COLS = 256
HEIGHT = 512
BREADTH = 8192
SEAM_COLS = 65536


def draw_start_field(key, part):
    noise_key, tile_key = jax.random.split(jax.random.fold_in(key, 11))
    tile_scale = jnp.exp(jnp.log(10.0) * jax.random.uniform(tile_key, (MONT_ROWS, MONT_COLS), jnp.float32))
    row_ramp = jnp.arange(MONT_ROWS, dtype=jnp.float32) / max(MONT_ROWS - 1, 1)
    col_ramp = jnp.arange(MONT_COLS, dtype=jnp.float32) / max(MONT_COLS - 1, 1)
    ramp = 1.0 + row_ramp[:, None] + col_ramp[None, :]
    scale = 0.2 * tile_scale * ramp
    cells = jnp.repeat(jnp.repeat(scale, GRID, axis=0), GRID, axis=1)
    noise = jnp.clip(jax.random.normal(noise_key, (2, HEIGHT, BREADTH), jnp.float32), -5.5, 5.5)
    return (noise * cells[None]).astype(jnp.float32)


def touch_ends(entries, rng, low, largest):
    longest = entries.shape.index(max(entries.shape))
    spots = []
    for shift in (0, 1):
        where = [jax.random.randint(jax.random.fold_in(rng, axis), (), 0, length) for axis, length in enumerate(entries.shape)]
        where[longest] = (where[longest] + shift) % entries.shape[longest]
        spots.append(tuple(where))
    return entries.at[spots[0]].set(low).at[spots[1]].set(largest)


def block_scale(own_key, shape, cuts, least, high):
    factor_of, own = 1.0, jax.random.fold_in(own_key, 6)
    for axis_at, shards_of in cuts:
        draws = jnp.exp(jax.random.uniform(jax.random.fold_in(own, axis_at), (shards_of,), jnp.float32, least / len(cuts), high / len(cuts)))
        factor_of = factor_of * jnp.repeat(draws, shape[axis_at] // shards_of).reshape([-1 if axis == axis_at else 1 for axis in range(len(shape))])
    return factor_of


def normal_values(own_key, dims, spread, limit, pieces=(), held_as=jnp.bfloat16):
    gain = block_scale(own_key, dims, pieces, -0.22, 0.18) if pieces else 1.0
    drawn = jax.random.normal(own_key, dims, jnp.float32) * spread * gain
    return jnp.minimum(jnp.maximum(drawn, -limit), limit).astype(held_as)


def setup_inputs(seed: int = 0) -> dict:
    arg_keys = jax.random.split(jax.random.key(seed), 7)
    start_field = draw_start_field(jax.random.fold_in(arg_keys[6], 71), 0)
    seam_target = normal_values(arg_keys[1], (2, 2, MONT_ROWS, SEAM_COLS), 1.0, 6.0, ((2, 8), (3, 32)), jnp.float32)
    seam_rows = touch_ends(jax.random.randint(arg_keys[2], (4, MONT_ROWS, SEAM_COLS), 0, GRID - 1), jax.random.fold_in(arg_keys[2], 1), 0, (GRID - 1) - 1).astype(jnp.int32)
    seam_band = touch_ends(jax.random.randint(arg_keys[3], (4, MONT_ROWS, SEAM_COLS), 0, BAND - 1), jax.random.fold_in(arg_keys[3], 1), 0, (BAND - 1) - 1).astype(jnp.int32)
    seam_frac = touch_ends(jax.random.randint(arg_keys[4], (4, 2, MONT_ROWS, SEAM_COLS), 0, 256), jax.random.fold_in(arg_keys[4], 1), 0, 255).astype(jnp.int32)
    adjacency = touch_ends((jax.random.randint(arg_keys[5], (2, MONT_ROWS, MONT_COLS), 0, 8) < 7).astype(jnp.int32), jax.random.fold_in(arg_keys[5], 1), 0, 1)
    return {"start_field": start_field, "seam_target": seam_target, "seam_rows": seam_rows, "seam_band": seam_band, "seam_frac": seam_frac, "adjacency": adjacency}


BEND_WEIGHT = 0.05
DAMPING = 0.5

def tile_view(control, tile_rows, tile_cols, points):
    return control.reshape(2, tile_rows, points, tile_cols, points)

def edge_band(tile_grid, facing, band_depth):
    if facing == 0:
        return tile_grid[..., ::-1][..., :band_depth].transpose(0, 1, 3, 2, 4)
    if facing == 1:
        return tile_grid[..., :band_depth].transpose(0, 1, 3, 2, 4)
    if facing == 2:
        return tile_grid[:, :, ::-1][:, :, :band_depth].transpose(0, 1, 3, 4, 2)
    return tile_grid[:, :, :band_depth].transpose(0, 1, 3, 4, 2)

def place_edge(band_part, facing, points):
    band_depth = band_part.shape[4]
    if facing < 2:
        widened = jnp.pad(band_part.transpose(0, 1, 3, 2, 4), ((0, 0), (0, 0), (0, 0), (0, 0), (0, points - band_depth)))
        if facing == 0:
            return widened[..., ::-1]
        return widened
    widened = jnp.pad(band_part.transpose(0, 1, 4, 2, 3), ((0, 0), (0, 0), (0, points - band_depth), (0, 0), (0, 0)))
    if facing == 2:
        return widened[:, :, ::-1]
    return widened

def make_tables(along_cell, across, frac_pair):
    weight_along = (frac_pair[0].astype(jnp.float32) + 0.5) / 256.0
    weight_across = (frac_pair[1].astype(jnp.float32) + 0.5) / 256.0
    return (along_cell, across, weight_along, weight_across)

def interpolate(band_part, tables):
    along_cell, across, weight_along, weight_across = tables
    band_depth = band_part.shape[4]
    flattened = band_part.reshape(band_part.shape[:3] + (band_part.shape[3] * band_depth,))
    base_index = (along_cell * band_depth + across).astype(jnp.int32)

    def sample_at(offset):
        gather_index = jnp.broadcast_to((base_index + offset)[None], (2,) + base_index.shape)
        return jnp.take_along_axis(flattened, gather_index, axis=3)
    near = (1.0 - weight_across) * sample_at(0) + weight_across * sample_at(1)
    far_side = (1.0 - weight_across) * sample_at(band_depth) + weight_across * sample_at(band_depth + 1)
    return (1.0 - weight_along) * near + weight_along * far_side

def spread_back(residual, tables, points, band_depth):
    blank_band = jnp.zeros(residual.shape[:3] + (points, band_depth), jnp.float32)
    _, pullback = jax.vjp(lambda band_part: interpolate(band_part, tables), blank_band)
    return pullback(residual)[0]

def bending(control, tile_rows, tile_cols):
    grid_view = tile_view(control, tile_rows, tile_cols, GRID)
    inner = grid_view[:, :, :-2, :, 1:-1] + grid_view[:, :, 2:, :, 1:-1] + grid_view[:, :, 1:-1, :, :-2] + grid_view[:, :, 1:-1, :, 2:] - 4.0 * grid_view[:, :, 1:-1, :, 1:-1]
    widths = ((0, 0), (0, 0), (1, 1), (0, 0), (1, 1))
    curvature = jnp.pad(inner, widths)
    padded = jnp.pad(curvature, widths)
    result = padded[:, :, :-2, :, 1:-1] + padded[:, :, 2:, :, 1:-1] + padded[:, :, 1:-1, :, :-2] + padded[:, :, 1:-1, :, 2:] - 4.0 * curvature
    return result.reshape(control.shape)

def seam_global(control, target, tables, adjacency):
    tile_rows, tile_cols = (adjacency.shape[1], adjacency.shape[2])
    grid_view = tile_view(control, tile_rows, tile_cols, GRID)
    edge_parts = [edge_band(grid_view, facing, BAND) for facing in range(4)]
    seam_values = [interpolate(edge_parts[facing], tables[facing]) for facing in range(4)]
    mask_east = adjacency[0].astype(jnp.float32) * (jnp.arange(tile_cols) < tile_cols - 1).astype(jnp.float32)[None, :]
    mask_south = adjacency[1].astype(jnp.float32) * (jnp.arange(tile_rows) < tile_rows - 1).astype(jnp.float32)[:, None]
    own_east = seam_values[0]
    own_south = seam_values[2]
    if target is not None:
        own_east = own_east - target[0]
        own_south = own_south - target[1]
    blank_col = jnp.zeros((2, tile_rows, 1, SAMPLES), jnp.float32)
    blank_row = jnp.zeros((2, 1, tile_cols, SAMPLES), jnp.float32)
    west_next = jnp.concatenate([seam_values[1][:, :, 1:], blank_col], axis=2)
    north_next = jnp.concatenate([seam_values[3][:, 1:], blank_row], axis=1)
    resid_east = (own_east - west_next) * mask_east[None, :, :, None]
    resid_south = (own_south - north_next) * mask_south[None, :, :, None]
    resid_west = -jnp.concatenate([blank_col, resid_east[:, :, :-1]], axis=2)
    resid_north = -jnp.concatenate([blank_row, resid_south[:, :-1]], axis=1)
    residuals = [resid_east, resid_west, resid_south, resid_north]
    placed = [place_edge(spread_back(residuals[facing], tables[facing], GRID, BAND), facing, GRID) for facing in range(4)]
    summed = placed[0] + placed[1] + placed[2] + placed[3]
    return summed.reshape(control.shape)

def hessian_apply(control, tables, adjacency):
    tile_rows, tile_cols = (adjacency.shape[1], adjacency.shape[2])
    return seam_global(control, None, tables, adjacency) + BEND_WEIGHT * bending(control, tile_rows, tile_cols) + DAMPING * control

def reference(start_field, seam_target, seam_rows, seam_band, seam_frac, adjacency):
    tile_rows, tile_cols = (adjacency.shape[1], adjacency.shape[2])
    along_cells = seam_rows.reshape(4, tile_rows, tile_cols, SAMPLES)
    across_cells = seam_band.reshape(4, tile_rows, tile_cols, SAMPLES)
    frac_cells = seam_frac.reshape(4, 2, tile_rows, tile_cols, SAMPLES)
    tables = [make_tables(along_cells[facing], across_cells[facing], frac_cells[facing]) for facing in range(4)]
    target_cells = seam_target.reshape(2, 2, tile_rows, tile_cols, SAMPLES)
    target = (target_cells[0], target_cells[1])
    control = start_field
    residual = start_field
    for outer_step in range(OUTER):
        gradient = seam_global(control, target, tables, adjacency) + BEND_WEIGHT * bending(control, tile_rows, tile_cols)
        residual = -gradient
        direction = residual
        update = jnp.zeros_like(control)
        norm_now = jnp.sum(residual * residual)
        for iteration in range(ITERS):
            hess_image = hessian_apply(direction, tables, adjacency)
            step_size = norm_now / jnp.sum(direction * hess_image)
            update = update + step_size * direction
            residual = residual - step_size * hess_image
            norm_next = jnp.sum(residual * residual)
            direction = residual + norm_next / norm_now * direction
            norm_now = norm_next
        control = control + update
    return (control, residual)
```

```python
import jax
import jax.numpy as jnp
from jax import lax
from jax.sharding import PartitionSpec as P

GRID = 32
BAND = 4
ITERS = 3


BEND_WEIGHT = 0.05
DAMPING = 0.5


def from_behind(value, axis, steps):
    count = lax.axis_size(axis)
    leading, last = (max(0, -steps), min(count, count - steps))
    return lax.ppermute(value, axis, [(source, source + steps) for source in range(leading, last)])


def tile_view(control, tile_rows, tile_cols, points):
    return control.reshape(2, tile_rows, points, tile_cols, points)


def edge_band(tile_grid, facing, band_depth):
    if facing == 0:
        return tile_grid[..., ::-1][..., :band_depth].transpose(0, 1, 3, 2, 4)
    if facing == 1:
        return tile_grid[..., :band_depth].transpose(0, 1, 3, 2, 4)
    if facing == 2:
        return tile_grid[:, :, ::-1][:, :, :band_depth].transpose(0, 1, 3, 4, 2)
    return tile_grid[:, :, :band_depth].transpose(0, 1, 3, 4, 2)


def place_edge(band_part, facing, points):
    band_depth = band_part.shape[4]
    if facing < 2:
        widened = jnp.pad(
            band_part.transpose(0, 1, 3, 2, 4),
            ((0, 0), (0, 0), (0, 0), (0, 0), (0, points - band_depth)),
        )
        if facing == 0:
            return widened[..., ::-1]
        return widened
    widened = jnp.pad(
        band_part.transpose(0, 1, 4, 2, 3),
        ((0, 0), (0, 0), (0, points - band_depth), (0, 0), (0, 0)),
    )
    if facing == 2:
        return widened[:, :, ::-1]
    return widened


def make_tables(along_cell, across, frac_pair):
    weight_along = (frac_pair[0].astype(jnp.float32) + 0.5) / 256.0
    weight_across = (frac_pair[1].astype(jnp.float32) + 0.5) / 256.0
    return (along_cell, across, weight_along, weight_across)


def weight_tables(tables, points, band_depth):
    along_cell, across, weight_along, weight_across = tables
    along_iota = jnp.arange(points, dtype=jnp.int32)[None, None, :, None]
    across_iota = jnp.arange(band_depth, dtype=jnp.int32)[None, None, :, None]
    cell_now = along_cell[:, :, None, :]
    depth_now = across[:, :, None, :]
    frac_along = weight_along[:, :, None, :]
    frac_across = weight_across[:, :, None, :]
    along_table = (1.0 - frac_along) * (along_iota == cell_now).astype(jnp.float32) + frac_along * (
        along_iota == cell_now + 1
    ).astype(jnp.float32)
    across_table = (1.0 - frac_across) * (across_iota == depth_now).astype(
        jnp.float32
    ) + frac_across * (across_iota == depth_now + 1).astype(jnp.float32)
    return (along_table, across_table)


def interpolate(band_part, tables):
    along_table, across_table = weight_tables(tables, band_part.shape[3], band_part.shape[4])
    partial_sum = jnp.einsum(
        "cabiq,abis->cabqs", band_part, along_table, precision=lax.Precision.HIGHEST
    )
    return jnp.sum(partial_sum * across_table[None], axis=3)


def spread_back(residual, tables, points, band_depth):
    along_table, across_table = weight_tables(tables, points, band_depth)
    weighted = residual[:, :, :, None, :] * across_table[None]
    return jnp.einsum("cabqs,abis->cabiq", weighted, along_table, precision=lax.Precision.HIGHEST)


def bending(control, tile_rows, tile_cols):
    grid_view = tile_view(control, tile_rows, tile_cols, GRID)
    inner = (
        grid_view[:, :, :-2, :, 1:-1]
        + grid_view[:, :, 2:, :, 1:-1]
        + grid_view[:, :, 1:-1, :, :-2]
        + grid_view[:, :, 1:-1, :, 2:]
        - 4.0 * grid_view[:, :, 1:-1, :, 1:-1]
    )
    widths = ((0, 0), (0, 0), (1, 1), (0, 0), (1, 1))
    curvature = jnp.pad(inner, widths)
    padded = jnp.pad(curvature, widths)
    result = (
        padded[:, :, :-2, :, 1:-1]
        + padded[:, :, 2:, :, 1:-1]
        + padded[:, :, 1:-1, :, :-2]
        + padded[:, :, 1:-1, :, 2:]
        - 4.0 * curvature
    )
    return result.reshape(control.shape)


def seam_term(control, target, tables, adjacency):
    tile_rows, tile_cols = (adjacency.shape[1], adjacency.shape[2])
    grid_view = tile_view(control, tile_rows, tile_cols, GRID)
    edge_parts = [edge_band(grid_view, facing, BAND) for facing in range(4)]
    seam_values = [interpolate(edge_parts[facing], tables[facing]) for facing in range(4)]
    col_pos = lax.axis_index("col") * tile_cols + jnp.arange(tile_cols)
    row_pos = lax.axis_index("row") * tile_rows + jnp.arange(tile_rows)
    mask_east = (
        adjacency[0].astype(jnp.float32)
        * (col_pos < lax.axis_size("col") * tile_cols - 1).astype(jnp.float32)[None, :]
    )
    mask_south = (
        adjacency[1].astype(jnp.float32)
        * (row_pos < lax.axis_size("row") * tile_rows - 1).astype(jnp.float32)[:, None]
    )
    own_east = seam_values[0]
    own_south = seam_values[2]
    if target is not None:
        own_east = own_east - target[0]
        own_south = own_south - target[1]
    far_west = from_behind(seam_values[1][:, :, :1], "col", -1)
    low_north = from_behind(seam_values[3][:, :1], "row", -1)
    west_next = jnp.concatenate([seam_values[1][:, :, 1:], far_west], axis=2)
    north_next = jnp.concatenate([seam_values[3][:, 1:], low_north], axis=1)
    resid_east = (own_east - west_next) * mask_east[None, :, :, None]
    resid_south = (own_south - north_next) * mask_south[None, :, :, None]
    from_west = from_behind(resid_east[:, :, tile_cols - 1 :], "col", 1)
    from_north = from_behind(resid_south[:, tile_rows - 1 :], "row", 1)
    resid_west = -jnp.concatenate([from_west, resid_east[:, :, :-1]], axis=2)
    resid_north = -jnp.concatenate([from_north, resid_south[:, :-1]], axis=1)
    residuals = [resid_east, resid_west, resid_south, resid_north]
    spread_parts = [
        spread_back(residuals[facing], tables[facing], GRID, BAND) for facing in range(4)
    ]
    summed = (
        place_edge(spread_parts[0], 0, GRID)
        + place_edge(spread_parts[1], 1, GRID)
        + place_edge(spread_parts[2], 2, GRID)
        + place_edge(spread_parts[3], 3, GRID)
    )
    return summed.reshape(control.shape)


def hessian_apply(control, tables, adjacency):
    tile_rows, tile_cols = (adjacency.shape[1], adjacency.shape[2])
    return (
        seam_term(control, None, tables, adjacency)
        + BEND_WEIGHT * bending(control, tile_rows, tile_cols)
        + DAMPING * control
    )


def total_squares(residual):
    return lax.psum(jnp.sum(residual * residual), ("col", "row"))


def shards(start_field, seam_target, seam_rows, seam_band, seam_frac, adjacency):
    tile_rows, tile_cols = (adjacency.shape[1], adjacency.shape[2])
    samples = seam_rows.shape[2] // tile_cols
    along_cells = seam_rows.reshape(4, tile_rows, tile_cols, samples)
    across_cells = seam_band.reshape(4, tile_rows, tile_cols, samples)
    frac_cells = seam_frac.reshape(4, 2, tile_rows, tile_cols, samples)
    tables = [
        make_tables(along_cells[facing], across_cells[facing], frac_cells[facing])
        for facing in range(4)
    ]
    target_cells = seam_target.reshape(2, 2, tile_rows, tile_cols, samples)
    target = (target_cells[0], target_cells[1])
    control = start_field
    gradient = seam_term(control, target, tables, adjacency) + BEND_WEIGHT * bending(
        control, tile_rows, tile_cols
    )
    residual = -gradient
    update = jnp.zeros_like(control)
    direction = residual
    norm_now = None
    for iteration in range(ITERS):
        hess_image = hessian_apply(direction, tables, adjacency)
        last = iteration == ITERS - 1
        parts = [jnp.sum(direction * hess_image)]
        if not last:
            parts += [jnp.sum(hess_image * hess_image)]
            if iteration > 0:
                parts += [jnp.sum(residual * hess_image)]
        if norm_now is None:
            parts += [jnp.sum(residual * residual)]
        sums = lax.psum(jnp.stack(parts), ("col", "row"))
        curv = sums[0]
        if norm_now is None:
            norm_now = sums[-1]
        step_size = norm_now / curv
        update = update + step_size * direction
        residual = residual - step_size * hess_image
        if not last:
            image_sq = sums[1]
            cross = sums[2] if iteration > 0 else curv
            norm_next = norm_now - 2.0 * step_size * cross + step_size * step_size * image_sq
            direction = residual + norm_next / norm_now * direction
            norm_now = norm_next
    control = control + update
    return (control, residual)


def solution(mesh):
    placed = (
        P(None, "row", "col"),
        P(None, None, "row", "col"),
        P(None, "row", "col"),
        P(None, "row", "col"),
        P(None, None, "row", "col"),
        P(None, "row", "col"),
    )
    return jax.shard_map(
        shards,
        mesh=mesh,
        in_specs=placed,
        out_specs=(P(None, "row", "col"), P(None, "row", "col")),
        check_vma=False,
    )
```

```python
import functools

import jax
import jax.numpy as jnp
from jax import lax
from jax.experimental import pallas as pl
from jax.experimental.pallas import tpu as pltpu
from jax.sharding import PartitionSpec as P

GRID = 32
BAND = 4
ITERS = 3


BEND_WEIGHT = 0.05
DAMPING = 0.5


MESH_ID = pl.DeviceIdType.MESH


def _sum_kernel(names, x_ref, o_ref, row_buf, col_buf, part, row_send, row_recv, col_send, col_recv):
    ncol = lax.axis_size("col")
    nrow = lax.axis_size("row")
    ci = lax.axis_index("col")
    ri = lax.axis_index("row")

    def dev(c, r):
        where = {"col": c, "row": r}
        return tuple(where[n] for n in names)

    barrier = pltpu.get_barrier_semaphore()
    for k in range(1, nrow):
        pl.semaphore_signal(barrier, 1, device_id=dev(ci, (ri + k) % nrow), device_id_type=MESH_ID)
    for k in range(1, ncol):
        pl.semaphore_signal(barrier, 1, device_id=dev((ci + k) % ncol, ri), device_id_type=MESH_ID)
    pl.semaphore_wait(barrier, nrow - 1 + ncol - 1)

    def row_copy(peer, slot):
        return pltpu.make_async_remote_copy(
            src_ref=x_ref, dst_ref=row_buf.at[slot], send_sem=row_send.at[peer],
            recv_sem=row_recv.at[slot], device_id=dev(ci, peer), device_id_type=MESH_ID)

    for k in range(1, nrow):
        row_copy((ri + k) % nrow, ri).start()
    row_buf[ri] = x_ref[...]
    for k in range(1, nrow):
        row_copy((ri + k) % nrow, ri).wait_send()
        peer = (ri + nrow - k) % nrow
        row_copy(peer, peer).wait_recv()
    total = row_buf[0]
    for j in range(1, nrow):
        total = total + row_buf[j]
    part[...] = total

    def col_copy(peer, slot):
        return pltpu.make_async_remote_copy(
            src_ref=part, dst_ref=col_buf.at[slot], send_sem=col_send.at[peer],
            recv_sem=col_recv.at[slot], device_id=dev(peer, ri), device_id_type=MESH_ID)

    for k in range(1, ncol):
        col_copy((ci + k) % ncol, ci).start()
    col_buf[ci] = total
    for k in range(1, ncol):
        col_copy((ci + k) % ncol, ci).wait_send()
        peer = (ci + ncol - k) % ncol
        col_copy(peer, peer).wait_recv()
    total = col_buf[0]
    for j in range(1, ncol):
        total = total + col_buf[j]
    o_ref[...] = total


def global_sum(values, names):
    ncol = lax.axis_size("col")
    nrow = lax.axis_size("row")
    count = values.shape[0]
    tile = jnp.zeros((8, 128), jnp.float32).at[0, :count].set(values)
    summed = pl.pallas_call(
        functools.partial(_sum_kernel, names),
        out_shape=jax.ShapeDtypeStruct((8, 128), jnp.float32),
        in_specs=[pl.BlockSpec(memory_space=pltpu.VMEM)],
        out_specs=pl.BlockSpec(memory_space=pltpu.VMEM),
        scratch_shapes=[
            pltpu.VMEM((nrow, 8, 128), jnp.float32),
            pltpu.VMEM((ncol, 8, 128), jnp.float32),
            pltpu.VMEM((8, 128), jnp.float32),
            pltpu.SemaphoreType.DMA((nrow,)),
            pltpu.SemaphoreType.DMA((nrow,)),
            pltpu.SemaphoreType.DMA((ncol,)),
            pltpu.SemaphoreType.DMA((ncol,)),
        ],
        compiler_params=pltpu.CompilerParams(collective_id=0, has_side_effects=True),
    )(tile)
    return summed[0, :count]


def from_behind(value, axis, steps):
    count = lax.axis_size(axis)
    leading, last = (max(0, -steps), min(count, count - steps))
    return lax.ppermute(value, axis, [(source, source + steps) for source in range(leading, last)])


def tile_view(control, tile_rows, tile_cols, points):
    return control.reshape(2, tile_rows, points, tile_cols, points)


def edge_band(tile_grid, facing, band_depth):
    if facing == 0:
        return tile_grid[..., ::-1][..., :band_depth].transpose(0, 1, 3, 2, 4)
    if facing == 1:
        return tile_grid[..., :band_depth].transpose(0, 1, 3, 2, 4)
    if facing == 2:
        return tile_grid[:, :, ::-1][:, :, :band_depth].transpose(0, 1, 3, 4, 2)
    return tile_grid[:, :, :band_depth].transpose(0, 1, 3, 4, 2)


def place_edge(band_part, facing, points):
    band_depth = band_part.shape[4]
    if facing < 2:
        widened = jnp.pad(
            band_part.transpose(0, 1, 3, 2, 4),
            ((0, 0), (0, 0), (0, 0), (0, 0), (0, points - band_depth)),
        )
        if facing == 0:
            return widened[..., ::-1]
        return widened
    widened = jnp.pad(
        band_part.transpose(0, 1, 4, 2, 3),
        ((0, 0), (0, 0), (0, points - band_depth), (0, 0), (0, 0)),
    )
    if facing == 2:
        return widened[:, :, ::-1]
    return widened


def make_tables(along_cell, across, frac_pair):
    weight_along = (frac_pair[0].astype(jnp.float32) + 0.5) / 256.0
    weight_across = (frac_pair[1].astype(jnp.float32) + 0.5) / 256.0
    return (along_cell, across, weight_along, weight_across)


def weight_tables(tables, points, band_depth):
    along_cell, across, weight_along, weight_across = tables
    along_iota = jnp.arange(points, dtype=jnp.int32)[None, None, :, None]
    across_iota = jnp.arange(band_depth, dtype=jnp.int32)[None, None, :, None]
    cell_now = along_cell[:, :, None, :]
    depth_now = across[:, :, None, :]
    frac_along = weight_along[:, :, None, :]
    frac_across = weight_across[:, :, None, :]
    along_table = (1.0 - frac_along) * (along_iota == cell_now).astype(jnp.float32) + frac_along * (
        along_iota == cell_now + 1
    ).astype(jnp.float32)
    across_table = (1.0 - frac_across) * (across_iota == depth_now).astype(
        jnp.float32
    ) + frac_across * (across_iota == depth_now + 1).astype(jnp.float32)
    return (along_table, across_table)


def interpolate(band_part, tables):
    along_table, across_table = weight_tables(tables, band_part.shape[3], band_part.shape[4])
    partial_sum = jnp.einsum(
        "cabiq,abis->cabqs", band_part, along_table, precision=lax.Precision.HIGHEST
    )
    return jnp.sum(partial_sum * across_table[None], axis=3)


def spread_back(residual, tables, points, band_depth):
    along_table, across_table = weight_tables(tables, points, band_depth)
    weighted = residual[:, :, :, None, :] * across_table[None]
    return jnp.einsum("cabqs,abis->cabiq", weighted, along_table, precision=lax.Precision.HIGHEST)


def bending(control, tile_rows, tile_cols):
    grid_view = tile_view(control, tile_rows, tile_cols, GRID)
    inner = (
        grid_view[:, :, :-2, :, 1:-1]
        + grid_view[:, :, 2:, :, 1:-1]
        + grid_view[:, :, 1:-1, :, :-2]
        + grid_view[:, :, 1:-1, :, 2:]
        - 4.0 * grid_view[:, :, 1:-1, :, 1:-1]
    )
    widths = ((0, 0), (0, 0), (1, 1), (0, 0), (1, 1))
    curvature = jnp.pad(inner, widths)
    padded = jnp.pad(curvature, widths)
    result = (
        padded[:, :, :-2, :, 1:-1]
        + padded[:, :, 2:, :, 1:-1]
        + padded[:, :, 1:-1, :, :-2]
        + padded[:, :, 1:-1, :, 2:]
        - 4.0 * curvature
    )
    return result.reshape(control.shape)


def seam_term(control, target, tables, adjacency):
    tile_rows, tile_cols = (adjacency.shape[1], adjacency.shape[2])
    grid_view = tile_view(control, tile_rows, tile_cols, GRID)
    edge_parts = [edge_band(grid_view, facing, BAND) for facing in range(4)]
    seam_values = [interpolate(edge_parts[facing], tables[facing]) for facing in range(4)]
    col_pos = lax.axis_index("col") * tile_cols + jnp.arange(tile_cols)
    row_pos = lax.axis_index("row") * tile_rows + jnp.arange(tile_rows)
    mask_east = (
        adjacency[0].astype(jnp.float32)
        * (col_pos < lax.axis_size("col") * tile_cols - 1).astype(jnp.float32)[None, :]
    )
    mask_south = (
        adjacency[1].astype(jnp.float32)
        * (row_pos < lax.axis_size("row") * tile_rows - 1).astype(jnp.float32)[:, None]
    )
    own_east = seam_values[0]
    own_south = seam_values[2]
    if target is not None:
        own_east = own_east - target[0]
        own_south = own_south - target[1]
    far_west = from_behind(seam_values[1][:, :, :1], "col", -1)
    low_north = from_behind(seam_values[3][:, :1], "row", -1)
    west_next = jnp.concatenate([seam_values[1][:, :, 1:], far_west], axis=2)
    north_next = jnp.concatenate([seam_values[3][:, 1:], low_north], axis=1)
    resid_east = (own_east - west_next) * mask_east[None, :, :, None]
    resid_south = (own_south - north_next) * mask_south[None, :, :, None]
    from_west = from_behind(resid_east[:, :, tile_cols - 1 :], "col", 1)
    from_north = from_behind(resid_south[:, tile_rows - 1 :], "row", 1)
    resid_west = -jnp.concatenate([from_west, resid_east[:, :, :-1]], axis=2)
    resid_north = -jnp.concatenate([from_north, resid_south[:, :-1]], axis=1)
    residuals = [resid_east, resid_west, resid_south, resid_north]
    spread_parts = [
        spread_back(residuals[facing], tables[facing], GRID, BAND) for facing in range(4)
    ]
    summed = (
        place_edge(spread_parts[0], 0, GRID)
        + place_edge(spread_parts[1], 1, GRID)
        + place_edge(spread_parts[2], 2, GRID)
        + place_edge(spread_parts[3], 3, GRID)
    )
    return summed.reshape(control.shape)


def hessian_apply(control, tables, adjacency):
    tile_rows, tile_cols = (adjacency.shape[1], adjacency.shape[2])
    return (
        seam_term(control, None, tables, adjacency)
        + BEND_WEIGHT * bending(control, tile_rows, tile_cols)
        + DAMPING * control
    )


def total_squares(residual):
    return lax.psum(jnp.sum(residual * residual), ("col", "row"))


def shards(names, start_field, seam_target, seam_rows, seam_band, seam_frac, adjacency):
    tile_rows, tile_cols = (adjacency.shape[1], adjacency.shape[2])
    samples = seam_rows.shape[2] // tile_cols
    along_cells = seam_rows.reshape(4, tile_rows, tile_cols, samples)
    across_cells = seam_band.reshape(4, tile_rows, tile_cols, samples)
    frac_cells = seam_frac.reshape(4, 2, tile_rows, tile_cols, samples)
    tables = [
        make_tables(along_cells[facing], across_cells[facing], frac_cells[facing])
        for facing in range(4)
    ]
    target_cells = seam_target.reshape(2, 2, tile_rows, tile_cols, samples)
    target = (target_cells[0], target_cells[1])
    control = start_field
    gradient = seam_term(control, target, tables, adjacency) + BEND_WEIGHT * bending(
        control, tile_rows, tile_cols
    )
    residual = -gradient
    update = jnp.zeros_like(control)
    direction = residual
    norm_now = None
    for iteration in range(ITERS):
        hess_image = hessian_apply(direction, tables, adjacency)
        last = iteration == ITERS - 1
        parts = [jnp.sum(direction * hess_image)]
        if not last:
            parts += [jnp.sum(hess_image * hess_image)]
            if iteration > 0:
                parts += [jnp.sum(residual * hess_image)]
        if norm_now is None:
            parts += [jnp.sum(residual * residual)]
        sums = global_sum(jnp.stack(parts), names)
        curv = sums[0]
        if norm_now is None:
            norm_now = sums[-1]
        step_size = norm_now / curv
        update = update + step_size * direction
        residual = residual - step_size * hess_image
        if not last:
            image_sq = sums[1]
            cross = sums[2] if iteration > 0 else curv
            norm_next = norm_now - 2.0 * step_size * cross + step_size * step_size * image_sq
            direction = residual + norm_next / norm_now * direction
            norm_now = norm_next
    control = control + update
    return (control, residual)


def solution(mesh):
    placed = (
        P(None, "row", "col"),
        P(None, None, "row", "col"),
        P(None, "row", "col"),
        P(None, "row", "col"),
        P(None, None, "row", "col"),
        P(None, "row", "col"),
    )
    return jax.shard_map(
        functools.partial(shards, tuple(mesh.axis_names)),
        mesh=mesh,
        in_specs=placed,
        out_specs=(P(None, "row", "col"), P(None, "row", "col")),
        check_vma=False,
    )
```

```python
import functools

import jax
import jax.numpy as jnp
from jax import lax
from jax.experimental import pallas as pl
from jax.experimental.pallas import tpu as pltpu
from jax.sharding import PartitionSpec as P

GRID = 32
BAND = 4
ITERS = 3


BEND_WEIGHT = 0.05
DAMPING = 0.5


MESH_ID = pl.DeviceIdType.MESH


def _sum_kernel(names, x_ref, o_ref, row_buf, col_buf, part, row_send, row_recv, col_send, col_recv):
    ncol = lax.axis_size("col")
    nrow = lax.axis_size("row")
    ci = lax.axis_index("col")
    ri = lax.axis_index("row")

    def dev(c, r):
        where = {"col": c, "row": r}
        return tuple(where[n] for n in names)

    barrier = pltpu.get_barrier_semaphore()
    for k in range(1, nrow):
        pl.semaphore_signal(barrier, 1, device_id=dev(ci, (ri + k) % nrow), device_id_type=MESH_ID)
    for k in range(1, ncol):
        pl.semaphore_signal(barrier, 1, device_id=dev((ci + k) % ncol, ri), device_id_type=MESH_ID)
    pl.semaphore_wait(barrier, nrow - 1 + ncol - 1)

    def row_copy(peer, slot):
        return pltpu.make_async_remote_copy(
            src_ref=x_ref, dst_ref=row_buf.at[slot], send_sem=row_send.at[peer],
            recv_sem=row_recv.at[slot], device_id=dev(ci, peer), device_id_type=MESH_ID)

    for k in range(1, nrow):
        row_copy((ri + k) % nrow, ri).start()
    row_buf[ri] = x_ref[...]
    for k in range(1, nrow):
        row_copy((ri + k) % nrow, ri).wait_send()
        peer = (ri + nrow - k) % nrow
        row_copy(peer, peer).wait_recv()
    total = row_buf[0]
    for j in range(1, nrow):
        total = total + row_buf[j]
    part[...] = total

    def col_copy(peer, slot):
        return pltpu.make_async_remote_copy(
            src_ref=part, dst_ref=col_buf.at[slot], send_sem=col_send.at[peer],
            recv_sem=col_recv.at[slot], device_id=dev(peer, ri), device_id_type=MESH_ID)

    for k in range(1, ncol):
        col_copy((ci + k) % ncol, ci).start()
    col_buf[ci] = total
    for k in range(1, ncol):
        col_copy((ci + k) % ncol, ci).wait_send()
        peer = (ci + ncol - k) % ncol
        col_copy(peer, peer).wait_recv()
    total = col_buf[0]
    for j in range(1, ncol):
        total = total + col_buf[j]
    o_ref[...] = total


def global_sum(values, names):
    ncol = lax.axis_size("col")
    nrow = lax.axis_size("row")
    count = values.shape[0]
    tile = jnp.zeros((8, 128), jnp.float32).at[0, :count].set(values)
    summed = pl.pallas_call(
        functools.partial(_sum_kernel, names),
        out_shape=jax.ShapeDtypeStruct((8, 128), jnp.float32),
        in_specs=[pl.BlockSpec(memory_space=pltpu.VMEM)],
        out_specs=pl.BlockSpec(memory_space=pltpu.VMEM),
        scratch_shapes=[
            pltpu.VMEM((nrow, 8, 128), jnp.float32),
            pltpu.VMEM((ncol, 8, 128), jnp.float32),
            pltpu.VMEM((8, 128), jnp.float32),
            pltpu.SemaphoreType.DMA((nrow,)),
            pltpu.SemaphoreType.DMA((nrow,)),
            pltpu.SemaphoreType.DMA((ncol,)),
            pltpu.SemaphoreType.DMA((ncol,)),
        ],
        compiler_params=pltpu.CompilerParams(collective_id=0, has_side_effects=True),
    )(tile)
    return summed[0, :count]


def tile_view(control, tile_rows, tile_cols, points):
    return control.reshape(2, tile_rows, points, tile_cols, points)


def edge_band(tile_grid, facing, band_depth):
    if facing == 0:
        return tile_grid[..., ::-1][..., :band_depth].transpose(0, 1, 3, 2, 4)
    if facing == 1:
        return tile_grid[..., :band_depth].transpose(0, 1, 3, 2, 4)
    if facing == 2:
        return tile_grid[:, :, ::-1][:, :, :band_depth].transpose(0, 1, 3, 4, 2)
    return tile_grid[:, :, :band_depth].transpose(0, 1, 3, 4, 2)


def place_edge(band_part, facing, points):
    band_depth = band_part.shape[4]
    if facing < 2:
        widened = jnp.pad(
            band_part.transpose(0, 1, 3, 2, 4),
            ((0, 0), (0, 0), (0, 0), (0, 0), (0, points - band_depth)),
        )
        if facing == 0:
            return widened[..., ::-1]
        return widened
    widened = jnp.pad(
        band_part.transpose(0, 1, 4, 2, 3),
        ((0, 0), (0, 0), (0, points - band_depth), (0, 0), (0, 0)),
    )
    if facing == 2:
        return widened[:, :, ::-1]
    return widened


def make_tables(along_cell, across, frac_pair):
    weight_along = (frac_pair[0].astype(jnp.float32) + 0.5) / 256.0
    weight_across = (frac_pair[1].astype(jnp.float32) + 0.5) / 256.0
    return (along_cell, across, weight_along, weight_across)


def weight_tables(tables, points, band_depth):
    along_cell, across, weight_along, weight_across = tables
    along_iota = jnp.arange(points, dtype=jnp.int32)[None, None, :, None]
    across_iota = jnp.arange(band_depth, dtype=jnp.int32)[None, None, :, None]
    cell_now = along_cell[:, :, None, :]
    depth_now = across[:, :, None, :]
    frac_along = weight_along[:, :, None, :]
    frac_across = weight_across[:, :, None, :]
    along_table = (1.0 - frac_along) * (along_iota == cell_now).astype(jnp.float32) + frac_along * (
        along_iota == cell_now + 1
    ).astype(jnp.float32)
    across_table = (1.0 - frac_across) * (across_iota == depth_now).astype(
        jnp.float32
    ) + frac_across * (across_iota == depth_now + 1).astype(jnp.float32)
    return (along_table, across_table)


def interpolate(band_part, tables):
    along_table, across_table = weight_tables(tables, band_part.shape[3], band_part.shape[4])
    partial_sum = jnp.einsum(
        "cabiq,abis->cabqs", band_part, along_table, precision=lax.Precision.HIGHEST
    )
    return jnp.sum(partial_sum * across_table[None], axis=3)


def spread_back(residual, tables, points, band_depth):
    along_table, across_table = weight_tables(tables, points, band_depth)
    weighted = residual[:, :, :, None, :] * across_table[None]
    return jnp.einsum("cabqs,abis->cabiq", weighted, along_table, precision=lax.Precision.HIGHEST)


def bending(control, tile_rows, tile_cols):
    grid_view = tile_view(control, tile_rows, tile_cols, GRID)
    inner = (
        grid_view[:, :, :-2, :, 1:-1]
        + grid_view[:, :, 2:, :, 1:-1]
        + grid_view[:, :, 1:-1, :, :-2]
        + grid_view[:, :, 1:-1, :, 2:]
        - 4.0 * grid_view[:, :, 1:-1, :, 1:-1]
    )
    widths = ((0, 0), (0, 0), (1, 1), (0, 0), (1, 1))
    curvature = jnp.pad(inner, widths)
    padded = jnp.pad(curvature, widths)
    result = (
        padded[:, :, :-2, :, 1:-1]
        + padded[:, :, 2:, :, 1:-1]
        + padded[:, :, 1:-1, :, :-2]
        + padded[:, :, 1:-1, :, 2:]
        - 4.0 * curvature
    )
    return result.reshape(control.shape)


def _halo_kernel(names, send_ref, recv_ref, send_sems, recv_sems):
    ncol = lax.axis_size("col")
    nrow = lax.axis_size("row")
    ci = lax.axis_index("col")
    ri = lax.axis_index("row")

    def dev(c, r):
        where = {"col": c, "row": r}
        return tuple(where[n] for n in names)

    peers = [
        dev((ci + 1) % ncol, ri),
        dev((ci + ncol - 1) % ncol, ri),
        dev(ci, (ri + 1) % nrow),
        dev(ci, (ri + nrow - 1) % nrow),
    ]
    barrier = pltpu.get_barrier_semaphore()
    for peer in peers:
        pl.semaphore_signal(barrier, 1, device_id=peer, device_id_type=MESH_ID)
    pl.semaphore_wait(barrier, len(peers))
    copies = [
        pltpu.make_async_remote_copy(
            src_ref=send_ref.at[k], dst_ref=recv_ref.at[k], send_sem=send_sems.at[k],
            recv_sem=recv_sems.at[k], device_id=peers[k], device_id_type=MESH_ID)
        for k in range(4)
    ]
    for copy in copies:
        copy.start()
    for copy in copies:
        copy.wait_send()
        copy.wait_recv()


def halo_exchange(names, to_east, to_west, to_south, to_north):
    slabs = [to_east, to_west, to_south, to_north]
    rows = max(slab.shape[0] for slab in slabs)
    lanes = slabs[0].shape[1]
    stacked = jnp.stack([jnp.pad(slab, ((0, rows - slab.shape[0]), (0, 0))) for slab in slabs])
    got = pl.pallas_call(
        functools.partial(_halo_kernel, names),
        out_shape=jax.ShapeDtypeStruct(stacked.shape, jnp.float32),
        in_specs=[pl.BlockSpec(memory_space=pltpu.VMEM)],
        out_specs=pl.BlockSpec(memory_space=pltpu.VMEM),
        scratch_shapes=[pltpu.SemaphoreType.DMA((4,)), pltpu.SemaphoreType.DMA((4,))],
        compiler_params=pltpu.CompilerParams(collective_id=1, has_side_effects=True),
    )(stacked)
    return [got[k, : slabs[k].shape[0]] for k in range(4)]


def seam_term(control, target, tables, adjacency, names):
    tile_rows, tile_cols = (adjacency.shape[1], adjacency.shape[2])
    grid_view = tile_view(control, tile_rows, tile_cols, GRID)
    edge_parts = [edge_band(grid_view, facing, BAND) for facing in range(4)]
    seam_values = [interpolate(edge_parts[facing], tables[facing]) for facing in range(4)]
    samples = seam_values[0].shape[3]
    col_pos = lax.axis_index("col") * tile_cols + jnp.arange(tile_cols)
    row_pos = lax.axis_index("row") * tile_rows + jnp.arange(tile_rows)
    mask_east = (
        adjacency[0].astype(jnp.float32)
        * (col_pos < lax.axis_size("col") * tile_cols - 1).astype(jnp.float32)[None, :]
    )
    mask_south = (
        adjacency[1].astype(jnp.float32)
        * (row_pos < lax.axis_size("row") * tile_rows - 1).astype(jnp.float32)[:, None]
    )
    own_east = seam_values[0]
    own_south = seam_values[2]
    if target is not None:
        own_east = own_east - target[0]
        own_south = own_south - target[1]
    to_east = jnp.concatenate(
        [
            own_east[:, :, -1].reshape(2 * tile_rows, samples),
            jnp.broadcast_to(mask_east[:, -1:], (tile_rows, samples)),
        ]
    )
    to_west = seam_values[1][:, :, 0].reshape(2 * tile_rows, samples)
    to_south = jnp.concatenate(
        [
            own_south[:, -1].reshape(2 * tile_cols, samples),
            jnp.broadcast_to(mask_south[-1][:, None], (tile_cols, samples)),
        ]
    )
    to_north = seam_values[3][:, 0].reshape(2 * tile_cols, samples)
    got_west, got_east, got_north, got_south = halo_exchange(
        names, to_east, to_west, to_south, to_north
    )
    west_east = got_west[: 2 * tile_rows].reshape(2, tile_rows, 1, samples)
    west_mask = got_west[2 * tile_rows :].reshape(1, tile_rows, 1, samples)
    east_next = got_east.reshape(2, tile_rows, 1, samples)
    north_south = got_north[: 2 * tile_cols].reshape(2, 1, tile_cols, samples)
    north_mask = got_north[2 * tile_cols :].reshape(1, 1, tile_cols, samples)
    south_next = got_south.reshape(2, 1, tile_cols, samples)
    west_next = jnp.concatenate([seam_values[1][:, :, 1:], east_next], axis=2)
    north_next = jnp.concatenate([seam_values[3][:, 1:], south_next], axis=1)
    resid_east = (own_east - west_next) * mask_east[None, :, :, None]
    resid_south = (own_south - north_next) * mask_south[None, :, :, None]
    from_west = (west_east - seam_values[1][:, :, :1]) * west_mask
    from_north = (north_south - seam_values[3][:, :1]) * north_mask
    resid_west = -jnp.concatenate([from_west, resid_east[:, :, :-1]], axis=2)
    resid_north = -jnp.concatenate([from_north, resid_south[:, :-1]], axis=1)
    residuals = [resid_east, resid_west, resid_south, resid_north]
    spread_parts = [
        spread_back(residuals[facing], tables[facing], GRID, BAND) for facing in range(4)
    ]
    summed = (
        place_edge(spread_parts[0], 0, GRID)
        + place_edge(spread_parts[1], 1, GRID)
        + place_edge(spread_parts[2], 2, GRID)
        + place_edge(spread_parts[3], 3, GRID)
    )
    return summed.reshape(control.shape)


def hessian_apply(control, tables, adjacency, names):
    tile_rows, tile_cols = (adjacency.shape[1], adjacency.shape[2])
    return (
        seam_term(control, None, tables, adjacency, names)
        + BEND_WEIGHT * bending(control, tile_rows, tile_cols)
        + DAMPING * control
    )


def shards(names, start_field, seam_target, seam_rows, seam_band, seam_frac, adjacency):
    tile_rows, tile_cols = (adjacency.shape[1], adjacency.shape[2])
    samples = seam_rows.shape[2] // tile_cols
    along_cells = seam_rows.reshape(4, tile_rows, tile_cols, samples)
    across_cells = seam_band.reshape(4, tile_rows, tile_cols, samples)
    frac_cells = seam_frac.reshape(4, 2, tile_rows, tile_cols, samples)
    tables = [
        make_tables(along_cells[facing], across_cells[facing], frac_cells[facing])
        for facing in range(4)
    ]
    target_cells = seam_target.reshape(2, 2, tile_rows, tile_cols, samples)
    target = (target_cells[0], target_cells[1])
    control = start_field
    gradient = seam_term(control, target, tables, adjacency, names) + BEND_WEIGHT * bending(
        control, tile_rows, tile_cols
    )
    residual = -gradient
    update = jnp.zeros_like(control)
    direction = residual
    norm_now = None
    for iteration in range(ITERS):
        hess_image = hessian_apply(direction, tables, adjacency, names)
        last = iteration == ITERS - 1
        parts = [jnp.sum(direction * hess_image)]
        if not last:
            parts += [jnp.sum(hess_image * hess_image)]
            if iteration > 0:
                parts += [jnp.sum(residual * hess_image)]
        if norm_now is None:
            parts += [jnp.sum(residual * residual)]
        sums = global_sum(jnp.stack(parts), names)
        curv = sums[0]
        if norm_now is None:
            norm_now = sums[-1]
        step_size = norm_now / curv
        update = update + step_size * direction
        residual = residual - step_size * hess_image
        if not last:
            image_sq = sums[1]
            cross = sums[2] if iteration > 0 else curv
            norm_next = norm_now - 2.0 * step_size * cross + step_size * step_size * image_sq
            direction = residual + norm_next / norm_now * direction
            norm_now = norm_next
    control = control + update
    return (control, residual)


def solution(mesh):
    placed = (
        P(None, "row", "col"),
        P(None, None, "row", "col"),
        P(None, "row", "col"),
        P(None, "row", "col"),
        P(None, None, "row", "col"),
        P(None, "row", "col"),
    )
    return jax.shard_map(
        functools.partial(shards, tuple(mesh.axis_names)),
        mesh=mesh,
        in_specs=placed,
        out_specs=(P(None, "row", "col"), P(None, "row", "col")),
        check_vma=False,
    )
```

```python
import functools

import jax
import jax.numpy as jnp
from jax import lax
from jax.experimental import pallas as pl
from jax.experimental.pallas import tpu as pltpu
from jax.sharding import PartitionSpec as P

GRID = 32
BAND = 4
ITERS = 3


BEND_WEIGHT = 0.05
DAMPING = 0.5


MESH_ID = pl.DeviceIdType.MESH


def _sum_kernel(names, with_halo, x_ref, *refs):
    if with_halo:
        (halo_ref, o_ref, halo_out, row_buf, col_buf, part, row_send, row_recv, col_send,
         col_recv, halo_send, halo_recv) = refs
    else:
        o_ref, row_buf, col_buf, part, row_send, row_recv, col_send, col_recv = refs
    ncol = lax.axis_size("col")
    nrow = lax.axis_size("row")
    ci = lax.axis_index("col")
    ri = lax.axis_index("row")

    def dev(c, r):
        where = {"col": c, "row": r}
        return tuple(where[n] for n in names)

    barrier = pltpu.get_barrier_semaphore()
    for k in range(1, nrow):
        pl.semaphore_signal(barrier, 1, device_id=dev(ci, (ri + k) % nrow), device_id_type=MESH_ID)
    for k in range(1, ncol):
        pl.semaphore_signal(barrier, 1, device_id=dev((ci + k) % ncol, ri), device_id_type=MESH_ID)
    pl.semaphore_wait(barrier, nrow - 1 + ncol - 1)

    halo_copies = []
    if with_halo:
        peers = [
            dev((ci + 1) % ncol, ri),
            dev((ci + ncol - 1) % ncol, ri),
            dev(ci, (ri + 1) % nrow),
            dev(ci, (ri + nrow - 1) % nrow),
        ]
        halo_copies = [
            pltpu.make_async_remote_copy(
                src_ref=halo_ref.at[k], dst_ref=halo_out.at[k], send_sem=halo_send.at[k],
                recv_sem=halo_recv.at[k], device_id=peers[k], device_id_type=MESH_ID)
            for k in range(4)
        ]
        for copy in halo_copies:
            copy.start()

    def row_copy(peer, slot):
        return pltpu.make_async_remote_copy(
            src_ref=x_ref, dst_ref=row_buf.at[slot], send_sem=row_send.at[peer],
            recv_sem=row_recv.at[slot], device_id=dev(ci, peer), device_id_type=MESH_ID)

    for k in range(1, nrow):
        row_copy((ri + k) % nrow, ri).start()
    row_buf[ri] = x_ref[...]
    for k in range(1, nrow):
        row_copy((ri + k) % nrow, ri).wait_send()
        peer = (ri + nrow - k) % nrow
        row_copy(peer, peer).wait_recv()
    total = row_buf[0]
    for j in range(1, nrow):
        total = total + row_buf[j]
    part[...] = total

    def col_copy(peer, slot):
        return pltpu.make_async_remote_copy(
            src_ref=part, dst_ref=col_buf.at[slot], send_sem=col_send.at[peer],
            recv_sem=col_recv.at[slot], device_id=dev(peer, ri), device_id_type=MESH_ID)

    for k in range(1, ncol):
        col_copy((ci + k) % ncol, ci).start()
    col_buf[ci] = total
    for k in range(1, ncol):
        col_copy((ci + k) % ncol, ci).wait_send()
        peer = (ci + ncol - k) % ncol
        col_copy(peer, peer).wait_recv()
    total = col_buf[0]
    for j in range(1, ncol):
        total = total + col_buf[j]
    o_ref[...] = total
    for copy in halo_copies:
        copy.wait_send()
        copy.wait_recv()


def global_sum(values, names, halo=None):
    ncol = lax.axis_size("col")
    nrow = lax.axis_size("row")
    count = values.shape[0]
    tile = jnp.zeros((8, 128), jnp.float32).at[0, :count].set(values)
    with_halo = halo is not None
    operands = [tile]
    out_shape = [jax.ShapeDtypeStruct((8, 128), jnp.float32)]
    scratch = [
        pltpu.VMEM((nrow, 8, 128), jnp.float32),
        pltpu.VMEM((ncol, 8, 128), jnp.float32),
        pltpu.VMEM((8, 128), jnp.float32),
        pltpu.SemaphoreType.DMA((nrow,)),
        pltpu.SemaphoreType.DMA((nrow,)),
        pltpu.SemaphoreType.DMA((ncol,)),
        pltpu.SemaphoreType.DMA((ncol,)),
    ]
    if with_halo:
        stacked, unstack = pack_slabs(halo)
        operands.append(stacked)
        out_shape.append(jax.ShapeDtypeStruct(stacked.shape, jnp.float32))
        scratch += [pltpu.SemaphoreType.DMA((4,)), pltpu.SemaphoreType.DMA((4,))]
    got = pl.pallas_call(
        functools.partial(_sum_kernel, names, with_halo),
        out_shape=tuple(out_shape),
        in_specs=[pl.BlockSpec(memory_space=pltpu.VMEM)] * len(operands),
        out_specs=tuple(pl.BlockSpec(memory_space=pltpu.VMEM) for _ in out_shape),
        scratch_shapes=scratch,
        compiler_params=pltpu.CompilerParams(
            collective_id=2 if with_halo else 0, has_side_effects=True
        ),
    )(*operands)
    summed = got[0][0, :count]
    if with_halo:
        return summed, unstack(got[1])
    return summed


def pack_slabs(slabs):
    rows = max(slab.shape[0] for slab in slabs)
    stacked = jnp.stack([jnp.pad(slab, ((0, rows - slab.shape[0]), (0, 0))) for slab in slabs])

    def unstack(got):
        return [got[k, : slabs[k].shape[0]] for k in range(len(slabs))]

    return stacked, unstack


def tile_view(control, tile_rows, tile_cols, points):
    return control.reshape(2, tile_rows, points, tile_cols, points)


def edge_band(tile_grid, facing, band_depth):
    if facing == 0:
        return tile_grid[..., ::-1][..., :band_depth].transpose(0, 1, 3, 2, 4)
    if facing == 1:
        return tile_grid[..., :band_depth].transpose(0, 1, 3, 2, 4)
    if facing == 2:
        return tile_grid[:, :, ::-1][:, :, :band_depth].transpose(0, 1, 3, 4, 2)
    return tile_grid[:, :, :band_depth].transpose(0, 1, 3, 4, 2)


def place_edge(band_part, facing, points):
    band_depth = band_part.shape[4]
    if facing < 2:
        widened = jnp.pad(
            band_part.transpose(0, 1, 3, 2, 4),
            ((0, 0), (0, 0), (0, 0), (0, 0), (0, points - band_depth)),
        )
        if facing == 0:
            return widened[..., ::-1]
        return widened
    widened = jnp.pad(
        band_part.transpose(0, 1, 4, 2, 3),
        ((0, 0), (0, 0), (0, points - band_depth), (0, 0), (0, 0)),
    )
    if facing == 2:
        return widened[:, :, ::-1]
    return widened


def make_tables(along_cell, across, frac_pair):
    weight_along = (frac_pair[0].astype(jnp.float32) + 0.5) / 256.0
    weight_across = (frac_pair[1].astype(jnp.float32) + 0.5) / 256.0
    return (along_cell, across, weight_along, weight_across)


def weight_tables(tables, points, band_depth):
    along_cell, across, weight_along, weight_across = tables
    along_iota = jnp.arange(points, dtype=jnp.int32)[None, None, :, None]
    across_iota = jnp.arange(band_depth, dtype=jnp.int32)[None, None, :, None]
    cell_now = along_cell[:, :, None, :]
    depth_now = across[:, :, None, :]
    frac_along = weight_along[:, :, None, :]
    frac_across = weight_across[:, :, None, :]
    along_table = (1.0 - frac_along) * (along_iota == cell_now).astype(jnp.float32) + frac_along * (
        along_iota == cell_now + 1
    ).astype(jnp.float32)
    across_table = (1.0 - frac_across) * (across_iota == depth_now).astype(
        jnp.float32
    ) + frac_across * (across_iota == depth_now + 1).astype(jnp.float32)
    return (along_table, across_table)


def interpolate(band_part, tables):
    along_table, across_table = weight_tables(tables, band_part.shape[3], band_part.shape[4])
    partial_sum = jnp.einsum(
        "cabiq,abis->cabqs", band_part, along_table, precision=lax.Precision.HIGHEST
    )
    return jnp.sum(partial_sum * across_table[None], axis=3)


def spread_back(residual, tables, points, band_depth):
    along_table, across_table = weight_tables(tables, points, band_depth)
    weighted = residual[:, :, :, None, :] * across_table[None]
    return jnp.einsum("cabqs,abis->cabiq", weighted, along_table, precision=lax.Precision.HIGHEST)


def bending(control, tile_rows, tile_cols):
    grid_view = tile_view(control, tile_rows, tile_cols, GRID)
    inner = (
        grid_view[:, :, :-2, :, 1:-1]
        + grid_view[:, :, 2:, :, 1:-1]
        + grid_view[:, :, 1:-1, :, :-2]
        + grid_view[:, :, 1:-1, :, 2:]
        - 4.0 * grid_view[:, :, 1:-1, :, 1:-1]
    )
    widths = ((0, 0), (0, 0), (1, 1), (0, 0), (1, 1))
    curvature = jnp.pad(inner, widths)
    padded = jnp.pad(curvature, widths)
    result = (
        padded[:, :, :-2, :, 1:-1]
        + padded[:, :, 2:, :, 1:-1]
        + padded[:, :, 1:-1, :, :-2]
        + padded[:, :, 1:-1, :, 2:]
        - 4.0 * curvature
    )
    return result.reshape(control.shape)


def _halo_kernel(names, send_ref, recv_ref, send_sems, recv_sems):
    ncol = lax.axis_size("col")
    nrow = lax.axis_size("row")
    ci = lax.axis_index("col")
    ri = lax.axis_index("row")

    def dev(c, r):
        where = {"col": c, "row": r}
        return tuple(where[n] for n in names)

    peers = [
        dev((ci + 1) % ncol, ri),
        dev((ci + ncol - 1) % ncol, ri),
        dev(ci, (ri + 1) % nrow),
        dev(ci, (ri + nrow - 1) % nrow),
    ]
    barrier = pltpu.get_barrier_semaphore()
    for peer in peers:
        pl.semaphore_signal(barrier, 1, device_id=peer, device_id_type=MESH_ID)
    pl.semaphore_wait(barrier, len(peers))
    copies = [
        pltpu.make_async_remote_copy(
            src_ref=send_ref.at[k], dst_ref=recv_ref.at[k], send_sem=send_sems.at[k],
            recv_sem=recv_sems.at[k], device_id=peers[k], device_id_type=MESH_ID)
        for k in range(4)
    ]
    for copy in copies:
        copy.start()
    for copy in copies:
        copy.wait_send()
        copy.wait_recv()


def halo_exchange(names, kernel_id, to_east, to_west, to_south, to_north):
    slabs = [to_east, to_west, to_south, to_north]
    rows = max(slab.shape[0] for slab in slabs)
    lanes = slabs[0].shape[1]
    stacked = jnp.stack([jnp.pad(slab, ((0, rows - slab.shape[0]), (0, 0))) for slab in slabs])
    got = pl.pallas_call(
        functools.partial(_halo_kernel, names),
        out_shape=jax.ShapeDtypeStruct(stacked.shape, jnp.float32),
        in_specs=[pl.BlockSpec(memory_space=pltpu.VMEM)],
        out_specs=pl.BlockSpec(memory_space=pltpu.VMEM),
        scratch_shapes=[pltpu.SemaphoreType.DMA((4,)), pltpu.SemaphoreType.DMA((4,))],
        compiler_params=pltpu.CompilerParams(collective_id=kernel_id, has_side_effects=True),
    )(stacked)
    return [got[k, : slabs[k].shape[0]] for k in range(4)]


def seam_masks(adjacency):
    tile_rows, tile_cols = (adjacency.shape[1], adjacency.shape[2])
    col_pos = lax.axis_index("col") * tile_cols + jnp.arange(tile_cols)
    row_pos = lax.axis_index("row") * tile_rows + jnp.arange(tile_rows)
    mask_east = (
        adjacency[0].astype(jnp.float32)
        * (col_pos < lax.axis_size("col") * tile_cols - 1).astype(jnp.float32)[None, :]
    )
    mask_south = (
        adjacency[1].astype(jnp.float32)
        * (row_pos < lax.axis_size("row") * tile_rows - 1).astype(jnp.float32)[:, None]
    )
    return mask_east, mask_south


def seam_values_of(field, tables, tile_rows, tile_cols):
    grid_view = tile_view(field, tile_rows, tile_cols, GRID)
    return [interpolate(edge_band(grid_view, facing, BAND), tables[facing]) for facing in range(4)]


def edge_tables(tables):
    return [
        tuple(part[:, -1:] for part in tables[0]),
        tuple(part[:, :1] for part in tables[1]),
        tuple(part[-1:] for part in tables[2]),
        tuple(part[:1] for part in tables[3]),
    ]


def edge_values(field, edge_tabs, tile_rows, tile_cols):
    grid_view = tile_view(field, tile_rows, tile_cols, GRID)
    bands = [edge_band(grid_view, facing, BAND) for facing in range(4)]
    strips = [bands[0][:, :, -1:], bands[1][:, :, :1], bands[2][:, -1:], bands[3][:, :1]]
    return [interpolate(strips[facing], edge_tabs[facing]) for facing in range(4)]


def payload(edges):
    samples = edges[0].shape[3]
    return [edge.reshape(-1, samples) for edge in edges]


def seam_finish(seam_values, target, got, masks, far_masks):
    mask_east, mask_south = masks
    west_mask, north_mask = far_masks
    samples = seam_values[0].shape[3]
    tile_rows, tile_cols = mask_east.shape
    own_east = seam_values[0]
    own_south = seam_values[2]
    if target is not None:
        own_east = own_east - target[0]
        own_south = own_south - target[1]
    west_east = got[0].reshape(2, tile_rows, 1, samples)
    east_next = got[1].reshape(2, tile_rows, 1, samples)
    north_south = got[2].reshape(2, 1, tile_cols, samples)
    south_next = got[3].reshape(2, 1, tile_cols, samples)
    west_next = jnp.concatenate([seam_values[1][:, :, 1:], east_next], axis=2)
    north_next = jnp.concatenate([seam_values[3][:, 1:], south_next], axis=1)
    resid_east = (own_east - west_next) * mask_east[None, :, :, None]
    resid_south = (own_south - north_next) * mask_south[None, :, :, None]
    from_west = (west_east - seam_values[1][:, :, :1]) * west_mask
    from_north = (north_south - seam_values[3][:, :1]) * north_mask
    resid_west = -jnp.concatenate([from_west, resid_east[:, :, :-1]], axis=2)
    resid_north = -jnp.concatenate([from_north, resid_south[:, :-1]], axis=1)
    return [resid_east, resid_west, resid_south, resid_north]


def spread_all(residuals, tables, shape):
    spread_parts = [
        spread_back(residuals[facing], tables[facing], GRID, BAND) for facing in range(4)
    ]
    summed = (
        place_edge(spread_parts[0], 0, GRID)
        + place_edge(spread_parts[1], 1, GRID)
        + place_edge(spread_parts[2], 2, GRID)
        + place_edge(spread_parts[3], 3, GRID)
    )
    return summed.reshape(shape)


def shards(names, start_field, seam_target, seam_rows, seam_band, seam_frac, adjacency):
    tile_rows, tile_cols = (adjacency.shape[1], adjacency.shape[2])
    samples = seam_rows.shape[2] // tile_cols
    along_cells = seam_rows.reshape(4, tile_rows, tile_cols, samples)
    across_cells = seam_band.reshape(4, tile_rows, tile_cols, samples)
    frac_cells = seam_frac.reshape(4, 2, tile_rows, tile_cols, samples)
    tables = [
        make_tables(along_cells[facing], across_cells[facing], frac_cells[facing])
        for facing in range(4)
    ]
    edge_tabs = edge_tables(tables)
    target_cells = seam_target.reshape(2, 2, tile_rows, tile_cols, samples)
    target = (target_cells[0], target_cells[1])
    masks = seam_masks(adjacency)
    mask_east, mask_south = masks
    control = start_field

    values = seam_values_of(control, tables, tile_rows, tile_cols)
    own_edges = [
        values[0][:, :, -1:] - target[0][:, :, -1:],
        values[1][:, :, :1],
        values[2][:, -1:] - target[1][:, -1:],
        values[3][:, :1],
    ]
    slabs = payload(own_edges)
    slabs[0] = jnp.concatenate(
        [slabs[0], jnp.broadcast_to(mask_east[:, -1:], (tile_rows, samples))]
    )
    slabs[2] = jnp.concatenate(
        [slabs[2], jnp.broadcast_to(mask_south[-1][:, None], (tile_cols, samples))]
    )
    got = halo_exchange(names, 1, *slabs)
    far_masks = (
        got[0][2 * tile_rows :].reshape(1, tile_rows, 1, samples),
        got[2][2 * tile_cols :].reshape(1, 1, tile_cols, samples),
    )
    got = [got[0][: 2 * tile_rows], got[1], got[2][: 2 * tile_cols], got[3]]
    residuals = seam_finish(values, target, got, masks, far_masks)
    gradient = spread_all(residuals, tables, control.shape) + BEND_WEIGHT * bending(
        control, tile_rows, tile_cols
    )
    residual = -gradient
    update = jnp.zeros_like(control)
    direction = residual
    values = seam_values_of(direction, tables, tile_rows, tile_cols)
    own_edges = [values[0][:, :, -1:], values[1][:, :, :1], values[2][:, -1:], values[3][:, :1]]
    far_direction = halo_exchange(names, 3, *payload(own_edges))
    far_residual = far_direction
    norm_now = None
    for iteration in range(ITERS):
        residuals = seam_finish(values, None, far_direction, masks, far_masks)
        hess_image = (
            spread_all(residuals, tables, direction.shape)
            + BEND_WEIGHT * bending(direction, tile_rows, tile_cols)
            + DAMPING * direction
        )
        last = iteration == ITERS - 1
        parts = [jnp.sum(direction * hess_image)]
        if not last:
            parts += [jnp.sum(hess_image * hess_image)]
            if iteration > 0:
                parts += [jnp.sum(residual * hess_image)]
        if norm_now is None:
            parts += [jnp.sum(residual * residual)]
        if last:
            sums = global_sum(jnp.stack(parts), names)
        else:
            image_edges = payload(edge_values(hess_image, edge_tabs, tile_rows, tile_cols))
            sums, far_image = global_sum(jnp.stack(parts), names, image_edges)
        curv = sums[0]
        if norm_now is None:
            norm_now = sums[-1]
        step_size = norm_now / curv
        update = update + step_size * direction
        residual = residual - step_size * hess_image
        if not last:
            image_sq = sums[1]
            cross = sums[2] if iteration > 0 else curv
            norm_next = norm_now - 2.0 * step_size * cross + step_size * step_size * image_sq
            ratio = norm_next / norm_now
            direction = residual + ratio * direction
            far_residual = [
                far - step_size * image for far, image in zip(far_residual, far_image)
            ]
            far_direction = [
                far + ratio * old for far, old in zip(far_residual, far_direction)
            ]
            values = seam_values_of(direction, tables, tile_rows, tile_cols)
            norm_now = norm_next
    control = control + update
    return (control, residual)


def solution(mesh):
    placed = (
        P(None, "row", "col"),
        P(None, None, "row", "col"),
        P(None, "row", "col"),
        P(None, "row", "col"),
        P(None, None, "row", "col"),
        P(None, "row", "col"),
    )
    return jax.shard_map(
        functools.partial(shards, tuple(mesh.axis_names)),
        mesh=mesh,
        in_specs=placed,
        out_specs=(P(None, "row", "col"), P(None, "row", "col")),
        check_vma=False,
    )
```

```python
import functools

import jax
import jax.numpy as jnp
from jax import lax
from jax.experimental import pallas as pl
from jax.experimental.pallas import tpu as pltpu
from jax.sharding import PartitionSpec as P

GRID = 32
BAND = 4
ITERS = 3


BEND_WEIGHT = 0.05
DAMPING = 0.5


MESH_ID = pl.DeviceIdType.MESH


def _cg_kernel(names, first, last, d_ref, h_ref, r_ref, u_ref, rr_ref, *refs):
    if last:
        u_out, r_out, row_buf, col_buf, mine, part, row_send, row_recv, col_send, col_recv = refs
    else:
        (u_out, r_out, d_out, rr_out, row_buf, col_buf, mine, part, row_send, row_recv, col_send,
         col_recv) = refs
    ncol = lax.axis_size("col")
    nrow = lax.axis_size("row")
    ci = lax.axis_index("col")
    ri = lax.axis_index("row")

    def dev(c, r):
        where = {"col": c, "row": r}
        return tuple(where[n] for n in names)

    direction = d_ref[...]
    image = h_ref[...]
    residual = r_ref[...]

    def total(x):
        return jnp.sum(jnp.sum(x, axis=0, keepdims=True), axis=1, keepdims=True)

    parts = [total(direction * image)]
    if not last:
        parts += [total(image * image), total(residual * image)]
    if first:
        parts += [total(residual * residual)]
    lane = lax.broadcasted_iota(jnp.int32, (8, 128), 1)
    sub = lax.broadcasted_iota(jnp.int32, (8, 128), 0)
    tile = jnp.zeros((8, 128), jnp.float32)
    for k, value in enumerate(parts):
        tile = jnp.where((sub == 0) & (lane == k), value, tile)
    mine[...] = tile

    barrier = pltpu.get_barrier_semaphore()
    for k in range(1, nrow):
        pl.semaphore_signal(barrier, 1, device_id=dev(ci, (ri + k) % nrow), device_id_type=MESH_ID)
    for k in range(1, ncol):
        pl.semaphore_signal(barrier, 1, device_id=dev((ci + k) % ncol, ri), device_id_type=MESH_ID)
    pl.semaphore_wait(barrier, nrow - 1 + ncol - 1)

    def row_copy(peer, slot):
        return pltpu.make_async_remote_copy(
            src_ref=mine, dst_ref=row_buf.at[slot], send_sem=row_send.at[peer],
            recv_sem=row_recv.at[slot], device_id=dev(ci, peer), device_id_type=MESH_ID)

    for k in range(1, nrow):
        row_copy((ri + k) % nrow, ri).start()
    row_buf[ri] = tile
    for k in range(1, nrow):
        row_copy((ri + k) % nrow, ri).wait_send()
        peer = (ri + nrow - k) % nrow
        row_copy(peer, peer).wait_recv()
    summed = row_buf[0]
    for j in range(1, nrow):
        summed = summed + row_buf[j]
    part[...] = summed

    def col_copy(peer, slot):
        return pltpu.make_async_remote_copy(
            src_ref=part, dst_ref=col_buf.at[slot], send_sem=col_send.at[peer],
            recv_sem=col_recv.at[slot], device_id=dev(peer, ri), device_id_type=MESH_ID)

    for k in range(1, ncol):
        col_copy((ci + k) % ncol, ci).start()
    col_buf[ci] = summed
    for k in range(1, ncol):
        col_copy((ci + k) % ncol, ci).wait_send()
        peer = (ci + ncol - k) % ncol
        col_copy(peer, peer).wait_recv()
    summed = col_buf[0]
    for j in range(1, ncol):
        summed = summed + col_buf[j]

    def pick(k):
        return jnp.sum(jnp.where((sub == 0) & (lane == k), summed, 0.0), axis=(0, 1), keepdims=True)

    curv = pick(0)
    norm_now = pick(len(parts) - 1) if first else rr_ref[0:1, 0:1]
    step_size = norm_now / curv
    u_out[...] = u_ref[...] + step_size * direction
    residual = residual - step_size * image
    r_out[...] = residual
    if not last:
        image_sq = pick(1)
        cross = curv if first else pick(2)
        norm_next = norm_now - 2.0 * step_size * cross + step_size * step_size * image_sq
        d_out[...] = residual + norm_next / norm_now * direction
        rr_out[...] = jnp.broadcast_to(norm_next, (8, 128))


def cg_step(names, iteration, direction, image, residual, update, norm_tile):
    ncol = lax.axis_size("col")
    nrow = lax.axis_size("row")
    first = iteration == 0
    last = iteration == ITERS - 1
    shape = direction.shape
    flat = (shape[0] * shape[1], shape[2])
    fields = [x.reshape(flat) for x in (direction, image, residual, update)]
    field_type = jax.ShapeDtypeStruct(flat, jnp.float32)
    out_shape = [field_type, field_type]
    if not last:
        out_shape += [field_type, jax.ShapeDtypeStruct((8, 128), jnp.float32)]
    got = pl.pallas_call(
        functools.partial(_cg_kernel, names, first, last),
        out_shape=tuple(out_shape),
        in_specs=[pl.BlockSpec(memory_space=pltpu.VMEM)] * 5,
        out_specs=tuple(pl.BlockSpec(memory_space=pltpu.VMEM) for _ in out_shape),
        scratch_shapes=[
            pltpu.VMEM((nrow, 8, 128), jnp.float32),
            pltpu.VMEM((ncol, 8, 128), jnp.float32),
            pltpu.VMEM((8, 128), jnp.float32),
            pltpu.VMEM((8, 128), jnp.float32),
            pltpu.SemaphoreType.DMA((nrow,)),
            pltpu.SemaphoreType.DMA((nrow,)),
            pltpu.SemaphoreType.DMA((ncol,)),
            pltpu.SemaphoreType.DMA((ncol,)),
        ],
        compiler_params=pltpu.CompilerParams(
            collective_id=10 + iteration, has_side_effects=True
        ),
    )(*fields, norm_tile)
    update = got[0].reshape(shape)
    residual = got[1].reshape(shape)
    if last:
        return update, residual, None, None
    return update, residual, got[2].reshape(shape), got[3]


def tile_view(control, tile_rows, tile_cols, points):
    return control.reshape(2, tile_rows, points, tile_cols, points)


def edge_band(tile_grid, facing, band_depth):
    if facing == 0:
        return tile_grid[..., ::-1][..., :band_depth].transpose(0, 1, 3, 2, 4)
    if facing == 1:
        return tile_grid[..., :band_depth].transpose(0, 1, 3, 2, 4)
    if facing == 2:
        return tile_grid[:, :, ::-1][:, :, :band_depth].transpose(0, 1, 3, 4, 2)
    return tile_grid[:, :, :band_depth].transpose(0, 1, 3, 4, 2)


def place_edge(band_part, facing, points):
    band_depth = band_part.shape[4]
    if facing < 2:
        widened = jnp.pad(
            band_part.transpose(0, 1, 3, 2, 4),
            ((0, 0), (0, 0), (0, 0), (0, 0), (0, points - band_depth)),
        )
        if facing == 0:
            return widened[..., ::-1]
        return widened
    widened = jnp.pad(
        band_part.transpose(0, 1, 4, 2, 3),
        ((0, 0), (0, 0), (0, points - band_depth), (0, 0), (0, 0)),
    )
    if facing == 2:
        return widened[:, :, ::-1]
    return widened


def make_tables(along_cell, across, frac_pair):
    weight_along = (frac_pair[0].astype(jnp.float32) + 0.5) / 256.0
    weight_across = (frac_pair[1].astype(jnp.float32) + 0.5) / 256.0
    return (along_cell, across, weight_along, weight_across)


def weight_tables(tables, points, band_depth):
    along_cell, across, weight_along, weight_across = tables
    along_iota = jnp.arange(points, dtype=jnp.int32)[None, None, :, None]
    across_iota = jnp.arange(band_depth, dtype=jnp.int32)[None, None, :, None]
    cell_now = along_cell[:, :, None, :]
    depth_now = across[:, :, None, :]
    frac_along = weight_along[:, :, None, :]
    frac_across = weight_across[:, :, None, :]
    along_table = (1.0 - frac_along) * (along_iota == cell_now).astype(jnp.float32) + frac_along * (
        along_iota == cell_now + 1
    ).astype(jnp.float32)
    across_table = (1.0 - frac_across) * (across_iota == depth_now).astype(
        jnp.float32
    ) + frac_across * (across_iota == depth_now + 1).astype(jnp.float32)
    return (along_table, across_table)


def interpolate(band_part, tables):
    along_table, across_table = weight_tables(tables, band_part.shape[3], band_part.shape[4])
    partial_sum = jnp.einsum(
        "cabiq,abis->cabqs", band_part, along_table, precision=lax.Precision.HIGHEST
    )
    return jnp.sum(partial_sum * across_table[None], axis=3)


def spread_back(residual, tables, points, band_depth):
    along_table, across_table = weight_tables(tables, points, band_depth)
    weighted = residual[:, :, :, None, :] * across_table[None]
    return jnp.einsum("cabqs,abis->cabiq", weighted, along_table, precision=lax.Precision.HIGHEST)


def bending(control, tile_rows, tile_cols):
    grid_view = tile_view(control, tile_rows, tile_cols, GRID)
    inner = (
        grid_view[:, :, :-2, :, 1:-1]
        + grid_view[:, :, 2:, :, 1:-1]
        + grid_view[:, :, 1:-1, :, :-2]
        + grid_view[:, :, 1:-1, :, 2:]
        - 4.0 * grid_view[:, :, 1:-1, :, 1:-1]
    )
    widths = ((0, 0), (0, 0), (1, 1), (0, 0), (1, 1))
    curvature = jnp.pad(inner, widths)
    padded = jnp.pad(curvature, widths)
    result = (
        padded[:, :, :-2, :, 1:-1]
        + padded[:, :, 2:, :, 1:-1]
        + padded[:, :, 1:-1, :, :-2]
        + padded[:, :, 1:-1, :, 2:]
        - 4.0 * curvature
    )
    return result.reshape(control.shape)


def _halo_kernel(names, send_ref, recv_ref, send_sems, recv_sems):
    ncol = lax.axis_size("col")
    nrow = lax.axis_size("row")
    ci = lax.axis_index("col")
    ri = lax.axis_index("row")

    def dev(c, r):
        where = {"col": c, "row": r}
        return tuple(where[n] for n in names)

    peers = [
        dev((ci + 1) % ncol, ri),
        dev((ci + ncol - 1) % ncol, ri),
        dev(ci, (ri + 1) % nrow),
        dev(ci, (ri + nrow - 1) % nrow),
    ]
    barrier = pltpu.get_barrier_semaphore()
    for peer in peers:
        pl.semaphore_signal(barrier, 1, device_id=peer, device_id_type=MESH_ID)
    pl.semaphore_wait(barrier, len(peers))
    copies = [
        pltpu.make_async_remote_copy(
            src_ref=send_ref.at[k], dst_ref=recv_ref.at[k], send_sem=send_sems.at[k],
            recv_sem=recv_sems.at[k], device_id=peers[k], device_id_type=MESH_ID)
        for k in range(4)
    ]
    for copy in copies:
        copy.start()
    for copy in copies:
        copy.wait_send()
        copy.wait_recv()


def halo_exchange(names, to_east, to_west, to_south, to_north):
    slabs = [to_east, to_west, to_south, to_north]
    rows = max(slab.shape[0] for slab in slabs)
    lanes = slabs[0].shape[1]
    stacked = jnp.stack([jnp.pad(slab, ((0, rows - slab.shape[0]), (0, 0))) for slab in slabs])
    got = pl.pallas_call(
        functools.partial(_halo_kernel, names),
        out_shape=jax.ShapeDtypeStruct(stacked.shape, jnp.float32),
        in_specs=[pl.BlockSpec(memory_space=pltpu.VMEM)],
        out_specs=pl.BlockSpec(memory_space=pltpu.VMEM),
        scratch_shapes=[pltpu.SemaphoreType.DMA((4,)), pltpu.SemaphoreType.DMA((4,))],
        compiler_params=pltpu.CompilerParams(collective_id=1, has_side_effects=True),
    )(stacked)
    return [got[k, : slabs[k].shape[0]] for k in range(4)]


def seam_term(control, target, tables, adjacency, names):
    tile_rows, tile_cols = (adjacency.shape[1], adjacency.shape[2])
    grid_view = tile_view(control, tile_rows, tile_cols, GRID)
    edge_parts = [edge_band(grid_view, facing, BAND) for facing in range(4)]
    seam_values = [interpolate(edge_parts[facing], tables[facing]) for facing in range(4)]
    samples = seam_values[0].shape[3]
    col_pos = lax.axis_index("col") * tile_cols + jnp.arange(tile_cols)
    row_pos = lax.axis_index("row") * tile_rows + jnp.arange(tile_rows)
    mask_east = (
        adjacency[0].astype(jnp.float32)
        * (col_pos < lax.axis_size("col") * tile_cols - 1).astype(jnp.float32)[None, :]
    )
    mask_south = (
        adjacency[1].astype(jnp.float32)
        * (row_pos < lax.axis_size("row") * tile_rows - 1).astype(jnp.float32)[:, None]
    )
    own_east = seam_values[0]
    own_south = seam_values[2]
    if target is not None:
        own_east = own_east - target[0]
        own_south = own_south - target[1]
    to_east = jnp.concatenate(
        [
            own_east[:, :, -1].reshape(2 * tile_rows, samples),
            jnp.broadcast_to(mask_east[:, -1:], (tile_rows, samples)),
        ]
    )
    to_west = seam_values[1][:, :, 0].reshape(2 * tile_rows, samples)
    to_south = jnp.concatenate(
        [
            own_south[:, -1].reshape(2 * tile_cols, samples),
            jnp.broadcast_to(mask_south[-1][:, None], (tile_cols, samples)),
        ]
    )
    to_north = seam_values[3][:, 0].reshape(2 * tile_cols, samples)
    got_west, got_east, got_north, got_south = halo_exchange(
        names, to_east, to_west, to_south, to_north
    )
    west_east = got_west[: 2 * tile_rows].reshape(2, tile_rows, 1, samples)
    west_mask = got_west[2 * tile_rows :].reshape(1, tile_rows, 1, samples)
    east_next = got_east.reshape(2, tile_rows, 1, samples)
    north_south = got_north[: 2 * tile_cols].reshape(2, 1, tile_cols, samples)
    north_mask = got_north[2 * tile_cols :].reshape(1, 1, tile_cols, samples)
    south_next = got_south.reshape(2, 1, tile_cols, samples)
    west_next = jnp.concatenate([seam_values[1][:, :, 1:], east_next], axis=2)
    north_next = jnp.concatenate([seam_values[3][:, 1:], south_next], axis=1)
    resid_east = (own_east - west_next) * mask_east[None, :, :, None]
    resid_south = (own_south - north_next) * mask_south[None, :, :, None]
    from_west = (west_east - seam_values[1][:, :, :1]) * west_mask
    from_north = (north_south - seam_values[3][:, :1]) * north_mask
    resid_west = -jnp.concatenate([from_west, resid_east[:, :, :-1]], axis=2)
    resid_north = -jnp.concatenate([from_north, resid_south[:, :-1]], axis=1)
    residuals = [resid_east, resid_west, resid_south, resid_north]
    spread_parts = [
        spread_back(residuals[facing], tables[facing], GRID, BAND) for facing in range(4)
    ]
    summed = (
        place_edge(spread_parts[0], 0, GRID)
        + place_edge(spread_parts[1], 1, GRID)
        + place_edge(spread_parts[2], 2, GRID)
        + place_edge(spread_parts[3], 3, GRID)
    )
    return summed.reshape(control.shape)


def hessian_apply(control, tables, adjacency, names):
    tile_rows, tile_cols = (adjacency.shape[1], adjacency.shape[2])
    return (
        seam_term(control, None, tables, adjacency, names)
        + BEND_WEIGHT * bending(control, tile_rows, tile_cols)
        + DAMPING * control
    )


def shards(names, start_field, seam_target, seam_rows, seam_band, seam_frac, adjacency):
    tile_rows, tile_cols = (adjacency.shape[1], adjacency.shape[2])
    samples = seam_rows.shape[2] // tile_cols
    along_cells = seam_rows.reshape(4, tile_rows, tile_cols, samples)
    across_cells = seam_band.reshape(4, tile_rows, tile_cols, samples)
    frac_cells = seam_frac.reshape(4, 2, tile_rows, tile_cols, samples)
    tables = [
        make_tables(along_cells[facing], across_cells[facing], frac_cells[facing])
        for facing in range(4)
    ]
    target_cells = seam_target.reshape(2, 2, tile_rows, tile_cols, samples)
    target = (target_cells[0], target_cells[1])
    control = start_field
    gradient = seam_term(control, target, tables, adjacency, names) + BEND_WEIGHT * bending(
        control, tile_rows, tile_cols
    )
    residual = -gradient
    update = jnp.zeros_like(control)
    direction = residual
    norm_tile = jnp.zeros((8, 128), jnp.float32)
    for iteration in range(ITERS):
        hess_image = hessian_apply(direction, tables, adjacency, names)
        update, residual, direction, norm_tile = cg_step(
            names, iteration, direction, hess_image, residual, update, norm_tile
        )
    control = control + update
    return (control, residual)


def solution(mesh):
    placed = (
        P(None, "row", "col"),
        P(None, None, "row", "col"),
        P(None, "row", "col"),
        P(None, "row", "col"),
        P(None, None, "row", "col"),
        P(None, "row", "col"),
    )
    return jax.shard_map(
        functools.partial(shards, tuple(mesh.axis_names)),
        mesh=mesh,
        in_specs=placed,
        out_specs=(P(None, "row", "col"), P(None, "row", "col")),
        check_vma=False,
    )
```

```python
import functools

import jax
import jax.numpy as jnp
from jax import lax
from jax.experimental import pallas as pl
from jax.experimental.pallas import tpu as pltpu
from jax.sharding import PartitionSpec as P

GRID = 32
BAND = 4
ITERS = 3


BEND_WEIGHT = 0.05
DAMPING = 0.5


MESH_ID = pl.DeviceIdType.MESH


def _cg_kernel(names, first, last, d_ref, h_ref, r_ref, u_ref, rr_ref, *refs):
    if last:
        u_out, r_out, row_buf, col_buf, mine, part, row_send, row_recv, col_send, col_recv = refs
    else:
        (u_out, r_out, d_out, rr_out, row_buf, col_buf, mine, part, row_send, row_recv, col_send,
         col_recv) = refs
    ncol = lax.axis_size("col")
    nrow = lax.axis_size("row")
    ci = lax.axis_index("col")
    ri = lax.axis_index("row")

    def dev(c, r):
        where = {"col": c, "row": r}
        return tuple(where[n] for n in names)

    direction = d_ref[...]
    image = h_ref[...]
    residual = r_ref[...]

    def total(x):
        return jnp.sum(jnp.sum(x, axis=0, keepdims=True), axis=1, keepdims=True)

    parts = [total(direction * image)]
    if not last:
        parts += [total(image * image), total(residual * image)]
    if first:
        parts += [total(residual * residual)]
    lane = lax.broadcasted_iota(jnp.int32, (8, 128), 1)
    sub = lax.broadcasted_iota(jnp.int32, (8, 128), 0)
    tile = jnp.zeros((8, 128), jnp.float32)
    for k, value in enumerate(parts):
        tile = jnp.where((sub == 0) & (lane == k), value, tile)
    mine[...] = tile

    barrier = pltpu.get_barrier_semaphore()
    for k in range(1, nrow):
        pl.semaphore_signal(barrier, 1, device_id=dev(ci, (ri + k) % nrow), device_id_type=MESH_ID)
    for k in range(1, ncol):
        pl.semaphore_signal(barrier, 1, device_id=dev((ci + k) % ncol, ri), device_id_type=MESH_ID)
    pl.semaphore_wait(barrier, nrow - 1 + ncol - 1)

    def row_copy(peer, slot):
        return pltpu.make_async_remote_copy(
            src_ref=mine, dst_ref=row_buf.at[slot], send_sem=row_send.at[peer],
            recv_sem=row_recv.at[slot], device_id=dev(ci, peer), device_id_type=MESH_ID)

    for k in range(1, nrow):
        row_copy((ri + k) % nrow, ri).start()
    row_buf[ri] = tile
    for k in range(1, nrow):
        row_copy((ri + k) % nrow, ri).wait_send()
        peer = (ri + nrow - k) % nrow
        row_copy(peer, peer).wait_recv()
    summed = row_buf[0]
    for j in range(1, nrow):
        summed = summed + row_buf[j]
    part[...] = summed

    def col_copy(peer, slot):
        return pltpu.make_async_remote_copy(
            src_ref=part, dst_ref=col_buf.at[slot], send_sem=col_send.at[peer],
            recv_sem=col_recv.at[slot], device_id=dev(peer, ri), device_id_type=MESH_ID)

    for k in range(1, ncol):
        col_copy((ci + k) % ncol, ci).start()
    col_buf[ci] = summed
    for k in range(1, ncol):
        col_copy((ci + k) % ncol, ci).wait_send()
        peer = (ci + ncol - k) % ncol
        col_copy(peer, peer).wait_recv()
    summed = col_buf[0]
    for j in range(1, ncol):
        summed = summed + col_buf[j]

    def pick(k):
        return jnp.sum(jnp.where((sub == 0) & (lane == k), summed, 0.0), axis=(0, 1), keepdims=True)

    curv = pick(0)
    norm_now = pick(len(parts) - 1) if first else rr_ref[0:1, 0:1]
    step_size = norm_now / curv
    u_out[...] = u_ref[...] + step_size * direction
    residual = residual - step_size * image
    r_out[...] = residual
    if not last:
        image_sq = pick(1)
        cross = curv if first else pick(2)
        norm_next = norm_now - 2.0 * step_size * cross + step_size * step_size * image_sq
        d_out[...] = residual + norm_next / norm_now * direction
        rr_out[...] = jnp.broadcast_to(norm_next, (8, 128))


def cg_step(names, iteration, direction, image, residual, update, norm_tile):
    ncol = lax.axis_size("col")
    nrow = lax.axis_size("row")
    first = iteration == 0
    last = iteration == ITERS - 1
    shape = direction.shape
    flat = (shape[0] * shape[1], shape[2])
    fields = [x.reshape(flat) for x in (direction, image, residual, update)]
    field_type = jax.ShapeDtypeStruct(flat, jnp.float32)
    out_shape = [field_type, field_type]
    if not last:
        out_shape += [field_type, jax.ShapeDtypeStruct((8, 128), jnp.float32)]
    got = pl.pallas_call(
        functools.partial(_cg_kernel, names, first, last),
        out_shape=tuple(out_shape),
        in_specs=[pl.BlockSpec(memory_space=pltpu.VMEM)] * 5,
        out_specs=tuple(pl.BlockSpec(memory_space=pltpu.VMEM) for _ in out_shape),
        scratch_shapes=[
            pltpu.VMEM((nrow, 8, 128), jnp.float32),
            pltpu.VMEM((ncol, 8, 128), jnp.float32),
            pltpu.VMEM((8, 128), jnp.float32),
            pltpu.VMEM((8, 128), jnp.float32),
            pltpu.SemaphoreType.DMA((nrow,)),
            pltpu.SemaphoreType.DMA((nrow,)),
            pltpu.SemaphoreType.DMA((ncol,)),
            pltpu.SemaphoreType.DMA((ncol,)),
        ],
        compiler_params=pltpu.CompilerParams(
            collective_id=10 + iteration, has_side_effects=True
        ),
    )(*fields, norm_tile)
    update = got[0].reshape(shape)
    residual = got[1].reshape(shape)
    if last:
        return update, residual, None, None
    return update, residual, got[2].reshape(shape), got[3]


def tile_view(control, tile_rows, tile_cols, points):
    return control.reshape(2, tile_rows, points, tile_cols, points)


def edge_band(tile_grid, facing, band_depth):
    if facing == 0:
        return tile_grid[..., ::-1][..., :band_depth].transpose(0, 1, 3, 2, 4)
    if facing == 1:
        return tile_grid[..., :band_depth].transpose(0, 1, 3, 2, 4)
    if facing == 2:
        return tile_grid[:, :, ::-1][:, :, :band_depth].transpose(0, 1, 3, 4, 2)
    return tile_grid[:, :, :band_depth].transpose(0, 1, 3, 4, 2)


def place_edge(band_part, facing, points):
    band_depth = band_part.shape[4]
    if facing < 2:
        widened = jnp.pad(
            band_part.transpose(0, 1, 3, 2, 4),
            ((0, 0), (0, 0), (0, 0), (0, 0), (0, points - band_depth)),
        )
        if facing == 0:
            return widened[..., ::-1]
        return widened
    widened = jnp.pad(
        band_part.transpose(0, 1, 4, 2, 3),
        ((0, 0), (0, 0), (0, points - band_depth), (0, 0), (0, 0)),
    )
    if facing == 2:
        return widened[:, :, ::-1]
    return widened


def make_tables(along_cell, across, frac_pair):
    weight_along = (frac_pair[0].astype(jnp.float32) + 0.5) / 256.0
    weight_across = (frac_pair[1].astype(jnp.float32) + 0.5) / 256.0
    return (along_cell, across, weight_along, weight_across)


def weight_tables(tables, points, band_depth):
    along_cell, across, weight_along, weight_across = tables
    along_iota = jnp.arange(points, dtype=jnp.int32)[None, None, :, None]
    across_iota = jnp.arange(band_depth, dtype=jnp.int32)[None, None, :, None]
    cell_now = along_cell[:, :, None, :]
    depth_now = across[:, :, None, :]
    frac_along = weight_along[:, :, None, :]
    frac_across = weight_across[:, :, None, :]
    along_table = (1.0 - frac_along) * (along_iota == cell_now).astype(jnp.float32) + frac_along * (
        along_iota == cell_now + 1
    ).astype(jnp.float32)
    across_table = (1.0 - frac_across) * (across_iota == depth_now).astype(
        jnp.float32
    ) + frac_across * (across_iota == depth_now + 1).astype(jnp.float32)
    return (along_table, across_table)


def interpolate(band_part, tables):
    along_table, across_table = weight_tables(tables, band_part.shape[3], band_part.shape[4])
    partial_sum = jnp.einsum(
        "cabiq,abis->cabqs", band_part, along_table, precision=lax.Precision.HIGHEST
    )
    return jnp.sum(partial_sum * across_table[None], axis=3)


def spread_back(residual, tables, points, band_depth):
    along_table, across_table = weight_tables(tables, points, band_depth)
    weighted = residual[:, :, :, None, :] * across_table[None]
    return jnp.einsum("cabqs,abis->cabiq", weighted, along_table, precision=lax.Precision.HIGHEST)


def bending(control, tile_rows, tile_cols):
    grid_view = tile_view(control, tile_rows, tile_cols, GRID)
    inner = (
        grid_view[:, :, :-2, :, 1:-1]
        + grid_view[:, :, 2:, :, 1:-1]
        + grid_view[:, :, 1:-1, :, :-2]
        + grid_view[:, :, 1:-1, :, 2:]
        - 4.0 * grid_view[:, :, 1:-1, :, 1:-1]
    )
    widths = ((0, 0), (0, 0), (1, 1), (0, 0), (1, 1))
    curvature = jnp.pad(inner, widths)
    padded = jnp.pad(curvature, widths)
    result = (
        padded[:, :, :-2, :, 1:-1]
        + padded[:, :, 2:, :, 1:-1]
        + padded[:, :, 1:-1, :, :-2]
        + padded[:, :, 1:-1, :, 2:]
        - 4.0 * curvature
    )
    return result.reshape(control.shape)


def _halo_kernel(names, send_ref, recv_ref, send_sems, recv_sems):
    ncol = lax.axis_size("col")
    nrow = lax.axis_size("row")
    ci = lax.axis_index("col")
    ri = lax.axis_index("row")

    def dev(c, r):
        where = {"col": c, "row": r}
        return tuple(where[n] for n in names)

    peers = [
        dev((ci + 1) % ncol, ri),
        dev((ci + ncol - 1) % ncol, ri),
        dev(ci, (ri + 1) % nrow),
        dev(ci, (ri + nrow - 1) % nrow),
    ]
    barrier = pltpu.get_barrier_semaphore()
    for peer in peers:
        pl.semaphore_signal(barrier, 1, device_id=peer, device_id_type=MESH_ID)
    pl.semaphore_wait(barrier, len(peers))
    copies = [
        pltpu.make_async_remote_copy(
            src_ref=send_ref.at[k], dst_ref=recv_ref.at[k], send_sem=send_sems.at[k],
            recv_sem=recv_sems.at[k], device_id=peers[k], device_id_type=MESH_ID)
        for k in range(4)
    ]
    for copy in copies:
        copy.start()
    for copy in copies:
        copy.wait_send()
        copy.wait_recv()


def halo_exchange(names, to_east, to_west, to_south, to_north):
    slabs = [to_east, to_west, to_south, to_north]
    rows = max(slab.shape[0] for slab in slabs)
    lanes = slabs[0].shape[1]
    stacked = jnp.stack([jnp.pad(slab, ((0, rows - slab.shape[0]), (0, 0))) for slab in slabs])
    got = pl.pallas_call(
        functools.partial(_halo_kernel, names),
        out_shape=jax.ShapeDtypeStruct(stacked.shape, jnp.float32),
        in_specs=[pl.BlockSpec(memory_space=pltpu.VMEM)],
        out_specs=pl.BlockSpec(memory_space=pltpu.VMEM),
        scratch_shapes=[pltpu.SemaphoreType.DMA((4,)), pltpu.SemaphoreType.DMA((4,))],
        compiler_params=pltpu.CompilerParams(collective_id=1, has_side_effects=True),
    )(stacked)
    return [got[k, : slabs[k].shape[0]] for k in range(4)]


def all_weight_tables(tables):
    pairs = [weight_tables(tables[facing], GRID, BAND) for facing in range(4)]
    return (jnp.stack([pair[0] for pair in pairs]), jnp.stack([pair[1] for pair in pairs]))


def seam_term(control, target, tables, adjacency, names):
    tile_rows, tile_cols = (adjacency.shape[1], adjacency.shape[2])
    along_table, across_table = tables
    grid_view = tile_view(control, tile_rows, tile_cols, GRID)
    bands = jnp.stack([edge_band(grid_view, facing, BAND) for facing in range(4)])
    partial_sum = jnp.einsum(
        "kcabiq,kabis->kcabqs", bands, along_table, precision=lax.Precision.HIGHEST
    )
    stacked_values = jnp.sum(partial_sum * across_table[:, None], axis=4)
    seam_values = [stacked_values[facing] for facing in range(4)]
    samples = seam_values[0].shape[3]
    col_pos = lax.axis_index("col") * tile_cols + jnp.arange(tile_cols)
    row_pos = lax.axis_index("row") * tile_rows + jnp.arange(tile_rows)
    mask_east = (
        adjacency[0].astype(jnp.float32)
        * (col_pos < lax.axis_size("col") * tile_cols - 1).astype(jnp.float32)[None, :]
    )
    mask_south = (
        adjacency[1].astype(jnp.float32)
        * (row_pos < lax.axis_size("row") * tile_rows - 1).astype(jnp.float32)[:, None]
    )
    own_east = seam_values[0]
    own_south = seam_values[2]
    if target is not None:
        own_east = own_east - target[0]
        own_south = own_south - target[1]
    to_east = jnp.concatenate(
        [
            own_east[:, :, -1].reshape(2 * tile_rows, samples),
            jnp.broadcast_to(mask_east[:, -1:], (tile_rows, samples)),
        ]
    )
    to_west = seam_values[1][:, :, 0].reshape(2 * tile_rows, samples)
    to_south = jnp.concatenate(
        [
            own_south[:, -1].reshape(2 * tile_cols, samples),
            jnp.broadcast_to(mask_south[-1][:, None], (tile_cols, samples)),
        ]
    )
    to_north = seam_values[3][:, 0].reshape(2 * tile_cols, samples)
    got_west, got_east, got_north, got_south = halo_exchange(
        names, to_east, to_west, to_south, to_north
    )
    west_east = got_west[: 2 * tile_rows].reshape(2, tile_rows, 1, samples)
    west_mask = got_west[2 * tile_rows :].reshape(1, tile_rows, 1, samples)
    east_next = got_east.reshape(2, tile_rows, 1, samples)
    north_south = got_north[: 2 * tile_cols].reshape(2, 1, tile_cols, samples)
    north_mask = got_north[2 * tile_cols :].reshape(1, 1, tile_cols, samples)
    south_next = got_south.reshape(2, 1, tile_cols, samples)
    west_next = jnp.concatenate([seam_values[1][:, :, 1:], east_next], axis=2)
    north_next = jnp.concatenate([seam_values[3][:, 1:], south_next], axis=1)
    resid_east = (own_east - west_next) * mask_east[None, :, :, None]
    resid_south = (own_south - north_next) * mask_south[None, :, :, None]
    from_west = (west_east - seam_values[1][:, :, :1]) * west_mask
    from_north = (north_south - seam_values[3][:, :1]) * north_mask
    resid_west = -jnp.concatenate([from_west, resid_east[:, :, :-1]], axis=2)
    resid_north = -jnp.concatenate([from_north, resid_south[:, :-1]], axis=1)
    residuals = jnp.stack([resid_east, resid_west, resid_south, resid_north])
    weighted = residuals[:, :, :, :, None, :] * across_table[:, None]
    spread_parts = jnp.einsum(
        "kcabqs,kabis->kcabiq", weighted, along_table, precision=lax.Precision.HIGHEST
    )
    summed = (
        place_edge(spread_parts[0], 0, GRID)
        + place_edge(spread_parts[1], 1, GRID)
        + place_edge(spread_parts[2], 2, GRID)
        + place_edge(spread_parts[3], 3, GRID)
    )
    return summed.reshape(control.shape)


def hessian_apply(control, tables, adjacency, names):
    tile_rows, tile_cols = (adjacency.shape[1], adjacency.shape[2])
    return (
        seam_term(control, None, tables, adjacency, names)
        + BEND_WEIGHT * bending(control, tile_rows, tile_cols)
        + DAMPING * control
    )


def shards(names, start_field, seam_target, seam_rows, seam_band, seam_frac, adjacency):
    tile_rows, tile_cols = (adjacency.shape[1], adjacency.shape[2])
    samples = seam_rows.shape[2] // tile_cols
    along_cells = seam_rows.reshape(4, tile_rows, tile_cols, samples)
    across_cells = seam_band.reshape(4, tile_rows, tile_cols, samples)
    frac_cells = seam_frac.reshape(4, 2, tile_rows, tile_cols, samples)
    tables = [
        make_tables(along_cells[facing], across_cells[facing], frac_cells[facing])
        for facing in range(4)
    ]
    tables = all_weight_tables(tables)
    target_cells = seam_target.reshape(2, 2, tile_rows, tile_cols, samples)
    target = (target_cells[0], target_cells[1])
    control = start_field
    gradient = seam_term(control, target, tables, adjacency, names) + BEND_WEIGHT * bending(
        control, tile_rows, tile_cols
    )
    residual = -gradient
    update = jnp.zeros_like(control)
    direction = residual
    norm_tile = jnp.zeros((8, 128), jnp.float32)
    for iteration in range(ITERS):
        hess_image = hessian_apply(direction, tables, adjacency, names)
        update, residual, direction, norm_tile = cg_step(
            names, iteration, direction, hess_image, residual, update, norm_tile
        )
    control = control + update
    return (control, residual)


def solution(mesh):
    placed = (
        P(None, "row", "col"),
        P(None, None, "row", "col"),
        P(None, "row", "col"),
        P(None, "row", "col"),
        P(None, None, "row", "col"),
        P(None, "row", "col"),
    )
    return jax.shard_map(
        functools.partial(shards, tuple(mesh.axis_names)),
        mesh=mesh,
        in_specs=placed,
        out_specs=(P(None, "row", "col"), P(None, "row", "col")),
        check_vma=False,
    )
```

```python
import functools

import jax
import jax.numpy as jnp
from jax import lax
from jax.experimental import pallas as pl
from jax.experimental.pallas import tpu as pltpu
from jax.sharding import PartitionSpec as P

GRID = 32
BAND = 4
ITERS = 3


BEND_WEIGHT = 0.05
DAMPING = 0.5


MESH_ID = pl.DeviceIdType.MESH


def _cg_kernel(names, first, last, d_ref, h_ref, r_ref, u_ref, rr_ref, *refs):
    if last:
        u_out, r_out, row_buf, col_buf, mine, part, row_send, row_recv, col_send, col_recv = refs
    else:
        (u_out, r_out, d_out, rr_out, row_buf, col_buf, mine, part, row_send, row_recv, col_send,
         col_recv) = refs
    ncol = lax.axis_size("col")
    nrow = lax.axis_size("row")
    ci = lax.axis_index("col")
    ri = lax.axis_index("row")

    def dev(c, r):
        where = {"col": c, "row": r}
        return tuple(where[n] for n in names)

    direction = d_ref[...]
    image = h_ref[...]
    residual = r_ref[...]

    def total(x):
        return jnp.sum(jnp.sum(x, axis=0, keepdims=True), axis=1, keepdims=True)

    parts = [total(direction * image)]
    if not last:
        parts += [total(image * image), total(residual * image)]
    if first:
        parts += [total(residual * residual)]
    lane = lax.broadcasted_iota(jnp.int32, (8, 128), 1)
    sub = lax.broadcasted_iota(jnp.int32, (8, 128), 0)
    tile = jnp.zeros((8, 128), jnp.float32)
    for k, value in enumerate(parts):
        tile = jnp.where((sub == 0) & (lane == k), value, tile)
    mine[...] = tile

    barrier = pltpu.get_barrier_semaphore()

    @pl.loop(1, nrow)
    def _(k):
        pl.semaphore_signal(barrier, 1, device_id=dev(ci, (ri + k) % nrow), device_id_type=MESH_ID)

    @pl.loop(1, ncol)
    def _(k):
        pl.semaphore_signal(barrier, 1, device_id=dev((ci + k) % ncol, ri), device_id_type=MESH_ID)

    pl.semaphore_wait(barrier, nrow - 1 + ncol - 1)

    def row_copy(peer, slot):
        return pltpu.make_async_remote_copy(
            src_ref=mine, dst_ref=row_buf.at[slot], send_sem=row_send.at[peer],
            recv_sem=row_recv.at[slot], device_id=dev(ci, peer), device_id_type=MESH_ID)

    for k in range(1, nrow):
        row_copy((ri + k) % nrow, ri).start()
    row_buf[ri] = tile
    for k in range(1, nrow):
        row_copy((ri + k) % nrow, ri).wait_send()
        peer = (ri + nrow - k) % nrow
        row_copy(peer, peer).wait_recv()
    summed = row_buf[0]
    for j in range(1, nrow):
        summed = summed + row_buf[j]
    part[...] = summed

    def col_copy(peer, slot):
        return pltpu.make_async_remote_copy(
            src_ref=part, dst_ref=col_buf.at[slot], send_sem=col_send.at[peer],
            recv_sem=col_recv.at[slot], device_id=dev(peer, ri), device_id_type=MESH_ID)

    @pl.loop(1, ncol)
    def _(k):
        col_copy((ci + k) % ncol, ci).start()

    col_buf[ci] = summed

    @pl.loop(1, ncol)
    def _(k):
        col_copy((ci + k) % ncol, ci).wait_send()
        peer = (ci + ncol - k) % ncol
        col_copy(peer, peer).wait_recv()

    summed = lax.fori_loop(1, ncol, lambda j, acc: acc + col_buf[j], col_buf[0])

    def pick(k):
        return jnp.sum(jnp.where((sub == 0) & (lane == k), summed, 0.0), axis=(0, 1), keepdims=True)

    curv = pick(0)
    norm_now = pick(len(parts) - 1) if first else rr_ref[0:1, 0:1]
    step_size = norm_now / curv
    u_out[...] = u_ref[...] + step_size * direction
    residual = residual - step_size * image
    r_out[...] = residual
    if not last:
        image_sq = pick(1)
        cross = curv if first else pick(2)
        norm_next = norm_now - 2.0 * step_size * cross + step_size * step_size * image_sq
        d_out[...] = residual + norm_next / norm_now * direction
        rr_out[...] = jnp.broadcast_to(norm_next, (8, 128))


def cg_step(names, iteration, direction, image, residual, update, norm_tile):
    ncol = lax.axis_size("col")
    nrow = lax.axis_size("row")
    first = iteration == 0
    last = iteration == ITERS - 1
    shape = direction.shape
    flat = (shape[0] * shape[1], shape[2])
    fields = [x.reshape(flat) for x in (direction, image, residual, update)]
    field_type = jax.ShapeDtypeStruct(flat, jnp.float32)
    out_shape = [field_type, field_type]
    if not last:
        out_shape += [field_type, jax.ShapeDtypeStruct((8, 128), jnp.float32)]
    got = pl.pallas_call(
        functools.partial(_cg_kernel, names, first, last),
        out_shape=tuple(out_shape),
        in_specs=[pl.BlockSpec(memory_space=pltpu.VMEM)] * 5,
        out_specs=tuple(pl.BlockSpec(memory_space=pltpu.VMEM) for _ in out_shape),
        scratch_shapes=[
            pltpu.VMEM((nrow, 8, 128), jnp.float32),
            pltpu.VMEM((ncol, 8, 128), jnp.float32),
            pltpu.VMEM((8, 128), jnp.float32),
            pltpu.VMEM((8, 128), jnp.float32),
            pltpu.SemaphoreType.DMA((nrow,)),
            pltpu.SemaphoreType.DMA((nrow,)),
            pltpu.SemaphoreType.DMA((ncol,)),
            pltpu.SemaphoreType.DMA((ncol,)),
        ],
        compiler_params=pltpu.CompilerParams(
            collective_id=10 + iteration, has_side_effects=True
        ),
    )(*fields, norm_tile)
    update = got[0].reshape(shape)
    residual = got[1].reshape(shape)
    if last:
        return update, residual, None, None
    return update, residual, got[2].reshape(shape), got[3]


def tile_view(control, tile_rows, tile_cols, points):
    return control.reshape(2, tile_rows, points, tile_cols, points)


def edge_band(tile_grid, facing, band_depth):
    if facing == 0:
        return tile_grid[..., ::-1][..., :band_depth].transpose(0, 1, 3, 2, 4)
    if facing == 1:
        return tile_grid[..., :band_depth].transpose(0, 1, 3, 2, 4)
    if facing == 2:
        return tile_grid[:, :, ::-1][:, :, :band_depth].transpose(0, 1, 3, 4, 2)
    return tile_grid[:, :, :band_depth].transpose(0, 1, 3, 4, 2)


def place_edge(band_part, facing, points):
    band_depth = band_part.shape[4]
    if facing < 2:
        widened = jnp.pad(
            band_part.transpose(0, 1, 3, 2, 4),
            ((0, 0), (0, 0), (0, 0), (0, 0), (0, points - band_depth)),
        )
        if facing == 0:
            return widened[..., ::-1]
        return widened
    widened = jnp.pad(
        band_part.transpose(0, 1, 4, 2, 3),
        ((0, 0), (0, 0), (0, points - band_depth), (0, 0), (0, 0)),
    )
    if facing == 2:
        return widened[:, :, ::-1]
    return widened


def make_tables(along_cell, across, frac_pair):
    weight_along = (frac_pair[0].astype(jnp.float32) + 0.5) / 256.0
    weight_across = (frac_pair[1].astype(jnp.float32) + 0.5) / 256.0
    return (along_cell, across, weight_along, weight_across)


def weight_tables(tables, points, band_depth):
    along_cell, across, weight_along, weight_across = tables
    along_iota = jnp.arange(points, dtype=jnp.int32)[None, None, :, None]
    across_iota = jnp.arange(band_depth, dtype=jnp.int32)[None, None, :, None]
    cell_now = along_cell[:, :, None, :]
    depth_now = across[:, :, None, :]
    frac_along = weight_along[:, :, None, :]
    frac_across = weight_across[:, :, None, :]
    along_table = (1.0 - frac_along) * (along_iota == cell_now).astype(jnp.float32) + frac_along * (
        along_iota == cell_now + 1
    ).astype(jnp.float32)
    across_table = (1.0 - frac_across) * (across_iota == depth_now).astype(
        jnp.float32
    ) + frac_across * (across_iota == depth_now + 1).astype(jnp.float32)
    return (along_table, across_table)


def interpolate(band_part, tables):
    along_table, across_table = weight_tables(tables, band_part.shape[3], band_part.shape[4])
    partial_sum = jnp.einsum(
        "cabiq,abis->cabqs", band_part, along_table, precision=lax.Precision.HIGHEST
    )
    return jnp.sum(partial_sum * across_table[None], axis=3)


def spread_back(residual, tables, points, band_depth):
    along_table, across_table = weight_tables(tables, points, band_depth)
    weighted = residual[:, :, :, None, :] * across_table[None]
    return jnp.einsum("cabqs,abis->cabiq", weighted, along_table, precision=lax.Precision.HIGHEST)


def bending(control, tile_rows, tile_cols):
    grid_view = tile_view(control, tile_rows, tile_cols, GRID)
    inner = (
        grid_view[:, :, :-2, :, 1:-1]
        + grid_view[:, :, 2:, :, 1:-1]
        + grid_view[:, :, 1:-1, :, :-2]
        + grid_view[:, :, 1:-1, :, 2:]
        - 4.0 * grid_view[:, :, 1:-1, :, 1:-1]
    )
    widths = ((0, 0), (0, 0), (1, 1), (0, 0), (1, 1))
    curvature = jnp.pad(inner, widths)
    padded = jnp.pad(curvature, widths)
    result = (
        padded[:, :, :-2, :, 1:-1]
        + padded[:, :, 2:, :, 1:-1]
        + padded[:, :, 1:-1, :, :-2]
        + padded[:, :, 1:-1, :, 2:]
        - 4.0 * curvature
    )
    return result.reshape(control.shape)


def _halo_kernel(names, send_ref, recv_ref, send_sems, recv_sems):
    ncol = lax.axis_size("col")
    nrow = lax.axis_size("row")
    ci = lax.axis_index("col")
    ri = lax.axis_index("row")

    def dev(c, r):
        where = {"col": c, "row": r}
        return tuple(where[n] for n in names)

    peers = [
        dev((ci + 1) % ncol, ri),
        dev((ci + ncol - 1) % ncol, ri),
        dev(ci, (ri + 1) % nrow),
        dev(ci, (ri + nrow - 1) % nrow),
    ]
    barrier = pltpu.get_barrier_semaphore()
    for peer in peers:
        pl.semaphore_signal(barrier, 1, device_id=peer, device_id_type=MESH_ID)
    pl.semaphore_wait(barrier, len(peers))
    copies = [
        pltpu.make_async_remote_copy(
            src_ref=send_ref.at[k], dst_ref=recv_ref.at[k], send_sem=send_sems.at[k],
            recv_sem=recv_sems.at[k], device_id=peers[k], device_id_type=MESH_ID)
        for k in range(4)
    ]
    for copy in copies:
        copy.start()
    for copy in copies:
        copy.wait_send()
        copy.wait_recv()


def halo_exchange(names, to_east, to_west, to_south, to_north):
    slabs = [to_east, to_west, to_south, to_north]
    rows = max(slab.shape[0] for slab in slabs)
    lanes = slabs[0].shape[1]
    stacked = jnp.stack([jnp.pad(slab, ((0, rows - slab.shape[0]), (0, 0))) for slab in slabs])
    got = pl.pallas_call(
        functools.partial(_halo_kernel, names),
        out_shape=jax.ShapeDtypeStruct(stacked.shape, jnp.float32),
        in_specs=[pl.BlockSpec(memory_space=pltpu.VMEM)],
        out_specs=pl.BlockSpec(memory_space=pltpu.VMEM),
        scratch_shapes=[pltpu.SemaphoreType.DMA((4,)), pltpu.SemaphoreType.DMA((4,))],
        compiler_params=pltpu.CompilerParams(collective_id=1, has_side_effects=True),
    )(stacked)
    return [got[k, : slabs[k].shape[0]] for k in range(4)]


def all_weight_tables(tables):
    pairs = [weight_tables(tables[facing], GRID, BAND) for facing in range(4)]
    return (jnp.stack([pair[0] for pair in pairs]), jnp.stack([pair[1] for pair in pairs]))


def seam_term(control, target, tables, adjacency, names):
    tile_rows, tile_cols = (adjacency.shape[1], adjacency.shape[2])
    along_table, across_table = tables
    grid_view = tile_view(control, tile_rows, tile_cols, GRID)
    bands = jnp.stack([edge_band(grid_view, facing, BAND) for facing in range(4)])
    partial_sum = jnp.einsum(
        "kcabiq,kabis->kcabqs", bands, along_table, precision=lax.Precision.HIGHEST
    )
    stacked_values = jnp.sum(partial_sum * across_table[:, None], axis=4)
    seam_values = [stacked_values[facing] for facing in range(4)]
    samples = seam_values[0].shape[3]
    col_pos = lax.axis_index("col") * tile_cols + jnp.arange(tile_cols)
    row_pos = lax.axis_index("row") * tile_rows + jnp.arange(tile_rows)
    mask_east = (
        adjacency[0].astype(jnp.float32)
        * (col_pos < lax.axis_size("col") * tile_cols - 1).astype(jnp.float32)[None, :]
    )
    mask_south = (
        adjacency[1].astype(jnp.float32)
        * (row_pos < lax.axis_size("row") * tile_rows - 1).astype(jnp.float32)[:, None]
    )
    own_east = seam_values[0]
    own_south = seam_values[2]
    if target is not None:
        own_east = own_east - target[0]
        own_south = own_south - target[1]
    to_east = jnp.concatenate(
        [
            own_east[:, :, -1].reshape(2 * tile_rows, samples),
            jnp.broadcast_to(mask_east[:, -1:], (tile_rows, samples)),
        ]
    )
    to_west = seam_values[1][:, :, 0].reshape(2 * tile_rows, samples)
    to_south = jnp.concatenate(
        [
            own_south[:, -1].reshape(2 * tile_cols, samples),
            jnp.broadcast_to(mask_south[-1][:, None], (tile_cols, samples)),
        ]
    )
    to_north = seam_values[3][:, 0].reshape(2 * tile_cols, samples)
    got_west, got_east, got_north, got_south = halo_exchange(
        names, to_east, to_west, to_south, to_north
    )
    west_east = got_west[: 2 * tile_rows].reshape(2, tile_rows, 1, samples)
    west_mask = got_west[2 * tile_rows :].reshape(1, tile_rows, 1, samples)
    east_next = got_east.reshape(2, tile_rows, 1, samples)
    north_south = got_north[: 2 * tile_cols].reshape(2, 1, tile_cols, samples)
    north_mask = got_north[2 * tile_cols :].reshape(1, 1, tile_cols, samples)
    south_next = got_south.reshape(2, 1, tile_cols, samples)
    west_next = jnp.concatenate([seam_values[1][:, :, 1:], east_next], axis=2)
    north_next = jnp.concatenate([seam_values[3][:, 1:], south_next], axis=1)
    resid_east = (own_east - west_next) * mask_east[None, :, :, None]
    resid_south = (own_south - north_next) * mask_south[None, :, :, None]
    from_west = (west_east - seam_values[1][:, :, :1]) * west_mask
    from_north = (north_south - seam_values[3][:, :1]) * north_mask
    resid_west = -jnp.concatenate([from_west, resid_east[:, :, :-1]], axis=2)
    resid_north = -jnp.concatenate([from_north, resid_south[:, :-1]], axis=1)
    residuals = jnp.stack([resid_east, resid_west, resid_south, resid_north])
    weighted = residuals[:, :, :, :, None, :] * across_table[:, None]
    spread_parts = jnp.einsum(
        "kcabqs,kabis->kcabiq", weighted, along_table, precision=lax.Precision.HIGHEST
    )
    summed = (
        place_edge(spread_parts[0], 0, GRID)
        + place_edge(spread_parts[1], 1, GRID)
        + place_edge(spread_parts[2], 2, GRID)
        + place_edge(spread_parts[3], 3, GRID)
    )
    return summed.reshape(control.shape)


def hessian_apply(control, tables, adjacency, names):
    tile_rows, tile_cols = (adjacency.shape[1], adjacency.shape[2])
    return (
        seam_term(control, None, tables, adjacency, names)
        + BEND_WEIGHT * bending(control, tile_rows, tile_cols)
        + DAMPING * control
    )


def shards(names, start_field, seam_target, seam_rows, seam_band, seam_frac, adjacency):
    tile_rows, tile_cols = (adjacency.shape[1], adjacency.shape[2])
    samples = seam_rows.shape[2] // tile_cols
    along_cells = seam_rows.reshape(4, tile_rows, tile_cols, samples)
    across_cells = seam_band.reshape(4, tile_rows, tile_cols, samples)
    frac_cells = seam_frac.reshape(4, 2, tile_rows, tile_cols, samples)
    tables = [
        make_tables(along_cells[facing], across_cells[facing], frac_cells[facing])
        for facing in range(4)
    ]
    tables = all_weight_tables(tables)
    target_cells = seam_target.reshape(2, 2, tile_rows, tile_cols, samples)
    target = (target_cells[0], target_cells[1])
    control = start_field
    gradient = seam_term(control, target, tables, adjacency, names) + BEND_WEIGHT * bending(
        control, tile_rows, tile_cols
    )
    residual = -gradient
    update = jnp.zeros_like(control)
    direction = residual
    norm_tile = jnp.zeros((8, 128), jnp.float32)
    for iteration in range(ITERS):
        hess_image = hessian_apply(direction, tables, adjacency, names)
        update, residual, direction, norm_tile = cg_step(
            names, iteration, direction, hess_image, residual, update, norm_tile
        )
    control = control + update
    return (control, residual)


def solution(mesh):
    placed = (
        P(None, "row", "col"),
        P(None, None, "row", "col"),
        P(None, "row", "col"),
        P(None, "row", "col"),
        P(None, None, "row", "col"),
        P(None, "row", "col"),
    )
    return jax.shard_map(
        functools.partial(shards, tuple(mesh.axis_names)),
        mesh=mesh,
        in_specs=placed,
        out_specs=(P(None, "row", "col"), P(None, "row", "col")),
        check_vma=False,
    )
```

```python
import functools

import jax
import jax.numpy as jnp
from jax import lax
from jax.experimental import pallas as pl
from jax.experimental.pallas import tpu as pltpu
from jax.sharding import PartitionSpec as P

GRID = 32
BAND = 4
ITERS = 3


BEND_WEIGHT = 0.05
DAMPING = 0.5


MESH_ID = pl.DeviceIdType.MESH


def _cg_kernel(names, first, last, d_ref, h_ref, r_ref, u_ref, rr_ref, *refs):
    if last:
        u_out, r_out, row_buf, col_buf, mine, part, row_send, row_recv, col_send, col_recv = refs
    else:
        (u_out, r_out, d_out, rr_out, row_buf, col_buf, mine, part, row_send, row_recv, col_send,
         col_recv) = refs
    ncol = lax.axis_size("col")
    nrow = lax.axis_size("row")
    ci = lax.axis_index("col")
    ri = lax.axis_index("row")

    def dev(c, r):
        where = {"col": c, "row": r}
        return tuple(where[n] for n in names)

    barrier = pltpu.get_barrier_semaphore()

    @pl.loop(1, nrow)
    def _(k):
        pl.semaphore_signal(barrier, 1, device_id=dev(ci, (ri + k) % nrow), device_id_type=MESH_ID)

    @pl.loop(1, ncol)
    def _(k):
        pl.semaphore_signal(barrier, 1, device_id=dev((ci + k) % ncol, ri), device_id_type=MESH_ID)

    direction = d_ref[...]
    residual = r_ref[...]
    rows, cols = direction.shape
    y = lax.broadcasted_iota(jnp.int32, (rows, cols), 0) % GRID
    x = lax.broadcasted_iota(jnp.int32, (rows, cols), 1) % GRID
    inside = (y >= 1) & (y <= GRID - 2) & (x >= 1) & (x <= GRID - 2)

    def five_point(f):
        return (
            pltpu.roll(f, 1, 0)
            + pltpu.roll(f, rows - 1, 0)
            + pltpu.roll(f, 1, 1)
            + pltpu.roll(f, cols - 1, 1)
            - 4.0 * f
        )

    curvature = jnp.where(inside, five_point(direction), 0.0)
    image = h_ref[...] + BEND_WEIGHT * five_point(curvature) + DAMPING * direction

    def total(x):
        return jnp.sum(jnp.sum(x, axis=0, keepdims=True), axis=1, keepdims=True)

    parts = [total(direction * image)]
    if not last:
        parts += [total(image * image), total(residual * image)]
    if first:
        parts += [total(residual * residual)]
    lane = lax.broadcasted_iota(jnp.int32, (8, 128), 1)
    sub = lax.broadcasted_iota(jnp.int32, (8, 128), 0)
    tile = jnp.zeros((8, 128), jnp.float32)
    for k, value in enumerate(parts):
        tile = jnp.where((sub == 0) & (lane == k), value, tile)
    mine[...] = tile

    pl.semaphore_wait(barrier, nrow - 1 + ncol - 1)

    def row_copy(peer, slot):
        return pltpu.make_async_remote_copy(
            src_ref=mine, dst_ref=row_buf.at[slot], send_sem=row_send.at[peer],
            recv_sem=row_recv.at[slot], device_id=dev(ci, peer), device_id_type=MESH_ID)

    for k in range(1, nrow):
        row_copy((ri + k) % nrow, ri).start()
    row_buf[ri] = tile
    for k in range(1, nrow):
        row_copy((ri + k) % nrow, ri).wait_send()
        peer = (ri + nrow - k) % nrow
        row_copy(peer, peer).wait_recv()
    summed = row_buf[0]
    for j in range(1, nrow):
        summed = summed + row_buf[j]
    part[...] = summed

    def col_copy(peer, slot):
        return pltpu.make_async_remote_copy(
            src_ref=part, dst_ref=col_buf.at[slot], send_sem=col_send.at[peer],
            recv_sem=col_recv.at[slot], device_id=dev(peer, ri), device_id_type=MESH_ID)

    @pl.loop(1, ncol)
    def _(k):
        col_copy((ci + k) % ncol, ci).start()

    col_buf[ci] = summed

    @pl.loop(1, ncol)
    def _(k):
        col_copy((ci + k) % ncol, ci).wait_send()
        peer = (ci + ncol - k) % ncol
        col_copy(peer, peer).wait_recv()

    summed = lax.fori_loop(1, ncol, lambda j, acc: acc + col_buf[j], col_buf[0])

    def pick(k):
        return jnp.sum(jnp.where((sub == 0) & (lane == k), summed, 0.0), axis=(0, 1), keepdims=True)

    curv = pick(0)
    norm_now = pick(len(parts) - 1) if first else rr_ref[0:1, 0:1]
    step_size = norm_now / curv
    u_out[...] = u_ref[...] + step_size * direction
    residual = residual - step_size * image
    r_out[...] = residual
    if not last:
        image_sq = pick(1)
        cross = curv if first else pick(2)
        norm_next = norm_now - 2.0 * step_size * cross + step_size * step_size * image_sq
        d_out[...] = residual + norm_next / norm_now * direction
        rr_out[...] = jnp.broadcast_to(norm_next, (8, 128))


def cg_step(names, iteration, direction, image, residual, update, norm_tile):
    ncol = lax.axis_size("col")
    nrow = lax.axis_size("row")
    first = iteration == 0
    last = iteration == ITERS - 1
    shape = direction.shape
    flat = (shape[0] * shape[1], shape[2])
    fields = [x.reshape(flat) for x in (direction, image, residual, update)]
    field_type = jax.ShapeDtypeStruct(flat, jnp.float32)
    out_shape = [field_type, field_type]
    if not last:
        out_shape += [field_type, jax.ShapeDtypeStruct((8, 128), jnp.float32)]
    got = pl.pallas_call(
        functools.partial(_cg_kernel, names, first, last),
        out_shape=tuple(out_shape),
        in_specs=[pl.BlockSpec(memory_space=pltpu.VMEM)] * 5,
        out_specs=tuple(pl.BlockSpec(memory_space=pltpu.VMEM) for _ in out_shape),
        scratch_shapes=[
            pltpu.VMEM((nrow, 8, 128), jnp.float32),
            pltpu.VMEM((ncol, 8, 128), jnp.float32),
            pltpu.VMEM((8, 128), jnp.float32),
            pltpu.VMEM((8, 128), jnp.float32),
            pltpu.SemaphoreType.DMA((nrow,)),
            pltpu.SemaphoreType.DMA((nrow,)),
            pltpu.SemaphoreType.DMA((ncol,)),
            pltpu.SemaphoreType.DMA((ncol,)),
        ],
        compiler_params=pltpu.CompilerParams(
            collective_id=10 + iteration, has_side_effects=True
        ),
    )(*fields, norm_tile)
    update = got[0].reshape(shape)
    residual = got[1].reshape(shape)
    if last:
        return update, residual, None, None
    return update, residual, got[2].reshape(shape), got[3]


def tile_view(control, tile_rows, tile_cols, points):
    return control.reshape(2, tile_rows, points, tile_cols, points)


def edge_band(tile_grid, facing, band_depth):
    if facing == 0:
        return tile_grid[..., ::-1][..., :band_depth].transpose(0, 1, 3, 2, 4)
    if facing == 1:
        return tile_grid[..., :band_depth].transpose(0, 1, 3, 2, 4)
    if facing == 2:
        return tile_grid[:, :, ::-1][:, :, :band_depth].transpose(0, 1, 3, 4, 2)
    return tile_grid[:, :, :band_depth].transpose(0, 1, 3, 4, 2)


def place_edge(band_part, facing, points):
    band_depth = band_part.shape[4]
    if facing < 2:
        widened = jnp.pad(
            band_part.transpose(0, 1, 3, 2, 4),
            ((0, 0), (0, 0), (0, 0), (0, 0), (0, points - band_depth)),
        )
        if facing == 0:
            return widened[..., ::-1]
        return widened
    widened = jnp.pad(
        band_part.transpose(0, 1, 4, 2, 3),
        ((0, 0), (0, 0), (0, points - band_depth), (0, 0), (0, 0)),
    )
    if facing == 2:
        return widened[:, :, ::-1]
    return widened


def make_tables(along_cell, across, frac_pair):
    weight_along = (frac_pair[0].astype(jnp.float32) + 0.5) / 256.0
    weight_across = (frac_pair[1].astype(jnp.float32) + 0.5) / 256.0
    return (along_cell, across, weight_along, weight_across)


def weight_tables(tables, points, band_depth):
    along_cell, across, weight_along, weight_across = tables
    along_iota = jnp.arange(points, dtype=jnp.int32)[None, None, :, None]
    across_iota = jnp.arange(band_depth, dtype=jnp.int32)[None, None, :, None]
    cell_now = along_cell[:, :, None, :]
    depth_now = across[:, :, None, :]
    frac_along = weight_along[:, :, None, :]
    frac_across = weight_across[:, :, None, :]
    along_table = (1.0 - frac_along) * (along_iota == cell_now).astype(jnp.float32) + frac_along * (
        along_iota == cell_now + 1
    ).astype(jnp.float32)
    across_table = (1.0 - frac_across) * (across_iota == depth_now).astype(
        jnp.float32
    ) + frac_across * (across_iota == depth_now + 1).astype(jnp.float32)
    return (along_table, across_table)


def interpolate(band_part, tables):
    along_table, across_table = weight_tables(tables, band_part.shape[3], band_part.shape[4])
    partial_sum = jnp.einsum(
        "cabiq,abis->cabqs", band_part, along_table, precision=lax.Precision.HIGHEST
    )
    return jnp.sum(partial_sum * across_table[None], axis=3)


def spread_back(residual, tables, points, band_depth):
    along_table, across_table = weight_tables(tables, points, band_depth)
    weighted = residual[:, :, :, None, :] * across_table[None]
    return jnp.einsum("cabqs,abis->cabiq", weighted, along_table, precision=lax.Precision.HIGHEST)


def bending(control, tile_rows, tile_cols):
    grid_view = tile_view(control, tile_rows, tile_cols, GRID)
    inner = (
        grid_view[:, :, :-2, :, 1:-1]
        + grid_view[:, :, 2:, :, 1:-1]
        + grid_view[:, :, 1:-1, :, :-2]
        + grid_view[:, :, 1:-1, :, 2:]
        - 4.0 * grid_view[:, :, 1:-1, :, 1:-1]
    )
    widths = ((0, 0), (0, 0), (1, 1), (0, 0), (1, 1))
    curvature = jnp.pad(inner, widths)
    padded = jnp.pad(curvature, widths)
    result = (
        padded[:, :, :-2, :, 1:-1]
        + padded[:, :, 2:, :, 1:-1]
        + padded[:, :, 1:-1, :, :-2]
        + padded[:, :, 1:-1, :, 2:]
        - 4.0 * curvature
    )
    return result.reshape(control.shape)


def _halo_kernel(names, send_ref, recv_ref, send_sems, recv_sems):
    ncol = lax.axis_size("col")
    nrow = lax.axis_size("row")
    ci = lax.axis_index("col")
    ri = lax.axis_index("row")

    def dev(c, r):
        where = {"col": c, "row": r}
        return tuple(where[n] for n in names)

    peers = [
        dev((ci + 1) % ncol, ri),
        dev((ci + ncol - 1) % ncol, ri),
        dev(ci, (ri + 1) % nrow),
        dev(ci, (ri + nrow - 1) % nrow),
    ]
    barrier = pltpu.get_barrier_semaphore()
    for peer in peers:
        pl.semaphore_signal(barrier, 1, device_id=peer, device_id_type=MESH_ID)
    pl.semaphore_wait(barrier, len(peers))
    copies = [
        pltpu.make_async_remote_copy(
            src_ref=send_ref.at[k], dst_ref=recv_ref.at[k], send_sem=send_sems.at[k],
            recv_sem=recv_sems.at[k], device_id=peers[k], device_id_type=MESH_ID)
        for k in range(4)
    ]
    for copy in copies:
        copy.start()
    for copy in copies:
        copy.wait_send()
        copy.wait_recv()


def halo_exchange(names, to_east, to_west, to_south, to_north):
    slabs = [to_east, to_west, to_south, to_north]
    rows = max(slab.shape[0] for slab in slabs)
    lanes = slabs[0].shape[1]
    stacked = jnp.stack([jnp.pad(slab, ((0, rows - slab.shape[0]), (0, 0))) for slab in slabs])
    got = pl.pallas_call(
        functools.partial(_halo_kernel, names),
        out_shape=jax.ShapeDtypeStruct(stacked.shape, jnp.float32),
        in_specs=[pl.BlockSpec(memory_space=pltpu.VMEM)],
        out_specs=pl.BlockSpec(memory_space=pltpu.VMEM),
        scratch_shapes=[pltpu.SemaphoreType.DMA((4,)), pltpu.SemaphoreType.DMA((4,))],
        compiler_params=pltpu.CompilerParams(collective_id=1, has_side_effects=True),
    )(stacked)
    return [got[k, : slabs[k].shape[0]] for k in range(4)]


def all_weight_tables(tables):
    pairs = [weight_tables(tables[facing], GRID, BAND) for facing in range(4)]
    return (jnp.stack([pair[0] for pair in pairs]), jnp.stack([pair[1] for pair in pairs]))


def seam_term(control, target, tables, adjacency, names):
    tile_rows, tile_cols = (adjacency.shape[1], adjacency.shape[2])
    along_table, across_table = tables
    grid_view = tile_view(control, tile_rows, tile_cols, GRID)
    bands = jnp.stack([edge_band(grid_view, facing, BAND) for facing in range(4)])
    partial_sum = jnp.einsum(
        "kcabiq,kabis->kcabqs", bands, along_table, precision=lax.Precision.HIGHEST
    )
    stacked_values = jnp.sum(partial_sum * across_table[:, None], axis=4)
    seam_values = [stacked_values[facing] for facing in range(4)]
    samples = seam_values[0].shape[3]
    col_pos = lax.axis_index("col") * tile_cols + jnp.arange(tile_cols)
    row_pos = lax.axis_index("row") * tile_rows + jnp.arange(tile_rows)
    mask_east = (
        adjacency[0].astype(jnp.float32)
        * (col_pos < lax.axis_size("col") * tile_cols - 1).astype(jnp.float32)[None, :]
    )
    mask_south = (
        adjacency[1].astype(jnp.float32)
        * (row_pos < lax.axis_size("row") * tile_rows - 1).astype(jnp.float32)[:, None]
    )
    own_east = seam_values[0]
    own_south = seam_values[2]
    if target is not None:
        own_east = own_east - target[0]
        own_south = own_south - target[1]
    to_east = jnp.concatenate(
        [
            own_east[:, :, -1].reshape(2 * tile_rows, samples),
            jnp.broadcast_to(mask_east[:, -1:], (tile_rows, samples)),
        ]
    )
    to_west = seam_values[1][:, :, 0].reshape(2 * tile_rows, samples)
    to_south = jnp.concatenate(
        [
            own_south[:, -1].reshape(2 * tile_cols, samples),
            jnp.broadcast_to(mask_south[-1][:, None], (tile_cols, samples)),
        ]
    )
    to_north = seam_values[3][:, 0].reshape(2 * tile_cols, samples)
    got_west, got_east, got_north, got_south = halo_exchange(
        names, to_east, to_west, to_south, to_north
    )
    west_east = got_west[: 2 * tile_rows].reshape(2, tile_rows, 1, samples)
    west_mask = got_west[2 * tile_rows :].reshape(1, tile_rows, 1, samples)
    east_next = got_east.reshape(2, tile_rows, 1, samples)
    north_south = got_north[: 2 * tile_cols].reshape(2, 1, tile_cols, samples)
    north_mask = got_north[2 * tile_cols :].reshape(1, 1, tile_cols, samples)
    south_next = got_south.reshape(2, 1, tile_cols, samples)
    west_next = jnp.concatenate([seam_values[1][:, :, 1:], east_next], axis=2)
    north_next = jnp.concatenate([seam_values[3][:, 1:], south_next], axis=1)
    resid_east = (own_east - west_next) * mask_east[None, :, :, None]
    resid_south = (own_south - north_next) * mask_south[None, :, :, None]
    from_west = (west_east - seam_values[1][:, :, :1]) * west_mask
    from_north = (north_south - seam_values[3][:, :1]) * north_mask
    resid_west = -jnp.concatenate([from_west, resid_east[:, :, :-1]], axis=2)
    resid_north = -jnp.concatenate([from_north, resid_south[:, :-1]], axis=1)
    residuals = jnp.stack([resid_east, resid_west, resid_south, resid_north])
    weighted = residuals[:, :, :, :, None, :] * across_table[:, None]
    spread_parts = jnp.einsum(
        "kcabqs,kabis->kcabiq", weighted, along_table, precision=lax.Precision.HIGHEST
    )
    summed = (
        place_edge(spread_parts[0], 0, GRID)
        + place_edge(spread_parts[1], 1, GRID)
        + place_edge(spread_parts[2], 2, GRID)
        + place_edge(spread_parts[3], 3, GRID)
    )
    return summed.reshape(control.shape)


def hessian_apply(control, tables, adjacency, names):
    tile_rows, tile_cols = (adjacency.shape[1], adjacency.shape[2])
    return (
        seam_term(control, None, tables, adjacency, names)
        + BEND_WEIGHT * bending(control, tile_rows, tile_cols)
        + DAMPING * control
    )


def shards(names, start_field, seam_target, seam_rows, seam_band, seam_frac, adjacency):
    tile_rows, tile_cols = (adjacency.shape[1], adjacency.shape[2])
    samples = seam_rows.shape[2] // tile_cols
    along_cells = seam_rows.reshape(4, tile_rows, tile_cols, samples)
    across_cells = seam_band.reshape(4, tile_rows, tile_cols, samples)
    frac_cells = seam_frac.reshape(4, 2, tile_rows, tile_cols, samples)
    tables = [
        make_tables(along_cells[facing], across_cells[facing], frac_cells[facing])
        for facing in range(4)
    ]
    tables = all_weight_tables(tables)
    target_cells = seam_target.reshape(2, 2, tile_rows, tile_cols, samples)
    target = (target_cells[0], target_cells[1])
    control = start_field
    gradient = seam_term(control, target, tables, adjacency, names) + BEND_WEIGHT * bending(
        control, tile_rows, tile_cols
    )
    residual = -gradient
    update = jnp.zeros_like(control)
    direction = residual
    norm_tile = jnp.zeros((8, 128), jnp.float32)
    for iteration in range(ITERS):
        seam_image = seam_term(direction, None, tables, adjacency, names)
        update, residual, direction, norm_tile = cg_step(
            names, iteration, direction, seam_image, residual, update, norm_tile
        )
    control = control + update
    return (control, residual)


def solution(mesh):
    placed = (
        P(None, "row", "col"),
        P(None, None, "row", "col"),
        P(None, "row", "col"),
        P(None, "row", "col"),
        P(None, None, "row", "col"),
        P(None, "row", "col"),
    )
    return jax.shard_map(
        functools.partial(shards, tuple(mesh.axis_names)),
        mesh=mesh,
        in_specs=placed,
        out_specs=(P(None, "row", "col"), P(None, "row", "col")),
        check_vma=False,
    )
```

```python
import functools

import jax
import jax.numpy as jnp
from jax import lax
from jax.experimental import pallas as pl
from jax.experimental.pallas import tpu as pltpu
from jax.sharding import PartitionSpec as P

GRID = 32
BAND = 4
ITERS = 3


BEND_WEIGHT = 0.05
DAMPING = 0.5


MESH_ID = pl.DeviceIdType.MESH


def _cg_kernel(names, first, last, d_ref, h_ref, r_ref, *refs):
    if not first:
        u_ref, rr_ref = refs[:2]
        refs = refs[2:]
    if last:
        u_out, r_out, row_buf, col_buf, mine, part, row_send, row_recv, col_send, col_recv = refs
    else:
        (u_out, r_out, d_out, rr_out, row_buf, col_buf, mine, part, row_send, row_recv, col_send,
         col_recv) = refs
    ncol = lax.axis_size("col")
    nrow = lax.axis_size("row")
    ci = lax.axis_index("col")
    ri = lax.axis_index("row")

    def dev(c, r):
        where = {"col": c, "row": r}
        return tuple(where[n] for n in names)

    barrier = pltpu.get_barrier_semaphore()

    @pl.loop(1, nrow)
    def _(k):
        pl.semaphore_signal(barrier, 1, device_id=dev(ci, (ri + k) % nrow), device_id_type=MESH_ID)

    @pl.loop(1, ncol)
    def _(k):
        pl.semaphore_signal(barrier, 1, device_id=dev((ci + k) % ncol, ri), device_id_type=MESH_ID)

    direction = d_ref[...]
    residual = r_ref[...]
    rows, cols = direction.shape
    y = lax.broadcasted_iota(jnp.int32, (rows, cols), 0) % GRID
    x = lax.broadcasted_iota(jnp.int32, (rows, cols), 1) % GRID
    inside = (y >= 1) & (y <= GRID - 2) & (x >= 1) & (x <= GRID - 2)

    def five_point(f):
        return (
            pltpu.roll(f, 1, 0)
            + pltpu.roll(f, rows - 1, 0)
            + pltpu.roll(f, 1, 1)
            + pltpu.roll(f, cols - 1, 1)
            - 4.0 * f
        )

    curvature = jnp.where(inside, five_point(direction), 0.0)
    image = h_ref[...] + BEND_WEIGHT * five_point(curvature) + DAMPING * direction

    def total(x):
        return jnp.sum(jnp.sum(x, axis=0, keepdims=True), axis=1, keepdims=True)

    parts = [total(direction * image)]
    if not last:
        parts += [total(image * image), total(residual * image)]
    if first:
        parts += [total(residual * residual)]
    lane = lax.broadcasted_iota(jnp.int32, (8, 128), 1)
    sub = lax.broadcasted_iota(jnp.int32, (8, 128), 0)
    tile = jnp.zeros((8, 128), jnp.float32)
    for k, value in enumerate(parts):
        tile = jnp.where((sub == 0) & (lane == k), value, tile)
    mine[...] = tile

    pl.semaphore_wait(barrier, nrow - 1 + ncol - 1)

    def row_copy(peer, slot):
        return pltpu.make_async_remote_copy(
            src_ref=mine, dst_ref=row_buf.at[slot], send_sem=row_send.at[peer],
            recv_sem=row_recv.at[slot], device_id=dev(ci, peer), device_id_type=MESH_ID)

    for k in range(1, nrow):
        row_copy((ri + k) % nrow, ri).start()
    row_buf[ri] = tile
    for k in range(1, nrow):
        row_copy((ri + k) % nrow, ri).wait_send()
        peer = (ri + nrow - k) % nrow
        row_copy(peer, peer).wait_recv()
    summed = row_buf[0]
    for j in range(1, nrow):
        summed = summed + row_buf[j]
    part[...] = summed

    def col_copy(peer, slot):
        return pltpu.make_async_remote_copy(
            src_ref=part, dst_ref=col_buf.at[slot], send_sem=col_send.at[peer],
            recv_sem=col_recv.at[slot], device_id=dev(peer, ri), device_id_type=MESH_ID)

    @pl.loop(1, ncol)
    def _(k):
        col_copy((ci + k) % ncol, ci).start()

    col_buf[ci] = summed

    @pl.loop(1, ncol)
    def _(k):
        col_copy((ci + k) % ncol, ci).wait_send()
        peer = (ci + ncol - k) % ncol
        col_copy(peer, peer).wait_recv()

    summed = lax.fori_loop(1, ncol, lambda j, acc: acc + col_buf[j], col_buf[0])

    def pick(k):
        return jnp.sum(jnp.where((sub == 0) & (lane == k), summed, 0.0), axis=(0, 1), keepdims=True)

    curv = pick(0)
    norm_now = pick(len(parts) - 1) if first else rr_ref[0:1, 0:1]
    step_size = norm_now / curv
    if first:
        u_out[...] = step_size * direction
    else:
        u_out[...] = u_ref[...] + step_size * direction
    residual = residual - step_size * image
    r_out[...] = residual
    if not last:
        image_sq = pick(1)
        cross = curv if first else pick(2)
        norm_next = norm_now - 2.0 * step_size * cross + step_size * step_size * image_sq
        d_out[...] = residual + norm_next / norm_now * direction
        rr_out[...] = jnp.broadcast_to(norm_next, (8, 128))


def cg_step(names, iteration, direction, image, residual, update, norm_tile):
    ncol = lax.axis_size("col")
    nrow = lax.axis_size("row")
    first = iteration == 0
    last = iteration == ITERS - 1
    shape = direction.shape
    flat = (shape[0] * shape[1], shape[2])
    fields = [x.reshape(flat) for x in (direction, image, residual)]
    if not first:
        fields += [update.reshape(flat), norm_tile]
    field_type = jax.ShapeDtypeStruct(flat, jnp.float32)
    out_shape = [field_type, field_type]
    if not last:
        out_shape += [field_type, jax.ShapeDtypeStruct((8, 128), jnp.float32)]
    got = pl.pallas_call(
        functools.partial(_cg_kernel, names, first, last),
        out_shape=tuple(out_shape),
        in_specs=[pl.BlockSpec(memory_space=pltpu.VMEM)] * len(fields),
        out_specs=tuple(pl.BlockSpec(memory_space=pltpu.VMEM) for _ in out_shape),
        scratch_shapes=[
            pltpu.VMEM((nrow, 8, 128), jnp.float32),
            pltpu.VMEM((ncol, 8, 128), jnp.float32),
            pltpu.VMEM((8, 128), jnp.float32),
            pltpu.VMEM((8, 128), jnp.float32),
            pltpu.SemaphoreType.DMA((nrow,)),
            pltpu.SemaphoreType.DMA((nrow,)),
            pltpu.SemaphoreType.DMA((ncol,)),
            pltpu.SemaphoreType.DMA((ncol,)),
        ],
        compiler_params=pltpu.CompilerParams(
            collective_id=10 + iteration, has_side_effects=True
        ),
    )(*fields)
    update = got[0].reshape(shape)
    residual = got[1].reshape(shape)
    if last:
        return update, residual, None, None
    return update, residual, got[2].reshape(shape), got[3]


def tile_view(control, tile_rows, tile_cols, points):
    return control.reshape(2, tile_rows, points, tile_cols, points)


def edge_band(tile_grid, facing, band_depth):
    if facing == 0:
        return tile_grid[..., ::-1][..., :band_depth].transpose(0, 1, 3, 2, 4)
    if facing == 1:
        return tile_grid[..., :band_depth].transpose(0, 1, 3, 2, 4)
    if facing == 2:
        return tile_grid[:, :, ::-1][:, :, :band_depth].transpose(0, 1, 3, 4, 2)
    return tile_grid[:, :, :band_depth].transpose(0, 1, 3, 4, 2)


def place_edge(band_part, facing, points):
    band_depth = band_part.shape[4]
    if facing < 2:
        widened = jnp.pad(
            band_part.transpose(0, 1, 3, 2, 4),
            ((0, 0), (0, 0), (0, 0), (0, 0), (0, points - band_depth)),
        )
        if facing == 0:
            return widened[..., ::-1]
        return widened
    widened = jnp.pad(
        band_part.transpose(0, 1, 4, 2, 3),
        ((0, 0), (0, 0), (0, points - band_depth), (0, 0), (0, 0)),
    )
    if facing == 2:
        return widened[:, :, ::-1]
    return widened


def make_tables(along_cell, across, frac_pair):
    weight_along = (frac_pair[0].astype(jnp.float32) + 0.5) / 256.0
    weight_across = (frac_pair[1].astype(jnp.float32) + 0.5) / 256.0
    return (along_cell, across, weight_along, weight_across)


def weight_tables(tables, points, band_depth):
    along_cell, across, weight_along, weight_across = tables
    along_iota = jnp.arange(points, dtype=jnp.int32)[None, None, :, None]
    across_iota = jnp.arange(band_depth, dtype=jnp.int32)[None, None, :, None]
    cell_now = along_cell[:, :, None, :]
    depth_now = across[:, :, None, :]
    frac_along = weight_along[:, :, None, :]
    frac_across = weight_across[:, :, None, :]
    along_table = (1.0 - frac_along) * (along_iota == cell_now).astype(jnp.float32) + frac_along * (
        along_iota == cell_now + 1
    ).astype(jnp.float32)
    across_table = (1.0 - frac_across) * (across_iota == depth_now).astype(
        jnp.float32
    ) + frac_across * (across_iota == depth_now + 1).astype(jnp.float32)
    return (along_table, across_table)


def interpolate(band_part, tables):
    along_table, across_table = weight_tables(tables, band_part.shape[3], band_part.shape[4])
    partial_sum = jnp.einsum(
        "cabiq,abis->cabqs", band_part, along_table, precision=lax.Precision.HIGHEST
    )
    return jnp.sum(partial_sum * across_table[None], axis=3)


def spread_back(residual, tables, points, band_depth):
    along_table, across_table = weight_tables(tables, points, band_depth)
    weighted = residual[:, :, :, None, :] * across_table[None]
    return jnp.einsum("cabqs,abis->cabiq", weighted, along_table, precision=lax.Precision.HIGHEST)


def bending(control, tile_rows, tile_cols):
    grid_view = tile_view(control, tile_rows, tile_cols, GRID)
    inner = (
        grid_view[:, :, :-2, :, 1:-1]
        + grid_view[:, :, 2:, :, 1:-1]
        + grid_view[:, :, 1:-1, :, :-2]
        + grid_view[:, :, 1:-1, :, 2:]
        - 4.0 * grid_view[:, :, 1:-1, :, 1:-1]
    )
    widths = ((0, 0), (0, 0), (1, 1), (0, 0), (1, 1))
    curvature = jnp.pad(inner, widths)
    padded = jnp.pad(curvature, widths)
    result = (
        padded[:, :, :-2, :, 1:-1]
        + padded[:, :, 2:, :, 1:-1]
        + padded[:, :, 1:-1, :, :-2]
        + padded[:, :, 1:-1, :, 2:]
        - 4.0 * curvature
    )
    return result.reshape(control.shape)


def _halo_kernel(names, send_ref, recv_ref, send_sems, recv_sems):
    ncol = lax.axis_size("col")
    nrow = lax.axis_size("row")
    ci = lax.axis_index("col")
    ri = lax.axis_index("row")

    def dev(c, r):
        where = {"col": c, "row": r}
        return tuple(where[n] for n in names)

    peers = [
        dev((ci + 1) % ncol, ri),
        dev((ci + ncol - 1) % ncol, ri),
        dev(ci, (ri + 1) % nrow),
        dev(ci, (ri + nrow - 1) % nrow),
    ]
    barrier = pltpu.get_barrier_semaphore()
    for peer in peers:
        pl.semaphore_signal(barrier, 1, device_id=peer, device_id_type=MESH_ID)
    pl.semaphore_wait(barrier, len(peers))
    copies = [
        pltpu.make_async_remote_copy(
            src_ref=send_ref.at[k], dst_ref=recv_ref.at[k], send_sem=send_sems.at[k],
            recv_sem=recv_sems.at[k], device_id=peers[k], device_id_type=MESH_ID)
        for k in range(4)
    ]
    for copy in copies:
        copy.start()
    for copy in copies:
        copy.wait_send()
        copy.wait_recv()


def halo_exchange(names, to_east, to_west, to_south, to_north):
    slabs = [to_east, to_west, to_south, to_north]
    rows = max(slab.shape[0] for slab in slabs)
    lanes = slabs[0].shape[1]
    stacked = jnp.stack([jnp.pad(slab, ((0, rows - slab.shape[0]), (0, 0))) for slab in slabs])
    got = pl.pallas_call(
        functools.partial(_halo_kernel, names),
        out_shape=jax.ShapeDtypeStruct(stacked.shape, jnp.float32),
        in_specs=[pl.BlockSpec(memory_space=pltpu.VMEM)],
        out_specs=pl.BlockSpec(memory_space=pltpu.VMEM),
        scratch_shapes=[pltpu.SemaphoreType.DMA((4,)), pltpu.SemaphoreType.DMA((4,))],
        compiler_params=pltpu.CompilerParams(collective_id=1, has_side_effects=True),
    )(stacked)
    return [got[k, : slabs[k].shape[0]] for k in range(4)]


def all_weight_tables(tables):
    pairs = [weight_tables(tables[facing], GRID, BAND) for facing in range(4)]
    return (jnp.stack([pair[0] for pair in pairs]), jnp.stack([pair[1] for pair in pairs]))


def seam_term(control, target, tables, adjacency, names):
    tile_rows, tile_cols = (adjacency.shape[1], adjacency.shape[2])
    along_table, across_table = tables
    grid_view = tile_view(control, tile_rows, tile_cols, GRID)
    bands = jnp.stack([edge_band(grid_view, facing, BAND) for facing in range(4)])
    partial_sum = jnp.einsum(
        "kcabiq,kabis->kcabqs", bands, along_table, precision=lax.Precision.HIGHEST
    )
    stacked_values = jnp.sum(partial_sum * across_table[:, None], axis=4)
    seam_values = [stacked_values[facing] for facing in range(4)]
    samples = seam_values[0].shape[3]
    col_pos = lax.axis_index("col") * tile_cols + jnp.arange(tile_cols)
    row_pos = lax.axis_index("row") * tile_rows + jnp.arange(tile_rows)
    mask_east = (
        adjacency[0].astype(jnp.float32)
        * (col_pos < lax.axis_size("col") * tile_cols - 1).astype(jnp.float32)[None, :]
    )
    mask_south = (
        adjacency[1].astype(jnp.float32)
        * (row_pos < lax.axis_size("row") * tile_rows - 1).astype(jnp.float32)[:, None]
    )
    own_east = seam_values[0]
    own_south = seam_values[2]
    if target is not None:
        own_east = own_east - target[0]
        own_south = own_south - target[1]
    to_east = jnp.concatenate(
        [
            own_east[:, :, -1].reshape(2 * tile_rows, samples),
            jnp.broadcast_to(mask_east[:, -1:], (tile_rows, samples)),
        ]
    )
    to_west = seam_values[1][:, :, 0].reshape(2 * tile_rows, samples)
    to_south = jnp.concatenate(
        [
            own_south[:, -1].reshape(2 * tile_cols, samples),
            jnp.broadcast_to(mask_south[-1][:, None], (tile_cols, samples)),
        ]
    )
    to_north = seam_values[3][:, 0].reshape(2 * tile_cols, samples)
    got_west, got_east, got_north, got_south = halo_exchange(
        names, to_east, to_west, to_south, to_north
    )
    west_east = got_west[: 2 * tile_rows].reshape(2, tile_rows, 1, samples)
    west_mask = got_west[2 * tile_rows :].reshape(1, tile_rows, 1, samples)
    east_next = got_east.reshape(2, tile_rows, 1, samples)
    north_south = got_north[: 2 * tile_cols].reshape(2, 1, tile_cols, samples)
    north_mask = got_north[2 * tile_cols :].reshape(1, 1, tile_cols, samples)
    south_next = got_south.reshape(2, 1, tile_cols, samples)
    west_next = jnp.concatenate([seam_values[1][:, :, 1:], east_next], axis=2)
    north_next = jnp.concatenate([seam_values[3][:, 1:], south_next], axis=1)
    resid_east = (own_east - west_next) * mask_east[None, :, :, None]
    resid_south = (own_south - north_next) * mask_south[None, :, :, None]
    from_west = (west_east - seam_values[1][:, :, :1]) * west_mask
    from_north = (north_south - seam_values[3][:, :1]) * north_mask
    resid_west = -jnp.concatenate([from_west, resid_east[:, :, :-1]], axis=2)
    resid_north = -jnp.concatenate([from_north, resid_south[:, :-1]], axis=1)
    residuals = jnp.stack([resid_east, resid_west, resid_south, resid_north])
    weighted = residuals[:, :, :, :, None, :] * across_table[:, None]
    spread_parts = jnp.einsum(
        "kcabqs,kabis->kcabiq", weighted, along_table, precision=lax.Precision.HIGHEST
    )
    summed = (
        place_edge(spread_parts[0], 0, GRID)
        + place_edge(spread_parts[1], 1, GRID)
        + place_edge(spread_parts[2], 2, GRID)
        + place_edge(spread_parts[3], 3, GRID)
    )
    return summed.reshape(control.shape)


def hessian_apply(control, tables, adjacency, names):
    tile_rows, tile_cols = (adjacency.shape[1], adjacency.shape[2])
    return (
        seam_term(control, None, tables, adjacency, names)
        + BEND_WEIGHT * bending(control, tile_rows, tile_cols)
        + DAMPING * control
    )


def shards(names, start_field, seam_target, seam_rows, seam_band, seam_frac, adjacency):
    tile_rows, tile_cols = (adjacency.shape[1], adjacency.shape[2])
    samples = seam_rows.shape[2] // tile_cols
    along_cells = seam_rows.reshape(4, tile_rows, tile_cols, samples)
    across_cells = seam_band.reshape(4, tile_rows, tile_cols, samples)
    frac_cells = seam_frac.reshape(4, 2, tile_rows, tile_cols, samples)
    tables = [
        make_tables(along_cells[facing], across_cells[facing], frac_cells[facing])
        for facing in range(4)
    ]
    tables = all_weight_tables(tables)
    target_cells = seam_target.reshape(2, 2, tile_rows, tile_cols, samples)
    target = (target_cells[0], target_cells[1])
    control = start_field
    gradient = seam_term(control, target, tables, adjacency, names) + BEND_WEIGHT * bending(
        control, tile_rows, tile_cols
    )
    residual = -gradient
    update = None
    direction = residual
    norm_tile = None
    for iteration in range(ITERS):
        seam_image = seam_term(direction, None, tables, adjacency, names)
        update, residual, direction, norm_tile = cg_step(
            names, iteration, direction, seam_image, residual, update, norm_tile
        )
    control = control + update
    return (control, residual)


def solution(mesh):
    placed = (
        P(None, "row", "col"),
        P(None, None, "row", "col"),
        P(None, "row", "col"),
        P(None, "row", "col"),
        P(None, None, "row", "col"),
        P(None, "row", "col"),
    )
    return jax.shard_map(
        functools.partial(shards, tuple(mesh.axis_names)),
        mesh=mesh,
        in_specs=placed,
        out_specs=(P(None, "row", "col"), P(None, "row", "col")),
        check_vma=False,
    )
```

```python
import functools

import jax
import jax.numpy as jnp
from jax import lax
from jax.experimental import pallas as pl
from jax.experimental.pallas import tpu as pltpu
from jax.sharding import PartitionSpec as P

GRID = 32
BAND = 4
ITERS = 3


BEND_WEIGHT = 0.05
DAMPING = 0.5


MESH_ID = pl.DeviceIdType.MESH


def _cg_kernel(names, first, last, d_ref, h_ref, r_ref, *refs):
    if not first:
        u_ref, rr_ref = refs[:2]
        refs = refs[2:]
    if last:
        image_out, step_out, row_buf, col_buf, mine, part, row_send, row_recv, col_send, col_recv = refs
    else:
        (u_out, r_out, d_out, rr_out, row_buf, col_buf, mine, part, row_send, row_recv, col_send,
         col_recv) = refs
    ncol = lax.axis_size("col")
    nrow = lax.axis_size("row")
    ci = lax.axis_index("col")
    ri = lax.axis_index("row")

    def dev(c, r):
        where = {"col": c, "row": r}
        return tuple(where[n] for n in names)

    barrier = pltpu.get_barrier_semaphore()

    @pl.loop(1, nrow)
    def _(k):
        pl.semaphore_signal(barrier, 1, device_id=dev(ci, (ri + k) % nrow), device_id_type=MESH_ID)

    @pl.loop(1, ncol)
    def _(k):
        pl.semaphore_signal(barrier, 1, device_id=dev((ci + k) % ncol, ri), device_id_type=MESH_ID)

    direction = d_ref[...]
    residual = r_ref[...]
    rows, cols = direction.shape
    y = lax.broadcasted_iota(jnp.int32, (rows, cols), 0) % GRID
    x = lax.broadcasted_iota(jnp.int32, (rows, cols), 1) % GRID
    inside = (y >= 1) & (y <= GRID - 2) & (x >= 1) & (x <= GRID - 2)

    def five_point(f):
        return (
            pltpu.roll(f, 1, 0)
            + pltpu.roll(f, rows - 1, 0)
            + pltpu.roll(f, 1, 1)
            + pltpu.roll(f, cols - 1, 1)
            - 4.0 * f
        )

    curvature = jnp.where(inside, five_point(direction), 0.0)
    image = h_ref[...] + BEND_WEIGHT * five_point(curvature) + DAMPING * direction

    def total(x):
        return jnp.sum(jnp.sum(x, axis=0, keepdims=True), axis=1, keepdims=True)

    parts = [total(direction * image)]
    if not last:
        parts += [total(image * image), total(residual * image)]
    if first:
        parts += [total(residual * residual)]
    lane = lax.broadcasted_iota(jnp.int32, (8, 128), 1)
    sub = lax.broadcasted_iota(jnp.int32, (8, 128), 0)
    tile = jnp.zeros((8, 128), jnp.float32)
    for k, value in enumerate(parts):
        tile = jnp.where((sub == 0) & (lane == k), value, tile)
    mine[...] = tile

    pl.semaphore_wait(barrier, nrow - 1 + ncol - 1)

    def row_copy(peer, slot):
        return pltpu.make_async_remote_copy(
            src_ref=mine, dst_ref=row_buf.at[slot], send_sem=row_send.at[peer],
            recv_sem=row_recv.at[slot], device_id=dev(ci, peer), device_id_type=MESH_ID)

    for k in range(1, nrow):
        row_copy((ri + k) % nrow, ri).start()
    row_buf[ri] = tile
    for k in range(1, nrow):
        row_copy((ri + k) % nrow, ri).wait_send()
        peer = (ri + nrow - k) % nrow
        row_copy(peer, peer).wait_recv()
    summed = row_buf[0]
    for j in range(1, nrow):
        summed = summed + row_buf[j]
    part[...] = summed

    def col_copy(peer, slot):
        return pltpu.make_async_remote_copy(
            src_ref=part, dst_ref=col_buf.at[slot], send_sem=col_send.at[peer],
            recv_sem=col_recv.at[slot], device_id=dev(peer, ri), device_id_type=MESH_ID)

    @pl.loop(1, ncol)
    def _(k):
        col_copy((ci + k) % ncol, ci).start()

    col_buf[ci] = summed

    @pl.loop(1, ncol)
    def _(k):
        col_copy((ci + k) % ncol, ci).wait_send()
        peer = (ci + ncol - k) % ncol
        col_copy(peer, peer).wait_recv()

    summed = lax.fori_loop(1, ncol, lambda j, acc: acc + col_buf[j], col_buf[0])

    def pick(k):
        return jnp.sum(jnp.where((sub == 0) & (lane == k), summed, 0.0), axis=(0, 1), keepdims=True)

    curv = pick(0)
    norm_now = pick(len(parts) - 1) if first else rr_ref[0:1, 0:1]
    step_size = norm_now / curv
    if last:
        image_out[...] = image
        step_out[...] = jnp.broadcast_to(step_size, (8, 128))
        return
    if first:
        u_out[...] = step_size * direction
    else:
        u_out[...] = u_ref[...] + step_size * direction
    residual = residual - step_size * image
    r_out[...] = residual
    if not last:
        image_sq = pick(1)
        cross = curv if first else pick(2)
        norm_next = norm_now - 2.0 * step_size * cross + step_size * step_size * image_sq
        d_out[...] = residual + norm_next / norm_now * direction
        rr_out[...] = jnp.broadcast_to(norm_next, (8, 128))


def cg_step(names, iteration, direction, image, residual, update, norm_tile):
    ncol = lax.axis_size("col")
    nrow = lax.axis_size("row")
    first = iteration == 0
    last = iteration == ITERS - 1
    shape = direction.shape
    flat = (shape[0] * shape[1], shape[2])
    fields = [x.reshape(flat) for x in (direction, image, residual)]
    if not first:
        fields += [update.reshape(flat), norm_tile]
    field_type = jax.ShapeDtypeStruct(flat, jnp.float32)
    tile_type = jax.ShapeDtypeStruct((8, 128), jnp.float32)
    out_shape = [field_type, tile_type] if last else [field_type, field_type, field_type, tile_type]
    got = pl.pallas_call(
        functools.partial(_cg_kernel, names, first, last),
        out_shape=tuple(out_shape),
        in_specs=[pl.BlockSpec(memory_space=pltpu.VMEM)] * len(fields),
        out_specs=tuple(pl.BlockSpec(memory_space=pltpu.VMEM) for _ in out_shape),
        scratch_shapes=[
            pltpu.VMEM((nrow, 8, 128), jnp.float32),
            pltpu.VMEM((ncol, 8, 128), jnp.float32),
            pltpu.VMEM((8, 128), jnp.float32),
            pltpu.VMEM((8, 128), jnp.float32),
            pltpu.SemaphoreType.DMA((nrow,)),
            pltpu.SemaphoreType.DMA((nrow,)),
            pltpu.SemaphoreType.DMA((ncol,)),
            pltpu.SemaphoreType.DMA((ncol,)),
        ],
        compiler_params=pltpu.CompilerParams(
            collective_id=10 + iteration, has_side_effects=True
        ),
    )(*fields)
    if last:
        step_size = got[1][0, 0]
        update = update + step_size * direction
        residual = residual - step_size * got[0].reshape(shape)
        return update, residual, None, None
    update = got[0].reshape(shape)
    residual = got[1].reshape(shape)
    return update, residual, got[2].reshape(shape), got[3]


def tile_view(control, tile_rows, tile_cols, points):
    return control.reshape(2, tile_rows, points, tile_cols, points)


def edge_band(tile_grid, facing, band_depth):
    if facing == 0:
        return tile_grid[..., ::-1][..., :band_depth].transpose(0, 1, 3, 2, 4)
    if facing == 1:
        return tile_grid[..., :band_depth].transpose(0, 1, 3, 2, 4)
    if facing == 2:
        return tile_grid[:, :, ::-1][:, :, :band_depth].transpose(0, 1, 3, 4, 2)
    return tile_grid[:, :, :band_depth].transpose(0, 1, 3, 4, 2)


def place_edge(band_part, facing, points):
    band_depth = band_part.shape[4]
    if facing < 2:
        widened = jnp.pad(
            band_part.transpose(0, 1, 3, 2, 4),
            ((0, 0), (0, 0), (0, 0), (0, 0), (0, points - band_depth)),
        )
        if facing == 0:
            return widened[..., ::-1]
        return widened
    widened = jnp.pad(
        band_part.transpose(0, 1, 4, 2, 3),
        ((0, 0), (0, 0), (0, points - band_depth), (0, 0), (0, 0)),
    )
    if facing == 2:
        return widened[:, :, ::-1]
    return widened


def make_tables(along_cell, across, frac_pair):
    weight_along = (frac_pair[0].astype(jnp.float32) + 0.5) / 256.0
    weight_across = (frac_pair[1].astype(jnp.float32) + 0.5) / 256.0
    return (along_cell, across, weight_along, weight_across)


def weight_tables(tables, points, band_depth):
    along_cell, across, weight_along, weight_across = tables
    along_iota = jnp.arange(points, dtype=jnp.int32)[None, None, :, None]
    across_iota = jnp.arange(band_depth, dtype=jnp.int32)[None, None, :, None]
    cell_now = along_cell[:, :, None, :]
    depth_now = across[:, :, None, :]
    frac_along = weight_along[:, :, None, :]
    frac_across = weight_across[:, :, None, :]
    along_table = (1.0 - frac_along) * (along_iota == cell_now).astype(jnp.float32) + frac_along * (
        along_iota == cell_now + 1
    ).astype(jnp.float32)
    across_table = (1.0 - frac_across) * (across_iota == depth_now).astype(
        jnp.float32
    ) + frac_across * (across_iota == depth_now + 1).astype(jnp.float32)
    return (along_table, across_table)


def interpolate(band_part, tables):
    along_table, across_table = weight_tables(tables, band_part.shape[3], band_part.shape[4])
    partial_sum = jnp.einsum(
        "cabiq,abis->cabqs", band_part, along_table, precision=lax.Precision.HIGHEST
    )
    return jnp.sum(partial_sum * across_table[None], axis=3)


def spread_back(residual, tables, points, band_depth):
    along_table, across_table = weight_tables(tables, points, band_depth)
    weighted = residual[:, :, :, None, :] * across_table[None]
    return jnp.einsum("cabqs,abis->cabiq", weighted, along_table, precision=lax.Precision.HIGHEST)


def bending(control, tile_rows, tile_cols):
    grid_view = tile_view(control, tile_rows, tile_cols, GRID)
    inner = (
        grid_view[:, :, :-2, :, 1:-1]
        + grid_view[:, :, 2:, :, 1:-1]
        + grid_view[:, :, 1:-1, :, :-2]
        + grid_view[:, :, 1:-1, :, 2:]
        - 4.0 * grid_view[:, :, 1:-1, :, 1:-1]
    )
    widths = ((0, 0), (0, 0), (1, 1), (0, 0), (1, 1))
    curvature = jnp.pad(inner, widths)
    padded = jnp.pad(curvature, widths)
    result = (
        padded[:, :, :-2, :, 1:-1]
        + padded[:, :, 2:, :, 1:-1]
        + padded[:, :, 1:-1, :, :-2]
        + padded[:, :, 1:-1, :, 2:]
        - 4.0 * curvature
    )
    return result.reshape(control.shape)


def _halo_kernel(names, send_ref, recv_ref, send_sems, recv_sems):
    ncol = lax.axis_size("col")
    nrow = lax.axis_size("row")
    ci = lax.axis_index("col")
    ri = lax.axis_index("row")

    def dev(c, r):
        where = {"col": c, "row": r}
        return tuple(where[n] for n in names)

    peers = [
        dev((ci + 1) % ncol, ri),
        dev((ci + ncol - 1) % ncol, ri),
        dev(ci, (ri + 1) % nrow),
        dev(ci, (ri + nrow - 1) % nrow),
    ]
    barrier = pltpu.get_barrier_semaphore()
    for peer in peers:
        pl.semaphore_signal(barrier, 1, device_id=peer, device_id_type=MESH_ID)
    pl.semaphore_wait(barrier, len(peers))
    copies = [
        pltpu.make_async_remote_copy(
            src_ref=send_ref.at[k], dst_ref=recv_ref.at[k], send_sem=send_sems.at[k],
            recv_sem=recv_sems.at[k], device_id=peers[k], device_id_type=MESH_ID)
        for k in range(4)
    ]
    for copy in copies:
        copy.start()
    for copy in copies:
        copy.wait_send()
        copy.wait_recv()


def halo_exchange(names, to_east, to_west, to_south, to_north):
    slabs = [to_east, to_west, to_south, to_north]
    rows = max(slab.shape[0] for slab in slabs)
    lanes = slabs[0].shape[1]
    stacked = jnp.stack([jnp.pad(slab, ((0, rows - slab.shape[0]), (0, 0))) for slab in slabs])
    got = pl.pallas_call(
        functools.partial(_halo_kernel, names),
        out_shape=jax.ShapeDtypeStruct(stacked.shape, jnp.float32),
        in_specs=[pl.BlockSpec(memory_space=pltpu.VMEM)],
        out_specs=pl.BlockSpec(memory_space=pltpu.VMEM),
        scratch_shapes=[pltpu.SemaphoreType.DMA((4,)), pltpu.SemaphoreType.DMA((4,))],
        compiler_params=pltpu.CompilerParams(collective_id=1, has_side_effects=True),
    )(stacked)
    return [got[k, : slabs[k].shape[0]] for k in range(4)]


def all_weight_tables(tables):
    pairs = [weight_tables(tables[facing], GRID, BAND) for facing in range(4)]
    return (jnp.stack([pair[0] for pair in pairs]), jnp.stack([pair[1] for pair in pairs]))


def seam_term(control, target, tables, adjacency, names):
    tile_rows, tile_cols = (adjacency.shape[1], adjacency.shape[2])
    along_table, across_table = tables
    grid_view = tile_view(control, tile_rows, tile_cols, GRID)
    bands = jnp.stack([edge_band(grid_view, facing, BAND) for facing in range(4)])
    partial_sum = jnp.einsum(
        "kcabiq,kabis->kcabqs", bands, along_table, precision=lax.Precision.HIGHEST
    )
    stacked_values = jnp.sum(partial_sum * across_table[:, None], axis=4)
    seam_values = [stacked_values[facing] for facing in range(4)]
    samples = seam_values[0].shape[3]
    col_pos = lax.axis_index("col") * tile_cols + jnp.arange(tile_cols)
    row_pos = lax.axis_index("row") * tile_rows + jnp.arange(tile_rows)
    mask_east = (
        adjacency[0].astype(jnp.float32)
        * (col_pos < lax.axis_size("col") * tile_cols - 1).astype(jnp.float32)[None, :]
    )
    mask_south = (
        adjacency[1].astype(jnp.float32)
        * (row_pos < lax.axis_size("row") * tile_rows - 1).astype(jnp.float32)[:, None]
    )
    own_east = seam_values[0]
    own_south = seam_values[2]
    if target is not None:
        own_east = own_east - target[0]
        own_south = own_south - target[1]
    to_east = jnp.concatenate(
        [
            own_east[:, :, -1].reshape(2 * tile_rows, samples),
            jnp.broadcast_to(mask_east[:, -1:], (tile_rows, samples)),
        ]
    )
    to_west = seam_values[1][:, :, 0].reshape(2 * tile_rows, samples)
    to_south = jnp.concatenate(
        [
            own_south[:, -1].reshape(2 * tile_cols, samples),
            jnp.broadcast_to(mask_south[-1][:, None], (tile_cols, samples)),
        ]
    )
    to_north = seam_values[3][:, 0].reshape(2 * tile_cols, samples)
    got_west, got_east, got_north, got_south = halo_exchange(
        names, to_east, to_west, to_south, to_north
    )
    west_east = got_west[: 2 * tile_rows].reshape(2, tile_rows, 1, samples)
    west_mask = got_west[2 * tile_rows :].reshape(1, tile_rows, 1, samples)
    east_next = got_east.reshape(2, tile_rows, 1, samples)
    north_south = got_north[: 2 * tile_cols].reshape(2, 1, tile_cols, samples)
    north_mask = got_north[2 * tile_cols :].reshape(1, 1, tile_cols, samples)
    south_next = got_south.reshape(2, 1, tile_cols, samples)
    west_next = jnp.concatenate([seam_values[1][:, :, 1:], east_next], axis=2)
    north_next = jnp.concatenate([seam_values[3][:, 1:], south_next], axis=1)
    resid_east = (own_east - west_next) * mask_east[None, :, :, None]
    resid_south = (own_south - north_next) * mask_south[None, :, :, None]
    from_west = (west_east - seam_values[1][:, :, :1]) * west_mask
    from_north = (north_south - seam_values[3][:, :1]) * north_mask
    resid_west = -jnp.concatenate([from_west, resid_east[:, :, :-1]], axis=2)
    resid_north = -jnp.concatenate([from_north, resid_south[:, :-1]], axis=1)
    residuals = jnp.stack([resid_east, resid_west, resid_south, resid_north])
    weighted = residuals[:, :, :, :, None, :] * across_table[:, None]
    spread_parts = jnp.einsum(
        "kcabqs,kabis->kcabiq", weighted, along_table, precision=lax.Precision.HIGHEST
    )
    summed = (
        place_edge(spread_parts[0], 0, GRID)
        + place_edge(spread_parts[1], 1, GRID)
        + place_edge(spread_parts[2], 2, GRID)
        + place_edge(spread_parts[3], 3, GRID)
    )
    return summed.reshape(control.shape)


def hessian_apply(control, tables, adjacency, names):
    tile_rows, tile_cols = (adjacency.shape[1], adjacency.shape[2])
    return (
        seam_term(control, None, tables, adjacency, names)
        + BEND_WEIGHT * bending(control, tile_rows, tile_cols)
        + DAMPING * control
    )


def shards(names, start_field, seam_target, seam_rows, seam_band, seam_frac, adjacency):
    tile_rows, tile_cols = (adjacency.shape[1], adjacency.shape[2])
    samples = seam_rows.shape[2] // tile_cols
    along_cells = seam_rows.reshape(4, tile_rows, tile_cols, samples)
    across_cells = seam_band.reshape(4, tile_rows, tile_cols, samples)
    frac_cells = seam_frac.reshape(4, 2, tile_rows, tile_cols, samples)
    tables = [
        make_tables(along_cells[facing], across_cells[facing], frac_cells[facing])
        for facing in range(4)
    ]
    tables = all_weight_tables(tables)
    target_cells = seam_target.reshape(2, 2, tile_rows, tile_cols, samples)
    target = (target_cells[0], target_cells[1])
    control = start_field
    gradient = seam_term(control, target, tables, adjacency, names) + BEND_WEIGHT * bending(
        control, tile_rows, tile_cols
    )
    residual = -gradient
    update = None
    direction = residual
    norm_tile = None
    for iteration in range(ITERS):
        seam_image = seam_term(direction, None, tables, adjacency, names)
        update, residual, direction, norm_tile = cg_step(
            names, iteration, direction, seam_image, residual, update, norm_tile
        )
    control = control + update
    return (control, residual)


def solution(mesh):
    placed = (
        P(None, "row", "col"),
        P(None, None, "row", "col"),
        P(None, "row", "col"),
        P(None, "row", "col"),
        P(None, None, "row", "col"),
        P(None, "row", "col"),
    )
    return jax.shard_map(
        functools.partial(shards, tuple(mesh.axis_names)),
        mesh=mesh,
        in_specs=placed,
        out_specs=(P(None, "row", "col"), P(None, "row", "col")),
        check_vma=False,
    )
```

```python
import functools

import jax
import jax.numpy as jnp
from jax import lax
from jax.experimental import pallas as pl
from jax.experimental.pallas import tpu as pltpu
from jax.sharding import PartitionSpec as P

GRID = 32
BAND = 4
ITERS = 3


BEND_WEIGHT = 0.05
DAMPING = 0.5


MESH_ID = pl.DeviceIdType.MESH


def _cg_kernel(names, first, last, d_ref, h_ref, r_ref, *refs):
    if not first:
        u_ref, rr_ref = refs[:2]
        refs = refs[2:]
    if last:
        u_out, r_out, row_buf, col_buf, mine, part, row_send, row_recv, col_send, col_recv = refs
    else:
        (u_out, r_out, d_out, rr_out, row_buf, col_buf, mine, part, row_send, row_recv, col_send,
         col_recv) = refs
    ncol = lax.axis_size("col")
    nrow = lax.axis_size("row")
    ci = lax.axis_index("col")
    ri = lax.axis_index("row")

    def dev(c, r):
        where = {"col": c, "row": r}
        return tuple(where[n] for n in names)

    barrier = pltpu.get_barrier_semaphore()

    @pl.loop(1, nrow)
    def _(k):
        pl.semaphore_signal(barrier, 1, device_id=dev(ci, (ri + k) % nrow), device_id_type=MESH_ID)

    @pl.loop(1, ncol)
    def _(k):
        pl.semaphore_signal(barrier, 1, device_id=dev((ci + k) % ncol, ri), device_id_type=MESH_ID)

    direction = d_ref[...]
    residual = r_ref[...]
    rows, cols = direction.shape
    y = lax.broadcasted_iota(jnp.int32, (rows, cols), 0) % GRID
    x = lax.broadcasted_iota(jnp.int32, (rows, cols), 1) % GRID
    inside = (y >= 1) & (y <= GRID - 2) & (x >= 1) & (x <= GRID - 2)

    def five_point(f):
        return (
            pltpu.roll(f, 1, 0)
            + pltpu.roll(f, rows - 1, 0)
            + pltpu.roll(f, 1, 1)
            + pltpu.roll(f, cols - 1, 1)
            - 4.0 * f
        )

    curvature = jnp.where(inside, five_point(direction), 0.0)
    image = h_ref[...] + BEND_WEIGHT * five_point(curvature) + DAMPING * direction

    def total(x):
        return jnp.sum(jnp.sum(x, axis=0, keepdims=True), axis=1, keepdims=True)

    parts = [total(direction * image)]
    if not last:
        parts += [total(image * image), total(residual * image)]
    if first:
        parts += [total(residual * residual)]
    lane = lax.broadcasted_iota(jnp.int32, (8, 128), 1)
    sub = lax.broadcasted_iota(jnp.int32, (8, 128), 0)
    tile = jnp.zeros((8, 128), jnp.float32)
    for k, value in enumerate(parts):
        tile = jnp.where((sub == 0) & (lane == k), value, tile)
    mine[...] = tile

    pl.semaphore_wait(barrier, nrow - 1 + ncol - 1)

    def row_copy(peer, slot):
        return pltpu.make_async_remote_copy(
            src_ref=mine, dst_ref=row_buf.at[slot], send_sem=row_send.at[peer],
            recv_sem=row_recv.at[slot], device_id=dev(ci, peer), device_id_type=MESH_ID)

    for k in range(1, nrow):
        row_copy((ri + k) % nrow, ri).start()
    row_buf[ri] = tile
    for k in range(1, nrow):
        row_copy((ri + k) % nrow, ri).wait_send()
        peer = (ri + nrow - k) % nrow
        row_copy(peer, peer).wait_recv()
    summed = row_buf[0]
    for j in range(1, nrow):
        summed = summed + row_buf[j]
    part[...] = summed

    def col_copy(peer, slot):
        return pltpu.make_async_remote_copy(
            src_ref=part, dst_ref=col_buf.at[slot], send_sem=col_send.at[peer],
            recv_sem=col_recv.at[slot], device_id=dev(peer, ri), device_id_type=MESH_ID)

    @pl.loop(1, ncol)
    def _(k):
        col_copy((ci + k) % ncol, ci).start()

    col_buf[ci] = summed

    @pl.loop(1, ncol)
    def _(k):
        col_copy((ci + k) % ncol, ci).wait_send()
        peer = (ci + ncol - k) % ncol
        col_copy(peer, peer).wait_recv()

    summed = lax.fori_loop(1, ncol, lambda j, acc: acc + col_buf[j], col_buf[0])

    def pick(k):
        return jnp.sum(jnp.where((sub == 0) & (lane == k), summed, 0.0), axis=(0, 1), keepdims=True)

    curv = pick(0)
    norm_now = pick(len(parts) - 1) if first else rr_ref[0:1, 0:1]
    step_size = norm_now / curv
    if first:
        u_out[...] = step_size * direction
    else:
        u_out[...] = u_ref[...] + step_size * direction
    residual = residual - step_size * image
    r_out[...] = residual
    if not last:
        image_sq = pick(1)
        cross = curv if first else pick(2)
        norm_next = norm_now - 2.0 * step_size * cross + step_size * step_size * image_sq
        d_out[...] = residual + norm_next / norm_now * direction
        rr_out[...] = jnp.broadcast_to(norm_next, (8, 128))


def cg_step(names, iteration, direction, image, residual, update, norm_tile):
    ncol = lax.axis_size("col")
    nrow = lax.axis_size("row")
    first = iteration == 0
    last = iteration == ITERS - 1
    shape = direction.shape
    flat = (shape[0] * shape[1], shape[2])
    fields = [x.reshape(flat) for x in (direction, image, residual)]
    if not first:
        fields += [update.reshape(flat), norm_tile]
    field_type = jax.ShapeDtypeStruct(flat, jnp.float32)
    out_shape = [field_type, field_type]
    if not last:
        out_shape += [field_type, jax.ShapeDtypeStruct((8, 128), jnp.float32)]
    got = pl.pallas_call(
        functools.partial(_cg_kernel, names, first, last),
        out_shape=tuple(out_shape),
        in_specs=[pl.BlockSpec(memory_space=pltpu.VMEM)] * len(fields),
        out_specs=tuple(pl.BlockSpec(memory_space=pltpu.VMEM) for _ in out_shape),
        scratch_shapes=[
            pltpu.VMEM((nrow, 8, 128), jnp.float32),
            pltpu.VMEM((ncol, 8, 128), jnp.float32),
            pltpu.VMEM((8, 128), jnp.float32),
            pltpu.VMEM((8, 128), jnp.float32),
            pltpu.SemaphoreType.DMA((nrow,)),
            pltpu.SemaphoreType.DMA((nrow,)),
            pltpu.SemaphoreType.DMA((ncol,)),
            pltpu.SemaphoreType.DMA((ncol,)),
        ],
        compiler_params=pltpu.CompilerParams(
            collective_id=10 + iteration, has_side_effects=True
        ),
    )(*fields)
    update = got[0].reshape(shape)
    residual = got[1].reshape(shape)
    if last:
        return update, residual, None, None
    return update, residual, got[2].reshape(shape), got[3]


def tile_view(control, tile_rows, tile_cols, points):
    return control.reshape(2, tile_rows, points, tile_cols, points)


def edge_band(tile_grid, facing, band_depth):
    if facing == 0:
        return tile_grid[..., ::-1][..., :band_depth].transpose(0, 1, 3, 2, 4)
    if facing == 1:
        return tile_grid[..., :band_depth].transpose(0, 1, 3, 2, 4)
    if facing == 2:
        return tile_grid[:, :, ::-1][:, :, :band_depth].transpose(0, 1, 3, 4, 2)
    return tile_grid[:, :, :band_depth].transpose(0, 1, 3, 4, 2)


def place_edge(band_part, facing, points):
    band_depth = band_part.shape[4]
    if facing < 2:
        widened = jnp.pad(
            band_part.transpose(0, 1, 3, 2, 4),
            ((0, 0), (0, 0), (0, 0), (0, 0), (0, points - band_depth)),
        )
        if facing == 0:
            return widened[..., ::-1]
        return widened
    widened = jnp.pad(
        band_part.transpose(0, 1, 4, 2, 3),
        ((0, 0), (0, 0), (0, points - band_depth), (0, 0), (0, 0)),
    )
    if facing == 2:
        return widened[:, :, ::-1]
    return widened


def make_tables(along_cell, across, frac_pair):
    weight_along = (frac_pair[0].astype(jnp.float32) + 0.5) / 256.0
    weight_across = (frac_pair[1].astype(jnp.float32) + 0.5) / 256.0
    return (along_cell, across, weight_along, weight_across)


def weight_tables(tables, points, band_depth):
    along_cell, across, weight_along, weight_across = tables
    along_iota = jnp.arange(points, dtype=jnp.int32)[None, None, :, None]
    across_iota = jnp.arange(band_depth, dtype=jnp.int32)[None, None, :, None]
    cell_now = along_cell[:, :, None, :]
    depth_now = across[:, :, None, :]
    frac_along = weight_along[:, :, None, :]
    frac_across = weight_across[:, :, None, :]
    along_table = (1.0 - frac_along) * (along_iota == cell_now).astype(jnp.float32) + frac_along * (
        along_iota == cell_now + 1
    ).astype(jnp.float32)
    across_table = (1.0 - frac_across) * (across_iota == depth_now).astype(
        jnp.float32
    ) + frac_across * (across_iota == depth_now + 1).astype(jnp.float32)
    return (along_table, across_table)


def interpolate(band_part, tables):
    along_table, across_table = weight_tables(tables, band_part.shape[3], band_part.shape[4])
    partial_sum = jnp.einsum(
        "cabiq,abis->cabqs", band_part, along_table, precision=lax.Precision.HIGHEST
    )
    return jnp.sum(partial_sum * across_table[None], axis=3)


def spread_back(residual, tables, points, band_depth):
    along_table, across_table = weight_tables(tables, points, band_depth)
    weighted = residual[:, :, :, None, :] * across_table[None]
    return jnp.einsum("cabqs,abis->cabiq", weighted, along_table, precision=lax.Precision.HIGHEST)


def bending(control, tile_rows, tile_cols):
    grid_view = tile_view(control, tile_rows, tile_cols, GRID)
    inner = (
        grid_view[:, :, :-2, :, 1:-1]
        + grid_view[:, :, 2:, :, 1:-1]
        + grid_view[:, :, 1:-1, :, :-2]
        + grid_view[:, :, 1:-1, :, 2:]
        - 4.0 * grid_view[:, :, 1:-1, :, 1:-1]
    )
    widths = ((0, 0), (0, 0), (1, 1), (0, 0), (1, 1))
    curvature = jnp.pad(inner, widths)
    padded = jnp.pad(curvature, widths)
    result = (
        padded[:, :, :-2, :, 1:-1]
        + padded[:, :, 2:, :, 1:-1]
        + padded[:, :, 1:-1, :, :-2]
        + padded[:, :, 1:-1, :, 2:]
        - 4.0 * curvature
    )
    return result.reshape(control.shape)


def _halo_kernel(names, *refs):
    send_refs, recv_refs, (send_sems, recv_sems) = refs[:4], refs[4:8], refs[8:]
    ncol = lax.axis_size("col")
    nrow = lax.axis_size("row")
    ci = lax.axis_index("col")
    ri = lax.axis_index("row")

    def dev(c, r):
        where = {"col": c, "row": r}
        return tuple(where[n] for n in names)

    peers = [
        dev((ci + 1) % ncol, ri),
        dev((ci + ncol - 1) % ncol, ri),
        dev(ci, (ri + 1) % nrow),
        dev(ci, (ri + nrow - 1) % nrow),
    ]
    barrier = pltpu.get_barrier_semaphore()
    for peer in peers:
        pl.semaphore_signal(barrier, 1, device_id=peer, device_id_type=MESH_ID)
    pl.semaphore_wait(barrier, len(peers))
    copies = [
        pltpu.make_async_remote_copy(
            src_ref=send_refs[k], dst_ref=recv_refs[k], send_sem=send_sems.at[k],
            recv_sem=recv_sems.at[k], device_id=peers[k], device_id_type=MESH_ID)
        for k in range(4)
    ]
    for copy in copies:
        copy.start()
    for copy in copies:
        copy.wait_send()
        copy.wait_recv()


def halo_exchange(names, to_east, to_west, to_south, to_north):
    slabs = [to_east, to_west, to_south, to_north]
    got = pl.pallas_call(
        functools.partial(_halo_kernel, names),
        out_shape=tuple(jax.ShapeDtypeStruct(slab.shape, jnp.float32) for slab in slabs),
        in_specs=[pl.BlockSpec(memory_space=pltpu.VMEM)] * 4,
        out_specs=tuple(pl.BlockSpec(memory_space=pltpu.VMEM) for _ in slabs),
        scratch_shapes=[pltpu.SemaphoreType.DMA((4,)), pltpu.SemaphoreType.DMA((4,))],
        compiler_params=pltpu.CompilerParams(collective_id=1, has_side_effects=True),
    )(*slabs)
    return list(got)


def all_weight_tables(tables):
    pairs = [weight_tables(tables[facing], GRID, BAND) for facing in range(4)]
    return (jnp.stack([pair[0] for pair in pairs]), jnp.stack([pair[1] for pair in pairs]))


def seam_term(control, target, tables, adjacency, names):
    tile_rows, tile_cols = (adjacency.shape[1], adjacency.shape[2])
    along_table, across_table = tables
    grid_view = tile_view(control, tile_rows, tile_cols, GRID)
    bands = jnp.stack([edge_band(grid_view, facing, BAND) for facing in range(4)])
    partial_sum = jnp.einsum(
        "kcabiq,kabis->kcabqs", bands, along_table, precision=lax.Precision.HIGHEST
    )
    stacked_values = jnp.sum(partial_sum * across_table[:, None], axis=4)
    seam_values = [stacked_values[facing] for facing in range(4)]
    samples = seam_values[0].shape[3]
    col_pos = lax.axis_index("col") * tile_cols + jnp.arange(tile_cols)
    row_pos = lax.axis_index("row") * tile_rows + jnp.arange(tile_rows)
    mask_east = (
        adjacency[0].astype(jnp.float32)
        * (col_pos < lax.axis_size("col") * tile_cols - 1).astype(jnp.float32)[None, :]
    )
    mask_south = (
        adjacency[1].astype(jnp.float32)
        * (row_pos < lax.axis_size("row") * tile_rows - 1).astype(jnp.float32)[:, None]
    )
    own_east = seam_values[0]
    own_south = seam_values[2]
    if target is not None:
        own_east = own_east - target[0]
        own_south = own_south - target[1]
    to_east = jnp.concatenate(
        [
            own_east[:, :, -1].reshape(2 * tile_rows, samples),
            jnp.broadcast_to(mask_east[:, -1:], (tile_rows, samples)),
        ]
    )
    to_west = seam_values[1][:, :, 0].reshape(2 * tile_rows, samples)
    to_south = jnp.concatenate(
        [
            own_south[:, -1].reshape(2 * tile_cols, samples),
            jnp.broadcast_to(mask_south[-1][:, None], (tile_cols, samples)),
        ]
    )
    to_north = seam_values[3][:, 0].reshape(2 * tile_cols, samples)
    got_west, got_east, got_north, got_south = halo_exchange(
        names, to_east, to_west, to_south, to_north
    )
    west_east = got_west[: 2 * tile_rows].reshape(2, tile_rows, 1, samples)
    west_mask = got_west[2 * tile_rows :].reshape(1, tile_rows, 1, samples)
    east_next = got_east.reshape(2, tile_rows, 1, samples)
    north_south = got_north[: 2 * tile_cols].reshape(2, 1, tile_cols, samples)
    north_mask = got_north[2 * tile_cols :].reshape(1, 1, tile_cols, samples)
    south_next = got_south.reshape(2, 1, tile_cols, samples)
    west_next = jnp.concatenate([seam_values[1][:, :, 1:], east_next], axis=2)
    north_next = jnp.concatenate([seam_values[3][:, 1:], south_next], axis=1)
    resid_east = (own_east - west_next) * mask_east[None, :, :, None]
    resid_south = (own_south - north_next) * mask_south[None, :, :, None]
    from_west = (west_east - seam_values[1][:, :, :1]) * west_mask
    from_north = (north_south - seam_values[3][:, :1]) * north_mask
    resid_west = -jnp.concatenate([from_west, resid_east[:, :, :-1]], axis=2)
    resid_north = -jnp.concatenate([from_north, resid_south[:, :-1]], axis=1)
    residuals = jnp.stack([resid_east, resid_west, resid_south, resid_north])
    weighted = residuals[:, :, :, :, None, :] * across_table[:, None]
    spread_parts = jnp.einsum(
        "kcabqs,kabis->kcabiq", weighted, along_table, precision=lax.Precision.HIGHEST
    )
    summed = (
        place_edge(spread_parts[0], 0, GRID)
        + place_edge(spread_parts[1], 1, GRID)
        + place_edge(spread_parts[2], 2, GRID)
        + place_edge(spread_parts[3], 3, GRID)
    )
    return summed.reshape(control.shape)


def hessian_apply(control, tables, adjacency, names):
    tile_rows, tile_cols = (adjacency.shape[1], adjacency.shape[2])
    return (
        seam_term(control, None, tables, adjacency, names)
        + BEND_WEIGHT * bending(control, tile_rows, tile_cols)
        + DAMPING * control
    )


def shards(names, start_field, seam_target, seam_rows, seam_band, seam_frac, adjacency):
    tile_rows, tile_cols = (adjacency.shape[1], adjacency.shape[2])
    samples = seam_rows.shape[2] // tile_cols
    along_cells = seam_rows.reshape(4, tile_rows, tile_cols, samples)
    across_cells = seam_band.reshape(4, tile_rows, tile_cols, samples)
    frac_cells = seam_frac.reshape(4, 2, tile_rows, tile_cols, samples)
    tables = [
        make_tables(along_cells[facing], across_cells[facing], frac_cells[facing])
        for facing in range(4)
    ]
    tables = all_weight_tables(tables)
    target_cells = seam_target.reshape(2, 2, tile_rows, tile_cols, samples)
    target = (target_cells[0], target_cells[1])
    control = start_field
    gradient = seam_term(control, target, tables, adjacency, names) + BEND_WEIGHT * bending(
        control, tile_rows, tile_cols
    )
    residual = -gradient
    update = None
    direction = residual
    norm_tile = None
    for iteration in range(ITERS):
        seam_image = seam_term(direction, None, tables, adjacency, names)
        update, residual, direction, norm_tile = cg_step(
            names, iteration, direction, seam_image, residual, update, norm_tile
        )
    control = control + update
    return (control, residual)


def solution(mesh):
    placed = (
        P(None, "row", "col"),
        P(None, None, "row", "col"),
        P(None, "row", "col"),
        P(None, "row", "col"),
        P(None, None, "row", "col"),
        P(None, "row", "col"),
    )
    return jax.shard_map(
        functools.partial(shards, tuple(mesh.axis_names)),
        mesh=mesh,
        in_specs=placed,
        out_specs=(P(None, "row", "col"), P(None, "row", "col")),
        check_vma=False,
    )
```

```python
import functools

import jax
import jax.numpy as jnp
from jax import lax
from jax.experimental import pallas as pl
from jax.experimental.pallas import tpu as pltpu
from jax.sharding import PartitionSpec as P

GRID = 32
BAND = 4
ITERS = 3


BEND_WEIGHT = 0.05
DAMPING = 0.5


MESH_ID = pl.DeviceIdType.MESH


def _cg_kernel(names, first, last, d_ref, h_ref, r_ref, *refs):
    if not first:
        u_ref, rr_ref = refs[:2]
        refs = refs[2:]
    if last:
        u_out, r_out, row_buf, col_buf, mine, part, row_send, row_recv, col_send, col_recv = refs
    else:
        (u_out, r_out, d_out, rr_out, row_buf, col_buf, mine, part, row_send, row_recv, col_send,
         col_recv) = refs
    ncol = lax.axis_size("col")
    nrow = lax.axis_size("row")
    ci = lax.axis_index("col")
    ri = lax.axis_index("row")

    def dev(c, r):
        where = {"col": c, "row": r}
        return tuple(where[n] for n in names)

    barrier = pltpu.get_barrier_semaphore()

    @pl.loop(1, nrow)
    def _(k):
        pl.semaphore_signal(barrier, 1, device_id=dev(ci, (ri + k) % nrow), device_id_type=MESH_ID)

    @pl.loop(1, ncol)
    def _(k):
        pl.semaphore_signal(barrier, 1, device_id=dev((ci + k) % ncol, ri), device_id_type=MESH_ID)

    direction = d_ref[...]
    residual = r_ref[...]
    rows, cols = direction.shape
    y = lax.broadcasted_iota(jnp.int32, (rows, cols), 0) % GRID
    x = lax.broadcasted_iota(jnp.int32, (rows, cols), 1) % GRID
    inside = (y >= 1) & (y <= GRID - 2) & (x >= 1) & (x <= GRID - 2)

    def five_point(f):
        return (
            pltpu.roll(f, 1, 0)
            + pltpu.roll(f, rows - 1, 0)
            + pltpu.roll(f, 1, 1)
            + pltpu.roll(f, cols - 1, 1)
            - 4.0 * f
        )

    curvature = jnp.where(inside, five_point(direction), 0.0)
    image = h_ref[...] + BEND_WEIGHT * five_point(curvature) + DAMPING * direction

    def total(x):
        return jnp.sum(jnp.sum(x, axis=0, keepdims=True), axis=1, keepdims=True)

    parts = [total(direction * image)]
    if not last:
        parts += [total(image * image), total(residual * image)]
    if first:
        parts += [total(residual * residual)]
    lane = lax.broadcasted_iota(jnp.int32, (8, 128), 1)
    sub = lax.broadcasted_iota(jnp.int32, (8, 128), 0)
    tile = jnp.zeros((8, 128), jnp.float32)
    for k, value in enumerate(parts):
        tile = jnp.where((sub == 0) & (lane == k), value, tile)
    mine[...] = tile

    pl.semaphore_wait(barrier, nrow - 1 + ncol - 1)

    def row_copy(peer, slot):
        return pltpu.make_async_remote_copy(
            src_ref=mine, dst_ref=row_buf.at[slot], send_sem=row_send.at[peer],
            recv_sem=row_recv.at[slot], device_id=dev(ci, peer), device_id_type=MESH_ID)

    for k in range(1, nrow):
        row_copy((ri + k) % nrow, ri).start()
    row_buf[ri] = tile
    for k in range(1, nrow):
        row_copy((ri + k) % nrow, ri).wait_send()
        peer = (ri + nrow - k) % nrow
        row_copy(peer, peer).wait_recv()
    summed = row_buf[0]
    for j in range(1, nrow):
        summed = summed + row_buf[j]
    part[...] = summed

    def col_copy(peer, slot):
        return pltpu.make_async_remote_copy(
            src_ref=part, dst_ref=col_buf.at[slot], send_sem=col_send.at[peer],
            recv_sem=col_recv.at[slot], device_id=dev(peer, ri), device_id_type=MESH_ID)

    @pl.loop(1, ncol)
    def _(k):
        col_copy((ci + k) % ncol, ci).start()

    col_buf[ci] = summed

    @pl.loop(1, ncol)
    def _(k):
        col_copy((ci + k) % ncol, ci).wait_send()
        peer = (ci + ncol - k) % ncol
        col_copy(peer, peer).wait_recv()

    summed = lax.fori_loop(1, ncol, lambda j, acc: acc + col_buf[j], col_buf[0])

    def pick(k):
        return jnp.sum(jnp.where((sub == 0) & (lane == k), summed, 0.0), axis=(0, 1), keepdims=True)

    curv = pick(0)
    norm_now = pick(len(parts) - 1) if first else rr_ref[0:1, 0:1]
    step_size = norm_now / curv
    if first:
        u_out[...] = step_size * direction
    else:
        u_out[...] = u_ref[...] + step_size * direction
    residual = residual - step_size * image
    r_out[...] = residual
    if not last:
        image_sq = pick(1)
        cross = curv if first else pick(2)
        norm_next = norm_now - 2.0 * step_size * cross + step_size * step_size * image_sq
        d_out[...] = residual + norm_next / norm_now * direction
        rr_out[...] = jnp.broadcast_to(norm_next, (8, 128))


def cg_step(names, iteration, direction, image, residual, update, norm_tile):
    ncol = lax.axis_size("col")
    nrow = lax.axis_size("row")
    first = iteration == 0
    last = iteration == ITERS - 1
    shape = direction.shape
    flat = (shape[0] * shape[1], shape[2])
    fields = [x.reshape(flat) for x in (direction, image, residual)]
    if not first:
        fields += [update.reshape(flat), norm_tile]
    field_type = jax.ShapeDtypeStruct(flat, jnp.float32)
    out_shape = [field_type, field_type]
    if not last:
        out_shape += [field_type, jax.ShapeDtypeStruct((8, 128), jnp.float32)]
    got = pl.pallas_call(
        functools.partial(_cg_kernel, names, first, last),
        out_shape=tuple(out_shape),
        in_specs=[pl.BlockSpec(memory_space=pltpu.VMEM)] * len(fields),
        out_specs=tuple(pl.BlockSpec(memory_space=pltpu.VMEM) for _ in out_shape),
        scratch_shapes=[
            pltpu.VMEM((nrow, 8, 128), jnp.float32),
            pltpu.VMEM((ncol, 8, 128), jnp.float32),
            pltpu.VMEM((8, 128), jnp.float32),
            pltpu.VMEM((8, 128), jnp.float32),
            pltpu.SemaphoreType.DMA((nrow,)),
            pltpu.SemaphoreType.DMA((nrow,)),
            pltpu.SemaphoreType.DMA((ncol,)),
            pltpu.SemaphoreType.DMA((ncol,)),
        ],
        compiler_params=pltpu.CompilerParams(
            collective_id=10 + iteration, has_side_effects=True
        ),
    )(*fields)
    update = got[0].reshape(shape)
    residual = got[1].reshape(shape)
    if last:
        return update, residual, None, None
    return update, residual, got[2].reshape(shape), got[3]


def tile_view(control, tile_rows, tile_cols, points):
    return control.reshape(2, tile_rows, points, tile_cols, points)


def edge_band(tile_grid, facing, band_depth):
    if facing == 0:
        return tile_grid[..., ::-1][..., :band_depth].transpose(0, 1, 3, 2, 4)
    if facing == 1:
        return tile_grid[..., :band_depth].transpose(0, 1, 3, 2, 4)
    if facing == 2:
        return tile_grid[:, :, ::-1][:, :, :band_depth].transpose(0, 1, 3, 4, 2)
    return tile_grid[:, :, :band_depth].transpose(0, 1, 3, 4, 2)


def place_edge(band_part, facing, points):
    band_depth = band_part.shape[4]
    if facing < 2:
        widened = jnp.pad(
            band_part.transpose(0, 1, 3, 2, 4),
            ((0, 0), (0, 0), (0, 0), (0, 0), (0, points - band_depth)),
        )
        if facing == 0:
            return widened[..., ::-1]
        return widened
    widened = jnp.pad(
        band_part.transpose(0, 1, 4, 2, 3),
        ((0, 0), (0, 0), (0, points - band_depth), (0, 0), (0, 0)),
    )
    if facing == 2:
        return widened[:, :, ::-1]
    return widened


def make_tables(along_cell, across, frac_pair):
    weight_along = (frac_pair[0].astype(jnp.float32) + 0.5) / 256.0
    weight_across = (frac_pair[1].astype(jnp.float32) + 0.5) / 256.0
    return (along_cell, across, weight_along, weight_across)


def weight_tables(tables, points, band_depth):
    along_cell, across, weight_along, weight_across = tables
    along_iota = jnp.arange(points, dtype=jnp.int32)[None, None, :, None]
    across_iota = jnp.arange(band_depth, dtype=jnp.int32)[None, None, :, None]
    cell_now = along_cell[:, :, None, :]
    depth_now = across[:, :, None, :]
    frac_along = weight_along[:, :, None, :]
    frac_across = weight_across[:, :, None, :]
    along_table = (1.0 - frac_along) * (along_iota == cell_now).astype(jnp.float32) + frac_along * (
        along_iota == cell_now + 1
    ).astype(jnp.float32)
    across_table = (1.0 - frac_across) * (across_iota == depth_now).astype(
        jnp.float32
    ) + frac_across * (across_iota == depth_now + 1).astype(jnp.float32)
    return (along_table, across_table)


def interpolate(band_part, tables):
    along_table, across_table = weight_tables(tables, band_part.shape[3], band_part.shape[4])
    partial_sum = jnp.einsum(
        "cabiq,abis->cabqs", band_part, along_table, precision=lax.Precision.HIGHEST
    )
    return jnp.sum(partial_sum * across_table[None], axis=3)


def spread_back(residual, tables, points, band_depth):
    along_table, across_table = weight_tables(tables, points, band_depth)
    weighted = residual[:, :, :, None, :] * across_table[None]
    return jnp.einsum("cabqs,abis->cabiq", weighted, along_table, precision=lax.Precision.HIGHEST)


def bending(control, tile_rows, tile_cols):
    grid_view = tile_view(control, tile_rows, tile_cols, GRID)
    inner = (
        grid_view[:, :, :-2, :, 1:-1]
        + grid_view[:, :, 2:, :, 1:-1]
        + grid_view[:, :, 1:-1, :, :-2]
        + grid_view[:, :, 1:-1, :, 2:]
        - 4.0 * grid_view[:, :, 1:-1, :, 1:-1]
    )
    widths = ((0, 0), (0, 0), (1, 1), (0, 0), (1, 1))
    curvature = jnp.pad(inner, widths)
    padded = jnp.pad(curvature, widths)
    result = (
        padded[:, :, :-2, :, 1:-1]
        + padded[:, :, 2:, :, 1:-1]
        + padded[:, :, 1:-1, :, :-2]
        + padded[:, :, 1:-1, :, 2:]
        - 4.0 * curvature
    )
    return result.reshape(control.shape)


def _halo_kernel(names, send_ref, recv_ref, send_sems, recv_sems):
    ncol = lax.axis_size("col")
    nrow = lax.axis_size("row")
    ci = lax.axis_index("col")
    ri = lax.axis_index("row")

    def dev(c, r):
        where = {"col": c, "row": r}
        return tuple(where[n] for n in names)

    peers = [
        dev((ci + 1) % ncol, ri),
        dev((ci + ncol - 1) % ncol, ri),
        dev(ci, (ri + 1) % nrow),
        dev(ci, (ri + nrow - 1) % nrow),
    ]
    barrier = pltpu.get_barrier_semaphore()
    for peer in peers:
        pl.semaphore_signal(barrier, 1, device_id=peer, device_id_type=MESH_ID)
    pl.semaphore_wait(barrier, len(peers))
    copies = [
        pltpu.make_async_remote_copy(
            src_ref=send_ref.at[k], dst_ref=recv_ref.at[k], send_sem=send_sems.at[k],
            recv_sem=recv_sems.at[k], device_id=peers[k], device_id_type=MESH_ID)
        for k in range(4)
    ]
    for copy in copies:
        copy.start()
    for copy in copies:
        copy.wait_send()
        copy.wait_recv()


def halo_exchange(names, to_east, to_west, to_south, to_north):
    slabs = [to_east, to_west, to_south, to_north]
    rows = max(slab.shape[0] for slab in slabs)
    lanes = slabs[0].shape[1]
    stacked = jnp.stack([jnp.pad(slab, ((0, rows - slab.shape[0]), (0, 0))) for slab in slabs])
    got = pl.pallas_call(
        functools.partial(_halo_kernel, names),
        out_shape=jax.ShapeDtypeStruct(stacked.shape, jnp.float32),
        in_specs=[pl.BlockSpec(memory_space=pltpu.VMEM)],
        out_specs=pl.BlockSpec(memory_space=pltpu.VMEM),
        scratch_shapes=[pltpu.SemaphoreType.DMA((4,)), pltpu.SemaphoreType.DMA((4,))],
        compiler_params=pltpu.CompilerParams(collective_id=1, has_side_effects=True),
    )(stacked)
    return [got[k, : slabs[k].shape[0]] for k in range(4)]


def all_weight_tables(tables):
    pairs = [weight_tables(tables[facing], GRID, BAND) for facing in range(4)]
    return (jnp.stack([pair[0] for pair in pairs]), jnp.stack([pair[1] for pair in pairs]))


def seam_term(control, target, tables, adjacency, names):
    tile_rows, tile_cols = (adjacency.shape[1], adjacency.shape[2])
    along_table, across_table = tables
    grid_view = tile_view(control, tile_rows, tile_cols, GRID)
    bands = jnp.stack([edge_band(grid_view, facing, BAND) for facing in range(4)])
    partial_sum = jnp.einsum(
        "kcabiq,kabis->kcabqs", bands, along_table, precision=lax.Precision.HIGH
    )
    stacked_values = jnp.sum(partial_sum * across_table[:, None], axis=4)
    seam_values = [stacked_values[facing] for facing in range(4)]
    samples = seam_values[0].shape[3]
    col_pos = lax.axis_index("col") * tile_cols + jnp.arange(tile_cols)
    row_pos = lax.axis_index("row") * tile_rows + jnp.arange(tile_rows)
    mask_east = (
        adjacency[0].astype(jnp.float32)
        * (col_pos < lax.axis_size("col") * tile_cols - 1).astype(jnp.float32)[None, :]
    )
    mask_south = (
        adjacency[1].astype(jnp.float32)
        * (row_pos < lax.axis_size("row") * tile_rows - 1).astype(jnp.float32)[:, None]
    )
    own_east = seam_values[0]
    own_south = seam_values[2]
    if target is not None:
        own_east = own_east - target[0]
        own_south = own_south - target[1]
    to_east = jnp.concatenate(
        [
            own_east[:, :, -1].reshape(2 * tile_rows, samples),
            jnp.broadcast_to(mask_east[:, -1:], (tile_rows, samples)),
        ]
    )
    to_west = seam_values[1][:, :, 0].reshape(2 * tile_rows, samples)
    to_south = jnp.concatenate(
        [
            own_south[:, -1].reshape(2 * tile_cols, samples),
            jnp.broadcast_to(mask_south[-1][:, None], (tile_cols, samples)),
        ]
    )
    to_north = seam_values[3][:, 0].reshape(2 * tile_cols, samples)
    got_west, got_east, got_north, got_south = halo_exchange(
        names, to_east, to_west, to_south, to_north
    )
    west_east = got_west[: 2 * tile_rows].reshape(2, tile_rows, 1, samples)
    west_mask = got_west[2 * tile_rows :].reshape(1, tile_rows, 1, samples)
    east_next = got_east.reshape(2, tile_rows, 1, samples)
    north_south = got_north[: 2 * tile_cols].reshape(2, 1, tile_cols, samples)
    north_mask = got_north[2 * tile_cols :].reshape(1, 1, tile_cols, samples)
    south_next = got_south.reshape(2, 1, tile_cols, samples)
    west_next = jnp.concatenate([seam_values[1][:, :, 1:], east_next], axis=2)
    north_next = jnp.concatenate([seam_values[3][:, 1:], south_next], axis=1)
    resid_east = (own_east - west_next) * mask_east[None, :, :, None]
    resid_south = (own_south - north_next) * mask_south[None, :, :, None]
    from_west = (west_east - seam_values[1][:, :, :1]) * west_mask
    from_north = (north_south - seam_values[3][:, :1]) * north_mask
    resid_west = -jnp.concatenate([from_west, resid_east[:, :, :-1]], axis=2)
    resid_north = -jnp.concatenate([from_north, resid_south[:, :-1]], axis=1)
    residuals = jnp.stack([resid_east, resid_west, resid_south, resid_north])
    weighted = residuals[:, :, :, :, None, :] * across_table[:, None]
    spread_parts = jnp.einsum(
        "kcabqs,kabis->kcabiq", weighted, along_table, precision=lax.Precision.HIGH
    )
    summed = (
        place_edge(spread_parts[0], 0, GRID)
        + place_edge(spread_parts[1], 1, GRID)
        + place_edge(spread_parts[2], 2, GRID)
        + place_edge(spread_parts[3], 3, GRID)
    )
    return summed.reshape(control.shape)


def hessian_apply(control, tables, adjacency, names):
    tile_rows, tile_cols = (adjacency.shape[1], adjacency.shape[2])
    return (
        seam_term(control, None, tables, adjacency, names)
        + BEND_WEIGHT * bending(control, tile_rows, tile_cols)
        + DAMPING * control
    )


def shards(names, start_field, seam_target, seam_rows, seam_band, seam_frac, adjacency):
    tile_rows, tile_cols = (adjacency.shape[1], adjacency.shape[2])
    samples = seam_rows.shape[2] // tile_cols
    along_cells = seam_rows.reshape(4, tile_rows, tile_cols, samples)
    across_cells = seam_band.reshape(4, tile_rows, tile_cols, samples)
    frac_cells = seam_frac.reshape(4, 2, tile_rows, tile_cols, samples)
    tables = [
        make_tables(along_cells[facing], across_cells[facing], frac_cells[facing])
        for facing in range(4)
    ]
    tables = all_weight_tables(tables)
    target_cells = seam_target.reshape(2, 2, tile_rows, tile_cols, samples)
    target = (target_cells[0], target_cells[1])
    control = start_field
    gradient = seam_term(control, target, tables, adjacency, names) + BEND_WEIGHT * bending(
        control, tile_rows, tile_cols
    )
    residual = -gradient
    update = None
    direction = residual
    norm_tile = None
    for iteration in range(ITERS):
        seam_image = seam_term(direction, None, tables, adjacency, names)
        update, residual, direction, norm_tile = cg_step(
            names, iteration, direction, seam_image, residual, update, norm_tile
        )
    control = control + update
    return (control, residual)


def solution(mesh):
    placed = (
        P(None, "row", "col"),
        P(None, None, "row", "col"),
        P(None, "row", "col"),
        P(None, "row", "col"),
        P(None, None, "row", "col"),
        P(None, "row", "col"),
    )
    return jax.shard_map(
        functools.partial(shards, tuple(mesh.axis_names)),
        mesh=mesh,
        in_specs=placed,
        out_specs=(P(None, "row", "col"), P(None, "row", "col")),
        check_vma=False,
    )
```

```python
import functools

import jax
import jax.numpy as jnp
from jax import lax
from jax.experimental import pallas as pl
from jax.experimental.pallas import tpu as pltpu
from jax.sharding import PartitionSpec as P

GRID = 32
BAND = 4
ITERS = 3


BEND_WEIGHT = 0.05
DAMPING = 0.5


MESH_ID = pl.DeviceIdType.MESH


def _cg_kernel(names, first, last, d_ref, h_ref, *refs):
    if first:
        r_ref = d_ref
    else:
        r_ref, u_ref, rr_ref = refs[:3]
        refs = refs[3:]
    if last:
        u_out, r_out, row_buf, col_buf, mine, part, row_send, row_recv, col_send, col_recv = refs
    else:
        (u_out, r_out, d_out, rr_out, row_buf, col_buf, mine, part, row_send, row_recv, col_send,
         col_recv) = refs
    ncol = lax.axis_size("col")
    nrow = lax.axis_size("row")
    ci = lax.axis_index("col")
    ri = lax.axis_index("row")

    def dev(c, r):
        where = {"col": c, "row": r}
        return tuple(where[n] for n in names)

    barrier = pltpu.get_barrier_semaphore()

    @pl.loop(1, nrow)
    def _(k):
        pl.semaphore_signal(barrier, 1, device_id=dev(ci, (ri + k) % nrow), device_id_type=MESH_ID)

    @pl.loop(1, ncol)
    def _(k):
        pl.semaphore_signal(barrier, 1, device_id=dev((ci + k) % ncol, ri), device_id_type=MESH_ID)

    direction = d_ref[...]
    residual = r_ref[...]
    rows, cols = direction.shape
    y = lax.broadcasted_iota(jnp.int32, (rows, cols), 0) % GRID
    x = lax.broadcasted_iota(jnp.int32, (rows, cols), 1) % GRID
    inside = (y >= 1) & (y <= GRID - 2) & (x >= 1) & (x <= GRID - 2)

    def five_point(f):
        return (
            pltpu.roll(f, 1, 0)
            + pltpu.roll(f, rows - 1, 0)
            + pltpu.roll(f, 1, 1)
            + pltpu.roll(f, cols - 1, 1)
            - 4.0 * f
        )

    curvature = jnp.where(inside, five_point(direction), 0.0)
    image = h_ref[...] + BEND_WEIGHT * five_point(curvature) + DAMPING * direction

    def total(x):
        return jnp.sum(jnp.sum(x, axis=0, keepdims=True), axis=1, keepdims=True)

    parts = [total(direction * image)]
    if not last:
        parts += [total(image * image), total(residual * image)]
    if first:
        parts += [total(residual * residual)]
    lane = lax.broadcasted_iota(jnp.int32, (8, 128), 1)
    sub = lax.broadcasted_iota(jnp.int32, (8, 128), 0)
    tile = jnp.zeros((8, 128), jnp.float32)
    for k, value in enumerate(parts):
        tile = jnp.where((sub == 0) & (lane == k), value, tile)
    mine[...] = tile

    pl.semaphore_wait(barrier, nrow - 1 + ncol - 1)

    def row_copy(peer, slot):
        return pltpu.make_async_remote_copy(
            src_ref=mine, dst_ref=row_buf.at[slot], send_sem=row_send.at[peer],
            recv_sem=row_recv.at[slot], device_id=dev(ci, peer), device_id_type=MESH_ID)

    for k in range(1, nrow):
        row_copy((ri + k) % nrow, ri).start()
    row_buf[ri] = tile
    for k in range(1, nrow):
        row_copy((ri + k) % nrow, ri).wait_send()
        peer = (ri + nrow - k) % nrow
        row_copy(peer, peer).wait_recv()
    summed = row_buf[0]
    for j in range(1, nrow):
        summed = summed + row_buf[j]
    part[...] = summed

    def col_copy(peer, slot):
        return pltpu.make_async_remote_copy(
            src_ref=part, dst_ref=col_buf.at[slot], send_sem=col_send.at[peer],
            recv_sem=col_recv.at[slot], device_id=dev(peer, ri), device_id_type=MESH_ID)

    @pl.loop(1, ncol)
    def _(k):
        col_copy((ci + k) % ncol, ci).start()

    col_buf[ci] = summed

    @pl.loop(1, ncol)
    def _(k):
        col_copy((ci + k) % ncol, ci).wait_send()
        peer = (ci + ncol - k) % ncol
        col_copy(peer, peer).wait_recv()

    summed = lax.fori_loop(1, ncol, lambda j, acc: acc + col_buf[j], col_buf[0])

    def pick(k):
        return jnp.sum(jnp.where((sub == 0) & (lane == k), summed, 0.0), axis=(0, 1), keepdims=True)

    curv = pick(0)
    norm_now = pick(len(parts) - 1) if first else rr_ref[0:1, 0:1]
    step_size = norm_now / curv
    if first:
        u_out[...] = step_size * direction
    else:
        u_out[...] = u_ref[...] + step_size * direction
    residual = residual - step_size * image
    r_out[...] = residual
    if not last:
        image_sq = pick(1)
        cross = curv if first else pick(2)
        norm_next = norm_now - 2.0 * step_size * cross + step_size * step_size * image_sq
        d_out[...] = residual + norm_next / norm_now * direction
        rr_out[...] = jnp.broadcast_to(norm_next, (8, 128))


def cg_step(names, iteration, direction, image, residual, update, norm_tile):
    ncol = lax.axis_size("col")
    nrow = lax.axis_size("row")
    first = iteration == 0
    last = iteration == ITERS - 1
    shape = direction.shape
    flat = (shape[0] * shape[1], shape[2])
    fields = [x.reshape(flat) for x in (direction, image)]
    if not first:
        fields += [residual.reshape(flat), update.reshape(flat), norm_tile]
    field_type = jax.ShapeDtypeStruct(flat, jnp.float32)
    out_shape = [field_type, field_type]
    if not last:
        out_shape += [field_type, jax.ShapeDtypeStruct((8, 128), jnp.float32)]
    got = pl.pallas_call(
        functools.partial(_cg_kernel, names, first, last),
        out_shape=tuple(out_shape),
        in_specs=[pl.BlockSpec(memory_space=pltpu.VMEM)] * len(fields),
        out_specs=tuple(pl.BlockSpec(memory_space=pltpu.VMEM) for _ in out_shape),
        scratch_shapes=[
            pltpu.VMEM((nrow, 8, 128), jnp.float32),
            pltpu.VMEM((ncol, 8, 128), jnp.float32),
            pltpu.VMEM((8, 128), jnp.float32),
            pltpu.VMEM((8, 128), jnp.float32),
            pltpu.SemaphoreType.DMA((nrow,)),
            pltpu.SemaphoreType.DMA((nrow,)),
            pltpu.SemaphoreType.DMA((ncol,)),
            pltpu.SemaphoreType.DMA((ncol,)),
        ],
        compiler_params=pltpu.CompilerParams(
            collective_id=10 + iteration, has_side_effects=True
        ),
    )(*fields)
    update = got[0].reshape(shape)
    residual = got[1].reshape(shape)
    if last:
        return update, residual, None, None
    return update, residual, got[2].reshape(shape), got[3]


def tile_view(control, tile_rows, tile_cols, points):
    return control.reshape(2, tile_rows, points, tile_cols, points)


def edge_band(tile_grid, facing, band_depth):
    if facing == 0:
        return tile_grid[..., ::-1][..., :band_depth].transpose(0, 1, 3, 2, 4)
    if facing == 1:
        return tile_grid[..., :band_depth].transpose(0, 1, 3, 2, 4)
    if facing == 2:
        return tile_grid[:, :, ::-1][:, :, :band_depth].transpose(0, 1, 3, 4, 2)
    return tile_grid[:, :, :band_depth].transpose(0, 1, 3, 4, 2)


def place_edge(band_part, facing, points):
    band_depth = band_part.shape[4]
    if facing < 2:
        widened = jnp.pad(
            band_part.transpose(0, 1, 3, 2, 4),
            ((0, 0), (0, 0), (0, 0), (0, 0), (0, points - band_depth)),
        )
        if facing == 0:
            return widened[..., ::-1]
        return widened
    widened = jnp.pad(
        band_part.transpose(0, 1, 4, 2, 3),
        ((0, 0), (0, 0), (0, points - band_depth), (0, 0), (0, 0)),
    )
    if facing == 2:
        return widened[:, :, ::-1]
    return widened


def make_tables(along_cell, across, frac_pair):
    weight_along = (frac_pair[0].astype(jnp.float32) + 0.5) / 256.0
    weight_across = (frac_pair[1].astype(jnp.float32) + 0.5) / 256.0
    return (along_cell, across, weight_along, weight_across)


def weight_tables(tables, points, band_depth):
    along_cell, across, weight_along, weight_across = tables
    along_iota = jnp.arange(points, dtype=jnp.int32)[None, None, :, None]
    across_iota = jnp.arange(band_depth, dtype=jnp.int32)[None, None, :, None]
    cell_now = along_cell[:, :, None, :]
    depth_now = across[:, :, None, :]
    frac_along = weight_along[:, :, None, :]
    frac_across = weight_across[:, :, None, :]
    along_table = (1.0 - frac_along) * (along_iota == cell_now).astype(jnp.float32) + frac_along * (
        along_iota == cell_now + 1
    ).astype(jnp.float32)
    across_table = (1.0 - frac_across) * (across_iota == depth_now).astype(
        jnp.float32
    ) + frac_across * (across_iota == depth_now + 1).astype(jnp.float32)
    return (along_table, across_table)


def interpolate(band_part, tables):
    along_table, across_table = weight_tables(tables, band_part.shape[3], band_part.shape[4])
    partial_sum = jnp.einsum(
        "cabiq,abis->cabqs", band_part, along_table, precision=lax.Precision.HIGHEST
    )
    return jnp.sum(partial_sum * across_table[None], axis=3)


def spread_back(residual, tables, points, band_depth):
    along_table, across_table = weight_tables(tables, points, band_depth)
    weighted = residual[:, :, :, None, :] * across_table[None]
    return jnp.einsum("cabqs,abis->cabiq", weighted, along_table, precision=lax.Precision.HIGHEST)


def bending(control, tile_rows, tile_cols):
    grid_view = tile_view(control, tile_rows, tile_cols, GRID)
    inner = (
        grid_view[:, :, :-2, :, 1:-1]
        + grid_view[:, :, 2:, :, 1:-1]
        + grid_view[:, :, 1:-1, :, :-2]
        + grid_view[:, :, 1:-1, :, 2:]
        - 4.0 * grid_view[:, :, 1:-1, :, 1:-1]
    )
    widths = ((0, 0), (0, 0), (1, 1), (0, 0), (1, 1))
    curvature = jnp.pad(inner, widths)
    padded = jnp.pad(curvature, widths)
    result = (
        padded[:, :, :-2, :, 1:-1]
        + padded[:, :, 2:, :, 1:-1]
        + padded[:, :, 1:-1, :, :-2]
        + padded[:, :, 1:-1, :, 2:]
        - 4.0 * curvature
    )
    return result.reshape(control.shape)


def _halo_kernel(names, send_ref, recv_ref, send_sems, recv_sems):
    ncol = lax.axis_size("col")
    nrow = lax.axis_size("row")
    ci = lax.axis_index("col")
    ri = lax.axis_index("row")

    def dev(c, r):
        where = {"col": c, "row": r}
        return tuple(where[n] for n in names)

    peers = [
        dev((ci + 1) % ncol, ri),
        dev((ci + ncol - 1) % ncol, ri),
        dev(ci, (ri + 1) % nrow),
        dev(ci, (ri + nrow - 1) % nrow),
    ]
    barrier = pltpu.get_barrier_semaphore()
    for peer in peers:
        pl.semaphore_signal(barrier, 1, device_id=peer, device_id_type=MESH_ID)
    pl.semaphore_wait(barrier, len(peers))
    copies = [
        pltpu.make_async_remote_copy(
            src_ref=send_ref.at[k], dst_ref=recv_ref.at[k], send_sem=send_sems.at[k],
            recv_sem=recv_sems.at[k], device_id=peers[k], device_id_type=MESH_ID)
        for k in range(4)
    ]
    for copy in copies:
        copy.start()
    for copy in copies:
        copy.wait_send()
        copy.wait_recv()


def halo_exchange(names, to_east, to_west, to_south, to_north):
    slabs = [to_east, to_west, to_south, to_north]
    rows = max(slab.shape[0] for slab in slabs)
    lanes = slabs[0].shape[1]
    stacked = jnp.stack([jnp.pad(slab, ((0, rows - slab.shape[0]), (0, 0))) for slab in slabs])
    got = pl.pallas_call(
        functools.partial(_halo_kernel, names),
        out_shape=jax.ShapeDtypeStruct(stacked.shape, jnp.float32),
        in_specs=[pl.BlockSpec(memory_space=pltpu.VMEM)],
        out_specs=pl.BlockSpec(memory_space=pltpu.VMEM),
        scratch_shapes=[pltpu.SemaphoreType.DMA((4,)), pltpu.SemaphoreType.DMA((4,))],
        compiler_params=pltpu.CompilerParams(collective_id=1, has_side_effects=True),
    )(stacked)
    return [got[k, : slabs[k].shape[0]] for k in range(4)]


def all_weight_tables(tables):
    pairs = [weight_tables(tables[facing], GRID, BAND) for facing in range(4)]
    return (jnp.stack([pair[0] for pair in pairs]), jnp.stack([pair[1] for pair in pairs]))


def seam_term(control, target, tables, adjacency, names):
    tile_rows, tile_cols = (adjacency.shape[1], adjacency.shape[2])
    along_table, across_table = tables
    grid_view = tile_view(control, tile_rows, tile_cols, GRID)
    bands = jnp.stack([edge_band(grid_view, facing, BAND) for facing in range(4)])
    partial_sum = jnp.einsum(
        "kcabiq,kabis->kcabqs", bands, along_table, precision=lax.Precision.HIGH
    )
    stacked_values = jnp.sum(partial_sum * across_table[:, None], axis=4)
    seam_values = [stacked_values[facing] for facing in range(4)]
    samples = seam_values[0].shape[3]
    col_pos = lax.axis_index("col") * tile_cols + jnp.arange(tile_cols)
    row_pos = lax.axis_index("row") * tile_rows + jnp.arange(tile_rows)
    mask_east = (
        adjacency[0].astype(jnp.float32)
        * (col_pos < lax.axis_size("col") * tile_cols - 1).astype(jnp.float32)[None, :]
    )
    mask_south = (
        adjacency[1].astype(jnp.float32)
        * (row_pos < lax.axis_size("row") * tile_rows - 1).astype(jnp.float32)[:, None]
    )
    own_east = seam_values[0]
    own_south = seam_values[2]
    if target is not None:
        own_east = own_east - target[0]
        own_south = own_south - target[1]
    to_east = jnp.concatenate(
        [
            own_east[:, :, -1].reshape(2 * tile_rows, samples),
            jnp.broadcast_to(mask_east[:, -1:], (tile_rows, samples)),
        ]
    )
    to_west = seam_values[1][:, :, 0].reshape(2 * tile_rows, samples)
    to_south = jnp.concatenate(
        [
            own_south[:, -1].reshape(2 * tile_cols, samples),
            jnp.broadcast_to(mask_south[-1][:, None], (tile_cols, samples)),
        ]
    )
    to_north = seam_values[3][:, 0].reshape(2 * tile_cols, samples)
    got_west, got_east, got_north, got_south = halo_exchange(
        names, to_east, to_west, to_south, to_north
    )
    west_east = got_west[: 2 * tile_rows].reshape(2, tile_rows, 1, samples)
    west_mask = got_west[2 * tile_rows :].reshape(1, tile_rows, 1, samples)
    east_next = got_east.reshape(2, tile_rows, 1, samples)
    north_south = got_north[: 2 * tile_cols].reshape(2, 1, tile_cols, samples)
    north_mask = got_north[2 * tile_cols :].reshape(1, 1, tile_cols, samples)
    south_next = got_south.reshape(2, 1, tile_cols, samples)
    west_next = jnp.concatenate([seam_values[1][:, :, 1:], east_next], axis=2)
    north_next = jnp.concatenate([seam_values[3][:, 1:], south_next], axis=1)
    resid_east = (own_east - west_next) * mask_east[None, :, :, None]
    resid_south = (own_south - north_next) * mask_south[None, :, :, None]
    from_west = (west_east - seam_values[1][:, :, :1]) * west_mask
    from_north = (north_south - seam_values[3][:, :1]) * north_mask
    resid_west = -jnp.concatenate([from_west, resid_east[:, :, :-1]], axis=2)
    resid_north = -jnp.concatenate([from_north, resid_south[:, :-1]], axis=1)
    residuals = jnp.stack([resid_east, resid_west, resid_south, resid_north])
    weighted = residuals[:, :, :, :, None, :] * across_table[:, None]
    spread_parts = jnp.einsum(
        "kcabqs,kabis->kcabiq", weighted, along_table, precision=lax.Precision.HIGH
    )
    summed = (
        place_edge(spread_parts[0], 0, GRID)
        + place_edge(spread_parts[1], 1, GRID)
        + place_edge(spread_parts[2], 2, GRID)
        + place_edge(spread_parts[3], 3, GRID)
    )
    return summed.reshape(control.shape)


def hessian_apply(control, tables, adjacency, names):
    tile_rows, tile_cols = (adjacency.shape[1], adjacency.shape[2])
    return (
        seam_term(control, None, tables, adjacency, names)
        + BEND_WEIGHT * bending(control, tile_rows, tile_cols)
        + DAMPING * control
    )


def shards(names, start_field, seam_target, seam_rows, seam_band, seam_frac, adjacency):
    tile_rows, tile_cols = (adjacency.shape[1], adjacency.shape[2])
    samples = seam_rows.shape[2] // tile_cols
    along_cells = seam_rows.reshape(4, tile_rows, tile_cols, samples)
    across_cells = seam_band.reshape(4, tile_rows, tile_cols, samples)
    frac_cells = seam_frac.reshape(4, 2, tile_rows, tile_cols, samples)
    tables = [
        make_tables(along_cells[facing], across_cells[facing], frac_cells[facing])
        for facing in range(4)
    ]
    tables = all_weight_tables(tables)
    target_cells = seam_target.reshape(2, 2, tile_rows, tile_cols, samples)
    target = (target_cells[0], target_cells[1])
    control = start_field
    gradient = seam_term(control, target, tables, adjacency, names) + BEND_WEIGHT * bending(
        control, tile_rows, tile_cols
    )
    residual = -gradient
    update = None
    direction = residual
    norm_tile = None
    for iteration in range(ITERS):
        seam_image = seam_term(direction, None, tables, adjacency, names)
        update, residual, direction, norm_tile = cg_step(
            names, iteration, direction, seam_image, residual, update, norm_tile
        )
    control = control + update
    return (control, residual)


def solution(mesh):
    placed = (
        P(None, "row", "col"),
        P(None, None, "row", "col"),
        P(None, "row", "col"),
        P(None, "row", "col"),
        P(None, None, "row", "col"),
        P(None, "row", "col"),
    )
    return jax.shard_map(
        functools.partial(shards, tuple(mesh.axis_names)),
        mesh=mesh,
        in_specs=placed,
        out_specs=(P(None, "row", "col"), P(None, "row", "col")),
        check_vma=False,
    )
```
